128 devices in a mesh: grp: 4 (over x_hi, core), sub: 32 (over x_lo, y, z).
Axes of the slice: x: 4 (x_hi: 2, x_lo: 2; x = x_hi * 2 + x_lo), y: 4, z: 4, core: 2. Of those that a mesh axis runs over, the one named last changes fastest.
Arguments:
- template: bfloat16 [96, 96, 128], P('sub'), may hold values from -4 to 4
- subjects: bfloat16 [128, 96, 96, 128], P(('grp', 'sub')), may hold values from -40 to 40
Outputs:
- velocity: float32 [96, 3, 96, 128], P('sub')
- new_template: float32 [96, 96, 128], P('sub')
- similarity: float32 [], replicated
The draws below stay inside these ranges and needn't reach their ends.
All inputs are finite; a program needn't handle non-finite values.
Results may differ from the reference program's by a relative error of at most 0.0003.
Values may be sent and summed in bfloat16 or wider, within the bound.
No kernel may reach another device: no remote copies, remote signals or barrier semaphores. Data moves between devices by JAX's collectives and lax.ppermute only.
A program may use at most 128 MiB of HBM per device.

```python
import math
import jax
import jax.numpy as jnp
from jax import lax

NZ = 96
NX = 96
NY = 128
RADIUS = 4
REACH = 5
SUBJECTS = 128


def joint_fields(key):
    base_key = jax.random.fold_in(key, 101)
    noise_key = jax.random.fold_in(key, 202)
    shift_key = jax.random.fold_in(key, 303)
    sign_key = jax.random.fold_in(key, 404)
    depth = jnp.arange(NZ, dtype=jnp.float32)[:, None, None] / (NZ - 1)
    position = jnp.arange(SUBJECTS, dtype=jnp.float32) / max(SUBJECTS - 1, 1)
    signs = (2 * jax.random.randint(sign_key, (SUBJECTS,), 0, 2) - 1).astype(jnp.float32)
    base = jnp.clip(jax.random.normal(base_key, (NZ, NX, NY), jnp.float32), -4.0, 4.0)
    bias = 1.0 + 2.0 * depth
    spread = 0.4 + 0.6 * depth
    noise = jnp.clip(jax.random.normal(noise_key, (SUBJECTS, NZ, NX, NY), jnp.float32), -4.0, 4.0)
    ratio = 0.5 * 4.0 ** position
    shift = jax.random.uniform(shift_key, (SUBJECTS,), jnp.float32, 0.3, 0.9)
    return (base, bias, spread, noise, ratio, shift, depth, signs)


def draw_template(key, part):
    base, bias, spread, noise, ratio, shift, depth, signs = joint_fields(key)
    return base.astype(jnp.bfloat16)


def draw_subjects(key, part):
    base, bias, spread, noise, ratio, shift, depth, signs = joint_fields(key)
    padded = jnp.pad(base, ((1, 1), (0, 0), (0, 0)))
    slope = (padded[2:] - padded[:-2]) * 0.5
    displacement = shift[:, None, None, None] * (0.2 + 0.8 * depth)[None]
    common = base[None] + displacement * slope[None]
    moved = signs[:, None, None, None] * common + spread[None] * ratio[:, None, None, None] * noise
    return jnp.clip(bias[None] * moved, -40.0, 40.0).astype(jnp.bfloat16)


def setup_inputs(seed: int = 0) -> dict:
    keys = jax.random.split(jax.random.key(seed), 3)
    template = draw_template(jax.random.fold_in(keys[2], 71), 0)
    subjects = draw_subjects(jax.random.fold_in(keys[2], 71), 0)
    return {"template": template, "subjects": subjects}


EPSILON = 1e-05
STEP_LENGTH = 0.5
VARIANCE = 3.0

def shifted_sum(volume, axis, weights):
    extent = (len(weights) - 1) // 2
    widths = [(0, 0), (0, 0), (0, 0)]
    widths[axis] = (extent, extent)
    padded = jnp.pad(volume, widths)
    length = volume.shape[axis]
    result = jnp.zeros_like(volume)
    for offset, weight in enumerate(weights):
        result = result + weight * lax.slice_in_dim(padded, offset, offset + length, axis=axis)
    return result

def filter_all(volume, weights):
    result = shifted_sum(volume, 0, weights)
    result = shifted_sum(result, 1, weights)
    return shifted_sum(result, 2, weights)

def central(volume):
    padded = jnp.pad(volume, 1)
    along_z = (padded[2:, 1:-1, 1:-1] - padded[:-2, 1:-1, 1:-1]) * 0.5
    along_x = (padded[1:-1, 2:, 1:-1] - padded[1:-1, :-2, 1:-1]) * 0.5
    along_y = (padded[1:-1, 1:-1, 2:] - padded[1:-1, 1:-1, :-2]) * 0.5
    return jnp.stack([along_z, along_x, along_y], axis=0)

def reference(template, subjects):
    box_weights = [1.0 / (2 * RADIUS + 1)] * (2 * RADIUS + 1)
    kernel_sum = sum((math.exp(-offset * offset / (2.0 * VARIANCE)) for offset in range(-REACH, REACH + 1)))
    gauss_weights = [math.exp(-offset * offset / (2.0 * VARIANCE)) / kernel_sum for offset in range(-REACH, REACH + 1)]
    cell_count = NZ * NX * NY
    fixed_image = template.astype(jnp.float32)
    mean_i = filter_all(fixed_image, box_weights)
    mean_ii = filter_all(fixed_image * fixed_image, box_weights)
    var_i = mean_ii - mean_i * mean_i
    centred_i = fixed_image - mean_i
    gradients = central(fixed_image)

    def accumulate(carry_state, moving):
        moving = moving.astype(jnp.float32)
        mean_j = filter_all(moving, box_weights)
        mean_jj = filter_all(moving * moving, box_weights)
        mean_ij = filter_all(fixed_image * moving, box_weights)
        cross_sum = mean_ij - mean_i * mean_j
        var_j = mean_jj - mean_j * mean_j
        denominator = var_i * var_j + EPSILON
        factor = 2.0 * cross_sum / denominator * (moving - mean_j - cross_sum / (var_i + EPSILON) * centred_i)
        force_sum, image_sum, cc_sum = carry_state
        return ((force_sum + factor[None] * gradients, image_sum + moving, cc_sum + jnp.sum(cross_sum * cross_sum / denominator)), None)
    initial = (jnp.zeros((3, NZ, NX, NY), jnp.float32), jnp.zeros((NZ, NX, NY), jnp.float32), jnp.zeros((), jnp.float32))
    (force_sum, image_sum, cc_sum), unused = lax.scan(accumulate, initial, subjects)
    smoothed = jnp.stack([filter_all(force_sum[comp], gauss_weights) for comp in range(3)], axis=0)
    mean_velocity = smoothed / SUBJECTS
    mean_image = image_sum / SUBJECTS
    velocity_norm = jnp.sqrt(jnp.sum(mean_velocity * mean_velocity) / cell_count + EPSILON)
    image_norm = jnp.sqrt(jnp.sum(mean_image * mean_image) / cell_count + EPSILON)
    velocity = STEP_LENGTH * mean_velocity / velocity_norm
    normed = mean_image / image_norm
    slopes = central(normed)
    new_template = normed - lax.optimization_barrier(jnp.sum(velocity * slopes, axis=0))
    similarity = cc_sum / (SUBJECTS * cell_count)
    return (jnp.transpose(velocity, (1, 0, 2, 3)), new_template, similarity)
```

```python
import math

import jax
import jax.numpy as jnp
from jax import lax
from jax.experimental import pallas as pl
from jax.experimental.pallas import tpu as pltpu
from jax.sharding import PartitionSpec as P

RADIUS = 4
REACH = 5
EPSILON = 1e-05
STEP_LENGTH = 0.5
VARIANCE = 3.0
HIGH = lax.Precision.HIGHEST
F32 = jnp.float32
BF16 = jnp.bfloat16

NZ, NX, NY = 96, 96, 128
WIN = 56
OWN = 48
COUNT = 729.0
BOTH = ("grp", "sub")
DEVICES = 128


def place(xh, co, xl, y, z):
    return (xh * 2 + co) * 32 + xl * 16 + y * 4 + z


def pairs(move):
    out = []
    for xh in range(2):
        for co in range(2):
            for xl in range(2):
                for y in range(4):
                    for z in range(4):
                        target = move(xh, co, xl, y, z)
                        if target is not None:
                            out.append((place(xh, co, xl, y, z), place(*target)))
    return out


def first_round(k):
    return pairs(
        lambda xh, co, xl, y, z: (xh, co, xl, y, (z + k) % 4) if co == 0 else (xh, co, xl, (y + k) % 4, z)
    )


def second_round(k):
    return pairs(
        lambda xh, co, xl, y, z: (xh, co, xl, (y + k) % 4, z) if co == 0 else (xh, co, xl, y, (z + k) % 4)
    )


def third_round(k):
    def move(xh, co, xl, y, z):
        x = (xh * 2 + xl + k) % 4
        return (x // 2, co, x % 2, y, z)

    return pairs(move)


CORE_PAIRS = pairs(lambda xh, co, xl, y, z: (xh, 1 - co, xl, y, z))


def slab_shift(k):
    return [
        (g * 32 + s, g * 32 + s + k) for g in range(4) for s in range(32) if 0 <= s + k < 32
    ]


def permute(x, table):
    return lax.ppermute(x, BOTH, table)


def slab_of(idx, kb, ka, kl):
    b = (idx[1] + kb) & 3
    a = (idx[2] + ka) & 3
    xl = (idx[3] + kl) & 1
    core = idx[0]
    y = jnp.where(core == 0, a, b)
    z = jnp.where(core == 0, b, a)
    return xl * 16 + y * 4 + z


def pair_sum_kernel(idx, ja_ref, jb_ref, o0, o1, o2, o3, page):
    shift = pl.multiple_of(idx[0] * 8, 8)
    for kb, out in enumerate((o0, o1, o2, o3)):

        def step(t, carry):
            slab = slab_of(idx, kb, t // 2, t % 2)
            for j in range(3):
                page[...] = ja_ref[slab * 3 + j].astype(F32) + jb_ref[slab * 3 + j].astype(F32)
                out[t, j] = page[pl.ds(shift, OWN), :]
            return carry

        lax.fori_loop(0, 8, step, 0)


def pair_sum(idx, ja, jb):
    vm = pl.BlockSpec(memory_space=pltpu.VMEM)
    return pl.pallas_call(
        pair_sum_kernel,
        out_shape=[jax.ShapeDtypeStruct((8, 3, OWN, NY), F32)] * 4,
        in_specs=[pl.BlockSpec(memory_space=pltpu.SMEM), vm, vm],
        out_specs=[vm] * 4,
        scratch_shapes=[pltpu.VMEM((WIN, NY), F32)],
        compiler_params=pltpu.CompilerParams(vmem_limit_bytes=24 << 20),
        cost_estimate=pl.CostEstimate(flops=10**6, bytes_accessed=6 * 10**6, transcendentals=0),
        name="pair_sum",
    )(idx, ja, jb)


CHUNK = 4
TOP = 16


def split(product):
    high = product.astype(BF16)
    low = (product - high.astype(F32)).astype(BF16)
    return jnp.concatenate([high, low], axis=1)


def factor_kernel(
    idx, i_ref, ja_ref, jb_ref, o0, o1, o2, o3, cc_ref, iext_ref,
    raw, line, three, ring, zsum,
):
    shift = pl.multiple_of(idx[0] * 8, 8)
    rows = lax.broadcasted_iota(jnp.int32, (2 * NY, NY), 0)
    cols = lax.broadcasted_iota(jnp.int32, (2 * NY, NY), 1)
    away = jnp.abs((rows & (NY - 1)) - cols)
    band2 = jnp.where(away <= RADIUS, 1.0, 0.0).astype(BF16)
    band1 = band2[:NY]
    zero_page = jnp.zeros((OWN, NY), F32)
    line[...] = jnp.zeros(line.shape, F32)
    for v in range(8):
        for p in range(8):
            ring[v, p] = zero_page
        zsum[v, 0] = zero_page
        zsum[v, 1] = zero_page

    def chunk(i, carry):
        base = i * CHUNK

        @pl.when(i < NZ // CHUNK)
        def _():
            def load(ref):
                return ref[pl.ds(base, CHUNK)].reshape(CHUNK * WIN, NY)

            bi, ba, bb = load(i_ref), load(ja_ref), load(jb_ref)
            fi, fa, fb = bi.astype(F32), ba.astype(F32), bb.astype(F32)
            for n, f in enumerate((fi, fa, fb)):
                raw[n, pl.ds(base, CHUNK)] = f.reshape(CHUNK, WIN, NY)

            def dot(lhs, rhs):
                return jnp.dot(lhs, rhs, preferred_element_type=F32)

            makers = (
                lambda: dot(bi, band1),
                lambda: dot(split(fi * fi), band2),
                lambda: dot(ba, band1),
                lambda: dot(split(fa * fa), band2),
                lambda: dot(split(fi * fa), band2),
                lambda: dot(bb, band1),
                lambda: dot(split(fb * fb), band2),
                lambda: dot(split(fi * fb), band2),
            )
            for v in range(8):
                sums = makers[v]()
                for j in range(CHUNK):
                    line[v, j, pl.ds(TOP, WIN), :] = sums[j * WIN : (j + 1) * WIN]
            for v in range(8):
                for j in range(CHUNK):
                    three[v, j, pl.ds(8, 72), :] = (
                        line[v, j, pl.ds(7, 72), :]
                        + line[v, j, pl.ds(8, 72), :]
                        + line[v, j, pl.ds(9, 72), :]
                    )
            for v in range(8):
                for j in range(CHUNK):
                    slot = (base + j) & 7
                    ring[v, slot] = (
                        three[v, j, pl.ds(TOP - 3 + shift, OWN), :]
                        + three[v, j, pl.ds(TOP + shift, OWN), :]
                        + three[v, j, pl.ds(TOP + 3 + shift, OWN), :]
                    )

        @pl.when(i >= NZ // CHUNK)
        def _():
            for v in range(8):
                for j in range(CHUNK):
                    ring[v, (base + j) & 7] = zero_page

        for v in range(8):
            for j in range(CHUNK):
                z = base - 1 + j
                zsum[v, z + 3] = ring[v, (z + 7) & 7] + ring[v, z & 7] + ring[v, (z + 1) & 7]
        return carry

    lax.fori_loop(0, NZ // CHUNK + 1, chunk, 0)

    eps_b = EPSILON * COUNT**2
    eps_bc = EPSILON * COUNT**4

    def block(out, kb, t, cc):
        slab = slab_of(idx, kb, t // 2, t % 2)
        for j in range(3):
            z = slab * 3 + j
            for r in range(OWN // 8):
                part = pl.ds(r * 8, 8)

                def box(v):
                    return zsum[v, z, part, :] + zsum[v, z + 3, part, :] + zsum[v, z + 6, part, :]

                own = pl.ds(shift + r * 8, 8)
                si = box(0)
                var_i = COUNT * box(1) - si * si
                centred = raw[0, z, own, :] - si * (1.0 / COUNT)
                slope = centred / (var_i + eps_b)
                total = None
                for n in range(2):
                    sj = box(2 + 3 * n)
                    var_j = COUNT * box(3 + 3 * n) - sj * sj
                    cross = COUNT * box(4 + 3 * n) - si * sj
                    gain = cross / (var_i * var_j + eps_bc)
                    cc = cc + cross * gain
                    moved = raw[1 + n, z, own, :] - sj * (1.0 / COUNT) - cross * slope
                    term = gain * moved
                    total = term if total is None else total + term
                out[t, j, part, :] = total * (2.0 * COUNT**2)
        return cc

    cc = jnp.zeros((8, NY), F32)
    for kb, out in enumerate((o0, o1, o2, o3)):
        cc = lax.fori_loop(0, 8, lambda t, cc, out=out, kb=kb: block(out, kb, t, cc), cc)
    cc_ref[...] = cc

    start = idx[4] * 3 - 6
    for j in range(15):
        z = start + j
        inside = jnp.logical_and(z >= 0, z < NZ)
        page = raw[0, jnp.clip(z, 0, NZ - 1), pl.ds(shift, OWN), :]
        iext_ref[j] = jnp.where(inside, page, 0.0)


def factors(idx, image, ja, jb):
    vm = pl.BlockSpec(memory_space=pltpu.VMEM)
    block = jax.ShapeDtypeStruct((8, 3, OWN, NY), F32)
    return pl.pallas_call(
        factor_kernel,
        out_shape=[block] * 4
        + [jax.ShapeDtypeStruct((8, NY), F32), jax.ShapeDtypeStruct((15, OWN, NY), F32)],
        in_specs=[pl.BlockSpec(memory_space=pltpu.SMEM), vm, vm, vm],
        out_specs=[vm] * 6,
        scratch_shapes=[
            pltpu.VMEM((3, NZ, WIN, NY), F32),
            pltpu.VMEM((8, CHUNK, 88, NY), F32),
            pltpu.VMEM((8, CHUNK, 88, NY), F32),
            pltpu.VMEM((8, 8, OWN, NY), F32),
            pltpu.VMEM((8, NZ + 6, OWN, NY), F32),
        ],
        compiler_params=pltpu.CompilerParams(vmem_limit_bytes=60 << 20),
        cost_estimate=pl.CostEstimate(flops=10**9, bytes_accessed=10**7, transcendentals=0),
        name="factors",
    )(idx, image, ja, jb)


def gauss(extent):
    weights = [math.exp(-o * o / (2.0 * VARIANCE)) for o in range(-extent, extent + 1)]
    total = sum(weights)
    return [w / total for w in weights]


def smooth_kernel(f_ref, i_ref, u_ref, sq_ref, prod):
    weights = gauss(REACH)
    norm = sum(math.exp(-o * o / (2.0 * VARIANCE)) for o in range(-REACH, REACH + 1))

    def matrix(n):
        r = lax.broadcasted_iota(jnp.int32, (n, n), 0)
        c = lax.broadcasted_iota(jnp.int32, (n, n), 1)
        d = (r - c).astype(F32)
        return jnp.where(jnp.abs(r - c) <= REACH, jnp.exp(-d * d / (2.0 * VARIANCE)) / norm, 0.0)

    gx, gy = matrix(NX), matrix(NY)
    row = lax.broadcasted_iota(jnp.int32, (NX, NY), 0)
    lane = lax.broadcasted_iota(jnp.int32, (NX, NY), 1)
    for p in range(13):
        f = f_ref[p] * 0.5
        here = i_ref[p + 1]
        prod[0, p] = f * (i_ref[p + 2] - i_ref[p])
        below = jnp.where(row == NX - 1, 0.0, pltpu.roll(here, NX - 1, 0))
        above = jnp.where(row == 0, 0.0, pltpu.roll(here, 1, 0))
        prod[1, p] = f * (below - above)
        right = jnp.where(lane == NY - 1, 0.0, pltpu.roll(here, NY - 1, 1))
        left = jnp.where(lane == 0, 0.0, pltpu.roll(here, 1, 1))
        prod[2, p] = f * (right - left)
    square = jnp.zeros((NX, NY), F32)
    for d in range(3):
        for j in range(3):
            acc = prod[d, j] * weights[0]
            for o in range(1, 11):
                acc = acc + prod[d, j + o] * weights[o]
            acc = jnp.dot(acc, gy, precision=HIGH, preferred_element_type=F32)
            acc = jnp.dot(gx, acc, precision=HIGH, preferred_element_type=F32)
            u = acc * (1.0 / DEVICES)
            u_ref[j, d] = u
            square = square + u * u
    sq_ref[...] = jnp.sum(square, axis=0, keepdims=True)


def smooth_slab(f, image):
    vm = pl.BlockSpec(memory_space=pltpu.VMEM)
    return pl.pallas_call(
        smooth_kernel,
        out_shape=[
            jax.ShapeDtypeStruct((3, 3, NX, NY), F32),
            jax.ShapeDtypeStruct((1, NY), F32),
        ],
        in_specs=[vm, vm],
        out_specs=[vm, vm],
        scratch_shapes=[pltpu.VMEM((3, 13, NX, NY), F32)],
        compiler_params=pltpu.CompilerParams(vmem_limit_bytes=24 << 20),
        name="smooth_slab",
    )(f, image)


def two_rounds(blocks):
    got = [permute(blocks[k], first_round(k)) for k in (1, 2, 3)]
    total = blocks[0] + got[0] + got[1] + got[2]
    parts = [total[2 * k : 2 * k + 2] for k in range(4)]
    got = [permute(parts[k], second_round(k)) for k in (1, 2, 3)]
    return parts[0] + got[0] + got[1] + got[2]


def on_device(template, subjects):
    grp = lax.axis_index("grp")
    sub = lax.axis_index("sub")
    core = grp % 2
    xl, y, z = sub // 16, (sub // 4) % 4, sub % 4
    first = jnp.where(core == 0, z, y)
    second = jnp.where(core == 0, y, z)
    idx = jnp.stack([core, first, second, xl, sub]).astype(jnp.int32)

    moving = subjects[0]
    keep = lax.dynamic_slice_in_dim(moving, 40 * core, WIN, axis=1)
    give = lax.dynamic_slice_in_dim(moving, 40 * (1 - core), WIN, axis=1)
    take = permute(give, CORE_PAIRS)

    mine = lax.dynamic_slice_in_dim(template, 40 * core, WIN, axis=1)
    image = lax.all_to_all(
        jnp.broadcast_to(mine[None], (32, 3, WIN, NY)), "sub", 0, 0, tiled=True
    ).reshape(NZ, WIN, NY)

    j_blocks = pair_sum(idx, keep, take)
    *f_blocks, cc, i_half = factors(idx, image, keep, take)
    j_part = two_rounds(j_blocks)
    f_part = two_rounds(f_blocks)
    both = jnp.concatenate([f_part, j_part], axis=1)
    half = both[0] + permute(both[0], third_round(2))
    half = half + permute(both[1], third_round(1)) + permute(both[1], third_round(3))

    def joined(own):
        other = permute(own, CORE_PAIRS)
        low = jnp.where(core == 0, own, other)
        high = jnp.where(core == 0, other, own)
        return jnp.concatenate([low, high], axis=1)

    i_slab = joined(i_half.astype(BF16)).astype(F32)
    slab = joined(half)
    f_slab, m_slab = slab[:3], slab[3:] * (1.0 / DEVICES)
    up1 = permute(jnp.concatenate([f_slab, m_slab[2:]], axis=0), slab_shift(1))
    up2 = permute(f_slab[1:], slab_shift(2))
    down1 = permute(jnp.concatenate([f_slab, m_slab[:1]], axis=0), slab_shift(-1))
    down2 = permute(f_slab[:2], slab_shift(-2))
    f_ext = jnp.concatenate([up2, up1[:3], f_slab, down1[:3], down2], axis=0)
    u, square = smooth_slab(f_ext, i_slab)

    msq = jnp.sum(m_slab * m_slab)
    cc = jnp.sum(cc)
    lane = lax.broadcasted_iota(jnp.int32, (1, NY), 1)
    cc_row = jnp.where(lane == 0, cc, 0.0)
    cc_row = cc_row + permute(cc_row, CORE_PAIRS)
    cc_row = cc_row + permute(cc_row, pairs(lambda xh, co, xl, y, z: (1 - xh, co, xl, y, z)))
    row = jnp.where(lane == 0, jnp.sum(square), jnp.where(lane == 1, msq, jnp.sum(cc_row)))
    rows = lax.all_to_all(jnp.broadcast_to(row[None], (32, 1, NY)), "sub", 0, 0, tiled=True)
    totals = jnp.sum(rows[:, 0, :3], axis=0)

    cells = NZ * NX * NY
    velocity_norm = jnp.sqrt(totals[0] / cells + EPSILON)
    image_norm = jnp.sqrt(totals[1] / cells + EPSILON)
    velocity = u * (STEP_LENGTH / velocity_norm)
    m_ext = jnp.concatenate([up1[3:], m_slab, down1[3:]], axis=0)
    slope_z = (m_ext[2:] - m_ext[:-2]) * 0.5
    padded_x = jnp.pad(m_slab, ((0, 0), (1, 1), (0, 0)))
    slope_x = (padded_x[:, 2:] - padded_x[:, :-2]) * 0.5
    padded_y = jnp.pad(m_slab, ((0, 0), (0, 0), (1, 1)))
    slope_y = (padded_y[:, :, 2:] - padded_y[:, :, :-2]) * 0.5
    advected = velocity[:, 0] * slope_z + velocity[:, 1] * slope_x + velocity[:, 2] * slope_y
    new_template = (m_slab - advected) / image_norm
    similarity = totals[2] / (DEVICES * cells)
    return velocity, new_template, similarity


def solution(mesh):
    return jax.shard_map(
        on_device,
        mesh=mesh,
        in_specs=(P("sub", None, None), P(("grp", "sub"), None, None, None)),
        out_specs=(P("sub", None, None, None), P("sub", None, None), P()),
        check_vma=False,
    )
```

```python
import math

import jax
import jax.numpy as jnp
from jax import lax
from jax.experimental import pallas as pl
from jax.experimental.pallas import tpu as pltpu
from jax.sharding import PartitionSpec as P

RADIUS = 4
REACH = 5
EPSILON = 1e-05
STEP_LENGTH = 0.5
VARIANCE = 3.0
HIGH = lax.Precision.HIGHEST
F32 = jnp.float32
BF16 = jnp.bfloat16

NZ, NX, NY = 96, 96, 128
WIN = 56
OWN = 48
COUNT = 729.0
BOTH = ("grp", "sub")
DEVICES = 128


def place(xh, co, xl, y, z):
    return (xh * 2 + co) * 32 + xl * 16 + y * 4 + z


def pairs(move):
    out = []
    for xh in range(2):
        for co in range(2):
            for xl in range(2):
                for y in range(4):
                    for z in range(4):
                        target = move(xh, co, xl, y, z)
                        if target is not None:
                            out.append((place(xh, co, xl, y, z), place(*target)))
    return out


def first_round(k):
    return pairs(
        lambda xh, co, xl, y, z: (xh, co, xl, y, (z + k) % 4) if co == 0 else (xh, co, xl, (y + k) % 4, z)
    )


def second_round(k):
    return pairs(
        lambda xh, co, xl, y, z: (xh, co, xl, (y + k) % 4, z) if co == 0 else (xh, co, xl, y, (z + k) % 4)
    )


def third_round(k):
    def move(xh, co, xl, y, z):
        x = (xh * 2 + xl + k) % 4
        return (x // 2, co, x % 2, y, z)

    return pairs(move)


CORE_PAIRS = pairs(lambda xh, co, xl, y, z: (xh, 1 - co, xl, y, z))


def slab_shift(k):
    return [
        (g * 32 + s, g * 32 + s + k) for g in range(4) for s in range(32) if 0 <= s + k < 32
    ]


def permute(x, table):
    return lax.ppermute(x, BOTH, table)


def slab_of(idx, kb, ka, kl):
    b = (idx[1] + kb) & 3
    a = (idx[2] + ka) & 3
    xl = (idx[3] + kl) & 1
    core = idx[0]
    y = jnp.where(core == 0, a, b)
    z = jnp.where(core == 0, b, a)
    return xl * 16 + y * 4 + z


def pair_sum_kernel(idx, ja_ref, jb_ref, o0, o1, o2, o3, page):
    shift = pl.multiple_of(idx[0] * 8, 8)
    for kb, out in enumerate((o0, o1, o2, o3)):

        def step(t, carry):
            slab = slab_of(idx, kb, t // 2, t % 2)
            for j in range(3):
                page[...] = ja_ref[slab * 3 + j].astype(F32) + jb_ref[slab * 3 + j].astype(F32)
                out[t, j] = page[pl.ds(shift, OWN), :]
            return carry

        lax.fori_loop(0, 8, step, 0)


def pair_sum(idx, ja, jb):
    vm = pl.BlockSpec(memory_space=pltpu.VMEM)
    return pl.pallas_call(
        pair_sum_kernel,
        out_shape=[jax.ShapeDtypeStruct((8, 3, OWN, NY), F32)] * 4,
        in_specs=[pl.BlockSpec(memory_space=pltpu.SMEM), vm, vm],
        out_specs=[vm] * 4,
        scratch_shapes=[pltpu.VMEM((WIN, NY), F32)],
        compiler_params=pltpu.CompilerParams(vmem_limit_bytes=24 << 20),
        cost_estimate=pl.CostEstimate(flops=10**6, bytes_accessed=6 * 10**6, transcendentals=0),
        name="pair_sum",
    )(idx, ja, jb)


CHUNK = 4
TOP = 16
PAGES = NZ + 8


def split(product):
    high = product.astype(BF16)
    low = (product - high.astype(F32)).astype(BF16)
    return jnp.concatenate([high, low], axis=1)


def bands():
    rows = lax.broadcasted_iota(jnp.int32, (2 * NY, NY), 0)
    cols = lax.broadcasted_iota(jnp.int32, (2 * NY, NY), 1)
    away = jnp.abs((rows & (NY - 1)) - cols)
    band2 = jnp.where(away <= RADIUS, 1.0, 0.0).astype(BF16)
    return band2[:NY], band2


def plane_sums(makers, shift, even, odd, three, plane):
    band1, band2 = bands()
    volumes = plane.shape[0]
    even[...] = jnp.zeros(even.shape, F32)
    odd[...] = jnp.zeros(odd.shape, F32)
    for v in range(volumes):
        for p in range(4):
            plane[v, NZ + 4 + p] = jnp.zeros((OWN, NY), F32)

    def along_y(thunk, v, line):
        sums = thunk(band1, band2)
        for j in range(CHUNK):
            line[v, j, pl.ds(TOP, WIN), :] = sums[j * WIN : (j + 1) * WIN]

    def along_x(v, line, base):
        for j in range(CHUNK):
            three[v, j] = (
                line[v, j, pl.ds(TOP - 9 + shift, 64), :]
                + line[v, j, pl.ds(TOP - 8 + shift, 64), :]
                + line[v, j, pl.ds(TOP - 7 + shift, 64), :]
            )
        for j in range(CHUNK):
            plane[v, base + j + 4] = (
                three[v, j, pl.ds(5, OWN), :]
                + three[v, j, pl.ds(8, OWN), :]
                + three[v, j, pl.ds(11, OWN), :]
            )

    def both(i, line, other):
        thunks = makers(i * CHUNK)
        for v in range(volumes):
            along_y(thunks[v], v, line)
            along_x(v, other, (i - 1) * CHUNK)

    def step(n, carry):
        both(2 * n, even, odd)
        both(2 * n + 1, odd, even)
        return carry

    lax.fori_loop(0, NZ // CHUNK // 2, step, 0)
    for v in range(volumes):
        along_x(v, odd, NZ - CHUNK)


def dot(lhs, rhs):
    return jnp.dot(lhs, rhs, preferred_element_type=F32)


def load(ref, base):
    return ref[pl.ds(base, CHUNK)].reshape(CHUNK * WIN, NY)


def moving_kernel(idx, ja_ref, jb_ref, plane, even, odd, three):
    shift = pl.multiple_of(idx[0] * 8, 8)

    def makers(base):
        out = []
        for ref in (ja_ref, jb_ref):

            def square(b1, b2, ref=ref):
                f = load(ref, base).astype(F32)
                return dot(split(f * f), b2)

            out.append(lambda b1, b2, ref=ref: dot(load(ref, base), b1))
            out.append(square)
        return out

    plane_sums(makers, shift, even, odd, three, plane)


def moving_planes(idx, ja, jb):
    vm = pl.BlockSpec(memory_space=pltpu.VMEM)
    return pl.pallas_call(
        moving_kernel,
        out_shape=jax.ShapeDtypeStruct((4, PAGES, OWN, NY), F32),
        in_specs=[pl.BlockSpec(memory_space=pltpu.SMEM), vm, vm],
        out_specs=vm,
        scratch_shapes=[
            pltpu.VMEM((4, CHUNK, 88, NY), F32),
            pltpu.VMEM((4, CHUNK, 88, NY), F32),
            pltpu.VMEM((4, CHUNK, 64, NY), F32),
        ],
        compiler_params=pltpu.CompilerParams(vmem_limit_bytes=24 << 20),
        cost_estimate=pl.CostEstimate(flops=4 * 10**9, bytes_accessed=13 * 10**6, transcendentals=0),
        name="moving_planes",
    )(idx, ja, jb)


def factor_kernel(
    idx, i_ref, ja_ref, jb_ref, jplane, o0, o1, o2, o3, cc_ref, iext_ref,
    raw, even, odd, three, iplane,
):
    shift = pl.multiple_of(idx[0] * 8, 8)

    def makers(base):
        def wide(n, keep):
            f = load((i_ref, ja_ref, jb_ref)[n], base).astype(F32)
            if keep:
                raw[n, pl.ds(base, CHUNK)] = f.reshape(CHUNK, WIN, NY)
            return f

        def square(b1, b2):
            f = wide(0, True)
            return dot(split(f * f), b2)

        return [
            lambda b1, b2: dot(load(i_ref, base), b1),
            square,
            lambda b1, b2: dot(split(wide(0, False) * wide(1, True)), b2),
            lambda b1, b2: dot(split(wide(0, False) * wide(2, True)), b2),
        ]

    plane_sums(makers, shift, even, odd, three, iplane)

    eps_b = EPSILON * COUNT**2
    eps_bc = EPSILON * COUNT**4

    def block(out, kb, t, cc):
        slab = slab_of(idx, kb, t // 2, t % 2)
        first = slab * 3
        for r in range(OWN // 8):
            part = pl.ds(r * 8, 8)

            def boxes(ref, v):
                pages = [ref[v, first + p, part, :] for p in range(11)]
                mid = pages[2]
                for p in range(3, 9):
                    mid = mid + pages[p]
                return (
                    mid + (pages[0] + pages[1]),
                    mid + (pages[1] + pages[9]),
                    mid + (pages[9] + pages[10]),
                )

            own = pl.ds(shift + r * 8, 8)
            si, sii = boxes(iplane, 0), boxes(iplane, 1)
            var_i = [COUNT * sii[j] - si[j] * si[j] for j in range(3)]
            slope = [
                (raw[0, first + j, own, :] - si[j] * (1.0 / COUNT)) / (var_i[j] + eps_b)
                for j in range(3)
            ]
            total = [None] * 3
            for n in range(2):
                sj, sjj = boxes(jplane, 2 * n), boxes(jplane, 2 * n + 1)
                sij = boxes(iplane, 2 + n)
                for j in range(3):
                    var_j = COUNT * sjj[j] - sj[j] * sj[j]
                    cross = COUNT * sij[j] - si[j] * sj[j]
                    gain = cross / (var_i[j] * var_j + eps_bc)
                    cc = cc + cross * gain
                    moved = raw[1 + n, first + j, own, :] - sj[j] * (1.0 / COUNT) - cross * slope[j]
                    term = gain * moved
                    total[j] = term if n == 0 else total[j] + term
            for j in range(3):
                out[t, j, part, :] = total[j] * (2.0 * COUNT**2)
        return cc

    cc = jnp.zeros((8, NY), F32)
    for kb, out in enumerate((o0, o1, o2, o3)):
        cc = lax.fori_loop(0, 8, lambda t, cc, out=out, kb=kb: block(out, kb, t, cc), cc)
    cc_ref[...] = cc

    start = idx[4] * 3 - 6
    for j in range(15):
        z = start + j
        inside = jnp.logical_and(z >= 0, z < NZ)
        page = raw[0, jnp.clip(z, 0, NZ - 1), pl.ds(shift, OWN), :]
        iext_ref[j] = jnp.where(inside, page, 0.0)


def factors(idx, image, ja, jb, jplane):
    vm = pl.BlockSpec(memory_space=pltpu.VMEM)
    block = jax.ShapeDtypeStruct((8, 3, OWN, NY), F32)
    return pl.pallas_call(
        factor_kernel,
        out_shape=[block] * 4
        + [jax.ShapeDtypeStruct((8, NY), F32), jax.ShapeDtypeStruct((15, OWN, NY), F32)],
        in_specs=[pl.BlockSpec(memory_space=pltpu.SMEM), vm, vm, vm, vm],
        out_specs=[vm] * 6,
        scratch_shapes=[
            pltpu.VMEM((3, NZ, WIN, NY), F32),
            pltpu.VMEM((4, CHUNK, 88, NY), F32),
            pltpu.VMEM((4, CHUNK, 88, NY), F32),
            pltpu.VMEM((4, CHUNK, 64, NY), F32),
            pltpu.VMEM((4, PAGES, OWN, NY), F32),
        ],
        compiler_params=pltpu.CompilerParams(vmem_limit_bytes=44 << 20),
        cost_estimate=pl.CostEstimate(flops=4 * 10**9, bytes_accessed=18 * 10**6, transcendentals=0),
        name="factors",
    )(idx, image, ja, jb, jplane)


EXT = 18
CC_ROWS = 8


def smooth_kernel(idx, own_ref, other_ref, iown_ref, iother_ref, u_ref, adv_ref, m_ref, st_ref, ext, image, prod):
    mine = pl.multiple_of(idx[0] * OWN, 8)
    others = pl.multiple_of((1 - idx[0]) * OWN, 8)
    for p in range(EXT):
        ext[p, pl.ds(mine, OWN), :] = own_ref[pl.ds(p * OWN, OWN), :]
        ext[p, pl.ds(others, OWN), :] = other_ref[pl.ds(p * OWN, OWN), :]
    for p in range(15):
        image[p, pl.ds(mine, OWN), :] = iown_ref[p]
        image[p, pl.ds(others, OWN), :] = iother_ref[p]

    weights = [math.exp(-o * o / (2.0 * VARIANCE)) for o in range(-REACH, REACH + 1)]
    norm = sum(weights)
    weights = [w / norm for w in weights]

    def matrix(n):
        r = lax.broadcasted_iota(jnp.int32, (n, n), 0)
        c = lax.broadcasted_iota(jnp.int32, (n, n), 1)
        d = (r - c).astype(F32)
        return jnp.where(jnp.abs(r - c) <= REACH, jnp.exp(-d * d / (2.0 * VARIANCE)) / norm, 0.0)

    gx, gy = matrix(NX), matrix(NY)
    row = lax.broadcasted_iota(jnp.int32, (NX, NY), 0)
    lane = lax.broadcasted_iota(jnp.int32, (NX, NY), 1)

    def twice_slopes(here):
        below = jnp.where(row == NX - 1, 0.0, pltpu.roll(here, NX - 1, 0))
        above = jnp.where(row == 0, 0.0, pltpu.roll(here, 1, 0))
        right = jnp.where(lane == NY - 1, 0.0, pltpu.roll(here, NY - 1, 1))
        left = jnp.where(lane == 0, 0.0, pltpu.roll(here, 1, 1))
        return below - above, right - left

    for p in range(13):
        f = ext[p] * 0.5
        sx, sy = twice_slopes(image[p + 1])
        prod[0, p] = f * (image[p + 2] - image[p])
        prod[1, p] = f * sx
        prod[2, p] = f * sy
    square = jnp.zeros((NX, NY), F32)
    image_square = jnp.zeros((NX, NY), F32)
    mean = 1.0 / DEVICES
    for j in range(3):
        m = ext[14 + j] * mean
        sx, sy = twice_slopes(m)
        slopes = ((ext[15 + j] - ext[13 + j]) * mean, sx, sy)
        image_square = image_square + m * m
        moved = None
        for d in range(3):
            acc = prod[d, j] * weights[0]
            for o in range(1, 11):
                acc = acc + prod[d, j + o] * weights[o]
            acc = jnp.dot(acc, gy, precision=HIGH, preferred_element_type=F32)
            acc = jnp.dot(gx, acc, precision=HIGH, preferred_element_type=F32)
            u = acc * mean
            u_ref[j, d] = u
            square = square + u * u
            term = u * slopes[d]
            moved = term if d == 0 else moved + term
        adv_ref[j] = moved * 0.5
        m_ref[j] = m
    tail = pl.ds(EXT * OWN, CC_ROWS)
    cc = jnp.sum(own_ref[tail, :] + other_ref[tail, :])
    one = lax.broadcasted_iota(jnp.int32, (1, NY), 1)
    st_ref[...] = jnp.where(
        one == 0, jnp.sum(square), jnp.where(one == 1, jnp.sum(image_square), cc)
    )


def smooth_slab(idx, own, other, iown, iother):
    vm = pl.BlockSpec(memory_space=pltpu.VMEM)
    return pl.pallas_call(
        smooth_kernel,
        out_shape=[
            jax.ShapeDtypeStruct((3, 3, NX, NY), F32),
            jax.ShapeDtypeStruct((3, NX, NY), F32),
            jax.ShapeDtypeStruct((3, NX, NY), F32),
            jax.ShapeDtypeStruct((1, NY), F32),
        ],
        in_specs=[pl.BlockSpec(memory_space=pltpu.SMEM), vm, vm, vm, vm],
        out_specs=[vm] * 4,
        scratch_shapes=[
            pltpu.VMEM((EXT, NX, NY), F32),
            pltpu.VMEM((15, NX, NY), F32),
            pltpu.VMEM((3, 13, NX, NY), F32),
        ],
        compiler_params=pltpu.CompilerParams(vmem_limit_bytes=24 << 20),
        cost_estimate=pl.CostEstimate(flops=10**8, bytes_accessed=3 * 10**6, transcendentals=0),
        name="smooth_slab",
    )(idx, own, other, iown, iother)


def after(value, *others):
    return lax.optimization_barrier((value, *others))[0]


def round_one(blocks):
    return [permute(blocks[k], first_round(k)) for k in (1, 2, 3)]


def round_two(total):
    parts = [total[2 * k : 2 * k + 2] for k in range(4)]
    got = [permute(parts[k], second_round(k)) for k in (1, 2, 3)]
    return parts[0] + got[0] + got[1] + got[2]


def on_device(template, subjects):
    grp = lax.axis_index("grp")
    sub = lax.axis_index("sub")
    core = grp % 2
    xl, y, z = sub // 16, (sub // 4) % 4, sub % 4
    first = jnp.where(core == 0, z, y)
    second = jnp.where(core == 0, y, z)
    idx = jnp.stack([core, first, second, xl, sub]).astype(jnp.int32)

    mine = lax.dynamic_slice_in_dim(template, 40 * core, WIN, axis=1)
    copies = jnp.broadcast_to(mine[None], (32, 3, WIN, NY))
    copies, moving = lax.optimization_barrier((copies, subjects))
    image = lax.all_to_all(copies, "sub", 0, 0, tiled=True).reshape(NZ, WIN, NY)

    moving = moving[0]
    give = lax.dynamic_slice_in_dim(moving, 40 * (1 - core), WIN, axis=1)
    take = permute(give, CORE_PAIRS)
    keep = lax.dynamic_slice_in_dim(moving, 40 * core, WIN, axis=1)

    j_blocks = pair_sum(idx, keep, take)
    jplane = moving_planes(after(idx, *j_blocks), keep, take)
    j_blocks, jplane = lax.optimization_barrier((j_blocks, jplane))
    j_got = round_one(j_blocks)
    *f_blocks, cc, i_half = factors(idx, image, keep, take, jplane)
    f_got = round_one(f_blocks)
    j_own = after(j_blocks[0], cc)
    j_part = round_two(j_own + j_got[0] + j_got[1] + j_got[2])
    f_part = round_two(f_blocks[0] + f_got[0] + f_got[1] + f_got[2])
    i_other = permute(i_half.astype(BF16), CORE_PAIRS).astype(F32)

    both = jnp.concatenate(
        [
            f_part.reshape(2, 3 * OWN, NY),
            j_part.reshape(2, 3 * OWN, NY),
            jnp.broadcast_to(cc[None], (2, CC_ROWS, NY)),
        ],
        axis=1,
    )
    half = both[0] + permute(both[0], third_round(2))
    half = half + permute(both[1], third_round(1)) + permute(both[1], third_round(3))

    f_half = half[: 3 * OWN]
    m_half = half[3 * OWN : 6 * OWN]
    up1 = permute(jnp.concatenate([f_half, m_half[2 * OWN :]], axis=0), slab_shift(1))
    down1 = permute(jnp.concatenate([f_half, m_half[:OWN]], axis=0), slab_shift(-1))
    up2 = permute(f_half[OWN:], slab_shift(2))
    down2 = permute(f_half[: 2 * OWN], slab_shift(-2))
    ext = jnp.concatenate(
        [
            up2, up1[: 3 * OWN], f_half, down1[: 3 * OWN], down2,
            up1[3 * OWN :], m_half, down1[3 * OWN :], half[6 * OWN :],
        ],
        axis=0,
    )
    other = permute(ext, CORE_PAIRS)
    u, advected, m, stats = smooth_slab(idx, ext, other, i_half, i_other)

    rows = lax.all_to_all(jnp.broadcast_to(stats[None], (32, 1, NY)), "sub", 0, 0, tiled=True)
    totals = jnp.sum(rows[:, 0, :3], axis=0)
    cells = NZ * NX * NY
    velocity_norm = jnp.sqrt(totals[0] / cells + EPSILON)
    image_norm = jnp.sqrt(totals[1] / cells + EPSILON)
    scale = STEP_LENGTH / velocity_norm
    velocity = u * scale
    new_template = (m - advected * scale) / image_norm
    similarity = totals[2] * 0.5 / (DEVICES * cells)
    return velocity, new_template, similarity


def solution(mesh):
    return jax.shard_map(
        on_device,
        mesh=mesh,
        in_specs=(P("sub", None, None), P(("grp", "sub"), None, None, None)),
        out_specs=(P("sub", None, None, None), P("sub", None, None), P()),
        check_vma=False,
    )
```

```python
import math

import jax
import jax.numpy as jnp
from jax import lax
from jax.experimental import pallas as pl
from jax.experimental.pallas import tpu as pltpu
from jax.sharding import PartitionSpec as P


RADIUS = 4
REACH = 5
EPSILON = 1e-05
STEP_LENGTH = 0.5
VARIANCE = 3.0
HIGH = lax.Precision.HIGHEST
F32 = jnp.float32
BF16 = jnp.bfloat16

NZ, NX, NY = 96, 96, 128
WIN = 56
OWN = 48
COUNT = 729.0
BOTH = ("grp", "sub")
DEVICES = 128


def place(xh, co, xl, y, z):
    return (xh * 2 + co) * 32 + xl * 16 + y * 4 + z


def pairs(move):
    out = []
    for xh in range(2):
        for co in range(2):
            for xl in range(2):
                for y in range(4):
                    for z in range(4):
                        target = move(xh, co, xl, y, z)
                        if target is not None:
                            out.append((place(xh, co, xl, y, z), place(*target)))
    return out


def first_round(k):
    return pairs(
        lambda xh, co, xl, y, z: (xh, co, xl, y, (z + k) % 4) if co == 0 else (xh, co, xl, (y + k) % 4, z)
    )


def second_round(k):
    return pairs(
        lambda xh, co, xl, y, z: (xh, co, xl, (y + k) % 4, z) if co == 0 else (xh, co, xl, y, (z + k) % 4)
    )


def third_round(k):
    def move(xh, co, xl, y, z):
        x = (xh * 2 + xl + k) % 4
        return (x // 2, co, x % 2, y, z)

    return pairs(move)


TWIN_PAIRS = pairs(lambda xh, co, xl, y, z: (1 - xh, co, xl, y, z))
CORE_PAIRS = pairs(lambda xh, co, xl, y, z: (xh, 1 - co, xl, y, z))


def slab_shift(k):
    return [
        (g * 32 + s, g * 32 + (s + (k if g < 2 else -k)) % 32) for g in range(4) for s in range(32)
    ]


def permute(x, table):
    return lax.ppermute(x, BOTH, table)


def slab_of(idx, kb, ka, kl):
    b = (idx[1] + kb) & 3
    a = (idx[2] + ka) & 3
    xl = (idx[3] + kl) & 1
    core = idx[0]
    y = jnp.where(core == 0, a, b)
    z = jnp.where(core == 0, b, a)
    return xl * 16 + y * 4 + z


def pair_sum_kernel(idx, ja_ref, jb_ref, o0, o1, o2, o3, page):
    shift = pl.multiple_of(idx[0] * 8, 8)
    for kb, out in enumerate((o0, o1, o2, o3)):

        def step(t, carry):
            slab = slab_of(idx, kb, t // 2, t % 2)
            for j in range(3):
                page[...] = ja_ref[slab * 3 + j].astype(F32) + jb_ref[slab * 3 + j].astype(F32)
                out[t, j] = page[pl.ds(shift, OWN), :]
            return carry

        lax.fori_loop(0, 8, step, 0)


def pair_sum(idx, ja, jb):
    vm = pl.BlockSpec(memory_space=pltpu.VMEM)
    return pl.pallas_call(
        pair_sum_kernel,
        out_shape=[jax.ShapeDtypeStruct((8, 3, OWN, NY), F32)] * 4,
        in_specs=[pl.BlockSpec(memory_space=pltpu.SMEM), vm, vm],
        out_specs=[vm] * 4,
        scratch_shapes=[pltpu.VMEM((WIN, NY), F32)],
        compiler_params=pltpu.CompilerParams(vmem_limit_bytes=24 << 20),
        cost_estimate=pl.CostEstimate(flops=10**6, bytes_accessed=6 * 10**6, transcendentals=0),
        name="pair_sum",
    )(idx, ja, jb)


TOP = 16
PAGES = NZ + 8


def split(product):
    high = product.astype(BF16)
    low = (product - high.astype(F32)).astype(BF16)
    return jnp.concatenate([high, low], axis=1)


def bands():
    rows = lax.broadcasted_iota(jnp.int32, (2 * NY, NY), 0)
    cols = lax.broadcasted_iota(jnp.int32, (2 * NY, NY), 1)
    away = jnp.abs((rows & (NY - 1)) - cols)
    band2 = jnp.where(away <= RADIUS, 1.0, 0.0).astype(BF16)
    return band2[:NY], band2


def plane_sums(makers, shift, even, odd, three, plane):
    band1, band2 = bands()
    volumes, chunk = three.shape[:2]
    even[...] = jnp.zeros(even.shape, F32)
    odd[...] = jnp.zeros(odd.shape, F32)
    for v in range(volumes):
        for p in range(4):
            plane[v, NZ + 4 + p] = jnp.zeros((OWN, NY), F32)

    def along_y(thunk, v, line):
        sums = thunk(band1, band2)
        for j in range(chunk):
            line[v, j, pl.ds(TOP, WIN), :] = sums[j * WIN : (j + 1) * WIN]

    def along_x(v, line, base):
        for j in range(chunk):
            three[v, j] = (
                line[v, j, pl.ds(TOP - 9 + shift, 64), :]
                + line[v, j, pl.ds(TOP - 8 + shift, 64), :]
                + line[v, j, pl.ds(TOP - 7 + shift, 64), :]
            )
        for j in range(chunk):
            plane[v, base + j + 4] = (
                three[v, j, pl.ds(5, OWN), :]
                + three[v, j, pl.ds(8, OWN), :]
                + three[v, j, pl.ds(11, OWN), :]
            )

    def both(i, line, other):
        thunks = makers(i * chunk)
        for v in range(volumes):
            along_y(thunks[v], v, line)
            along_x(v, other, (i - 1) * chunk)

    def step(n, carry):
        both(2 * n, even, odd)
        both(2 * n + 1, odd, even)
        return carry

    lax.fori_loop(0, NZ // chunk // 2, step, 0)
    for v in range(volumes):
        along_x(v, odd, NZ - chunk)


MOVING_CHUNK = 4
FACTOR_CHUNK = 2


def dot(lhs, rhs):
    return jnp.dot(lhs, rhs, preferred_element_type=F32)


def load(ref, base, chunk):
    return ref[pl.ds(base, chunk)].reshape(chunk * WIN, NY)


def moving_kernel(idx, ja_ref, jb_ref, plane, even, odd, three):
    shift = pl.multiple_of(idx[0] * 8, 8)

    def makers(base):
        out = []
        for ref in (ja_ref, jb_ref):

            def square(b1, b2, ref=ref):
                f = load(ref, base, MOVING_CHUNK).astype(F32)
                return dot(split(f * f), b2)

            out.append(lambda b1, b2, ref=ref: dot(load(ref, base, MOVING_CHUNK), b1))
            out.append(square)
        return out

    plane_sums(makers, shift, even, odd, three, plane)


def moving_planes(idx, ja, jb):
    vm = pl.BlockSpec(memory_space=pltpu.VMEM)
    return pl.pallas_call(
        moving_kernel,
        out_shape=jax.ShapeDtypeStruct((4, PAGES, OWN, NY), F32),
        in_specs=[pl.BlockSpec(memory_space=pltpu.SMEM), vm, vm],
        out_specs=vm,
        scratch_shapes=[
            pltpu.VMEM((4, MOVING_CHUNK, 88, NY), F32),
            pltpu.VMEM((4, MOVING_CHUNK, 88, NY), F32),
            pltpu.VMEM((4, MOVING_CHUNK, 64, NY), F32),
        ],
        compiler_params=pltpu.CompilerParams(vmem_limit_bytes=24 << 20),
        cost_estimate=pl.CostEstimate(flops=4 * 10**9, bytes_accessed=13 * 10**6, transcendentals=0),
        name="moving_planes",
    )(idx, ja, jb)


def factor_kernel(
    idx, i_ref, ja_ref, jb_ref, jplane_ref, o0, o1, o2, o3, cc_ref, iext_ref,
    raw, even, odd, three, iplane, jplane, sem,
):
    shift = pl.multiple_of(idx[0] * 8, 8)
    fetch = pltpu.make_async_copy(jplane_ref, jplane, sem)
    fetch.start()

    def makers(base):
        def wide(n, keep):
            f = load((i_ref, ja_ref, jb_ref)[n], base, FACTOR_CHUNK).astype(F32)
            if keep:
                raw[n, pl.ds(base, FACTOR_CHUNK)] = f.reshape(FACTOR_CHUNK, WIN, NY)
            return f

        def square(b1, b2):
            f = wide(0, True)
            return dot(split(f * f), b2)

        return [
            lambda b1, b2: dot(load(i_ref, base, FACTOR_CHUNK), b1),
            square,
            lambda b1, b2: dot(split(wide(0, False) * wide(1, True)), b2),
            lambda b1, b2: dot(split(wide(0, False) * wide(2, True)), b2),
        ]

    plane_sums(makers, shift, even, odd, three, iplane)
    fetch.wait()

    eps_b = EPSILON * COUNT**2
    eps_bc = EPSILON * COUNT**4

    def block(out, kb, t, cc):
        slab = slab_of(idx, kb, t // 2, t % 2)
        first = slab * 3
        for r in range(OWN // 8):
            part = pl.ds(r * 8, 8)

            def boxes(ref, v):
                pages = [ref[v, first + p, part, :] for p in range(11)]
                mid = pages[2]
                for p in range(3, 9):
                    mid = mid + pages[p]
                return (
                    mid + (pages[0] + pages[1]),
                    mid + (pages[1] + pages[9]),
                    mid + (pages[9] + pages[10]),
                )

            own = pl.ds(shift + r * 8, 8)
            si, sii = boxes(iplane, 0), boxes(iplane, 1)
            var_i = [COUNT * sii[j] - si[j] * si[j] for j in range(3)]
            slope = [
                (raw[0, first + j, own, :] - si[j] * (1.0 / COUNT)) / (var_i[j] + eps_b)
                for j in range(3)
            ]
            total = [None] * 3
            for n in range(2):
                sj, sjj = boxes(jplane, 2 * n), boxes(jplane, 2 * n + 1)
                sij = boxes(iplane, 2 + n)
                for j in range(3):
                    var_j = COUNT * sjj[j] - sj[j] * sj[j]
                    cross = COUNT * sij[j] - si[j] * sj[j]
                    gain = cross / (var_i[j] * var_j + eps_bc)
                    cc = cc + cross * gain
                    moved = raw[1 + n, first + j, own, :] - sj[j] * (1.0 / COUNT) - cross * slope[j]
                    term = gain * moved
                    total[j] = term if n == 0 else total[j] + term
            for j in range(3):
                out[t, j, part, :] = total[j] * (2.0 * COUNT**2)
        return cc

    cc = jnp.zeros((8, NY), F32)
    for kb, out in enumerate((o0, o1, o2, o3)):
        cc = lax.fori_loop(0, 8, lambda t, cc, out=out, kb=kb: block(out, kb, t, cc), cc)
    cc_ref[...] = cc

    start = idx[4] * 3 - 6
    for j in range(15):
        z = start + j
        inside = jnp.logical_and(z >= 0, z < NZ)
        page = raw[0, jnp.clip(z, 0, NZ - 1), pl.ds(shift, OWN), :]
        iext_ref[j] = jnp.where(inside, page, 0.0)


def factors(idx, image, ja, jb, jplane):
    vm = pl.BlockSpec(memory_space=pltpu.VMEM)
    block = jax.ShapeDtypeStruct((8, 3, OWN, NY), F32)
    return pl.pallas_call(
        factor_kernel,
        out_shape=[block] * 4
        + [jax.ShapeDtypeStruct((8, NY), F32), jax.ShapeDtypeStruct((15, OWN, NY), F32)],
        in_specs=[pl.BlockSpec(memory_space=pltpu.SMEM), vm, vm, vm]
        + [pl.BlockSpec(memory_space=pl.ANY)],
        out_specs=[vm] * 6,
        scratch_shapes=[
            pltpu.VMEM((3, NZ, WIN, NY), F32),
            pltpu.VMEM((4, FACTOR_CHUNK, 88, NY), F32),
            pltpu.VMEM((4, FACTOR_CHUNK, 88, NY), F32),
            pltpu.VMEM((4, FACTOR_CHUNK, 64, NY), F32),
            pltpu.VMEM((4, PAGES, OWN, NY), F32),
            pltpu.VMEM((4, PAGES, OWN, NY), F32),
            pltpu.SemaphoreType.DMA,
        ],
        compiler_params=pltpu.CompilerParams(vmem_limit_bytes=48 << 20),
        cost_estimate=pl.CostEstimate(flops=4 * 10**9, bytes_accessed=18 * 10**6, transcendentals=0),
        name="factors",
    )(idx, image, ja, jb, jplane)


CC_ROWS = 8
SIDE = 6 * OWN
CENTRE = 6 * OWN + CC_ROWS


def smooth_kernel(
    idx, own_ref, twin_ref, other_ref, iown_ref, iother_ref, u_ref, adv_ref, m_ref, st_ref,
    ext, mext, image, prod,
):
    core, sub, xh = idx[0], idx[4], idx[5]
    mine = pl.multiple_of(core * OWN, 8)
    others = pl.multiple_of((1 - core) * OWN, 8)

    def centre(rows, ref):
        for j in range(3):
            ext[5 + j, rows, :] = ref[pl.ds(j * OWN, OWN), :]
            mext[1 + j, rows, :] = ref[pl.ds((3 + j) * OWN, OWN), :]

    def sides(rows, low, high):
        for d, (ref, at) in enumerate((low, high)):
            for j in range(5):
                z = sub * 3 + (j - 5 if d == 0 else j + 3)
                inside = jnp.logical_and(z >= 0, z < NZ)
                page = ref[pl.ds(at + j * OWN, OWN), :]
                ext[j if d == 0 else 8 + j, rows, :] = jnp.where(inside, page, 0.0)
            z = sub * 3 + (-1 if d == 0 else 3)
            inside = jnp.logical_and(z >= 0, z < NZ)
            page = ref[pl.ds(at + 5 * OWN, OWN), :]
            mext[0 if d == 0 else 4, rows, :] = jnp.where(inside, page, 0.0)

    my_rows, other_rows = pl.ds(mine, OWN), pl.ds(others, OWN)
    centre(my_rows, own_ref)
    centre(other_rows, other_ref)

    @pl.when(xh == 0)
    def _():
        sides(my_rows, (own_ref, CENTRE), (twin_ref, 0))
        sides(other_rows, (other_ref, CENTRE), (other_ref, CENTRE + SIDE))

    @pl.when(xh == 1)
    def _():
        sides(my_rows, (twin_ref, 0), (own_ref, CENTRE))
        sides(other_rows, (other_ref, CENTRE + SIDE), (other_ref, CENTRE))

    for p in range(15):
        image[p, my_rows, :] = iown_ref[p]
        image[p, other_rows, :] = iother_ref[p].astype(F32)

    weights = [math.exp(-o * o / (2.0 * VARIANCE)) for o in range(-REACH, REACH + 1)]
    norm = sum(weights)
    weights = [w / norm for w in weights]

    def matrix(n):
        r = lax.broadcasted_iota(jnp.int32, (n, n), 0)
        c = lax.broadcasted_iota(jnp.int32, (n, n), 1)
        d = (r - c).astype(F32)
        return jnp.where(jnp.abs(r - c) <= REACH, jnp.exp(-d * d / (2.0 * VARIANCE)) / norm, 0.0)

    gx, gy = matrix(NX), matrix(NY)
    row = lax.broadcasted_iota(jnp.int32, (NX, NY), 0)
    lane = lax.broadcasted_iota(jnp.int32, (NX, NY), 1)

    def twice_slopes(here):
        below = jnp.where(row == NX - 1, 0.0, pltpu.roll(here, NX - 1, 0))
        above = jnp.where(row == 0, 0.0, pltpu.roll(here, 1, 0))
        right = jnp.where(lane == NY - 1, 0.0, pltpu.roll(here, NY - 1, 1))
        left = jnp.where(lane == 0, 0.0, pltpu.roll(here, 1, 1))
        return below - above, right - left

    for p in range(13):
        f = ext[p] * 0.5
        sx, sy = twice_slopes(image[p + 1])
        prod[0, p] = f * (image[p + 2] - image[p])
        prod[1, p] = f * sx
        prod[2, p] = f * sy
    square = jnp.zeros((NX, NY), F32)
    image_square = jnp.zeros((NX, NY), F32)
    mean = 1.0 / DEVICES
    for j in range(3):
        m = mext[1 + j] * mean
        sx, sy = twice_slopes(m)
        slopes = ((mext[2 + j] - mext[j]) * mean, sx, sy)
        image_square = image_square + m * m
        moved = None
        for d in range(3):
            acc = prod[d, j] * weights[0]
            for o in range(1, 11):
                acc = acc + prod[d, j + o] * weights[o]
            acc = jnp.dot(acc, gy, precision=HIGH, preferred_element_type=F32)
            acc = jnp.dot(gx, acc, precision=HIGH, preferred_element_type=F32)
            u = acc * mean
            u_ref[j, d] = u
            square = square + u * u
            term = u * slopes[d]
            moved = term if d == 0 else moved + term
        adv_ref[j] = moved * 0.5
        m_ref[j] = m
    tail = pl.ds(6 * OWN, CC_ROWS)
    cc = jnp.sum(own_ref[tail, :] + other_ref[tail, :])
    one = lax.broadcasted_iota(jnp.int32, (1, NY), 1)
    st_ref[...] = jnp.where(
        one == 0, jnp.sum(square), jnp.where(one == 1, jnp.sum(image_square), cc)
    )


def smooth_slab(idx, own, twin, other, iown, iother):
    vm = pl.BlockSpec(memory_space=pltpu.VMEM)
    return pl.pallas_call(
        smooth_kernel,
        out_shape=[
            jax.ShapeDtypeStruct((3, 3, NX, NY), F32),
            jax.ShapeDtypeStruct((3, NX, NY), F32),
            jax.ShapeDtypeStruct((3, NX, NY), F32),
            jax.ShapeDtypeStruct((1, NY), F32),
        ],
        in_specs=[pl.BlockSpec(memory_space=pltpu.SMEM), vm, vm, vm, vm, vm],
        out_specs=[vm] * 4,
        scratch_shapes=[
            pltpu.VMEM((13, NX, NY), F32),
            pltpu.VMEM((5, NX, NY), F32),
            pltpu.VMEM((15, NX, NY), F32),
            pltpu.VMEM((3, 13, NX, NY), F32),
        ],
        compiler_params=pltpu.CompilerParams(vmem_limit_bytes=24 << 20),
        cost_estimate=pl.CostEstimate(flops=10**8, bytes_accessed=3 * 10**6, transcendentals=0),
        name="smooth_slab",
    )(idx, own, twin, other, iown, iother)


def finish_kernel(rows_ref, u_ref, adv_ref, m_ref, v_ref, t_ref, sim_ref):
    totals = jnp.sum(rows_ref[...], axis=0, keepdims=True)
    cells = NZ * NX * NY
    velocity_scale = STEP_LENGTH / jnp.sqrt(totals[:, 0:1] / cells + EPSILON)
    image_scale = 1.0 / jnp.sqrt(totals[:, 1:2] / cells + EPSILON)
    sim_ref[...] = totals[:, 2:3] * (0.5 / (DEVICES * cells))
    for j in range(3):
        for d in range(3):
            v_ref[j, d] = u_ref[j, d] * velocity_scale
        t_ref[j] = (m_ref[j] - adv_ref[j] * velocity_scale) * image_scale


def finish(rows, u, advected, m):
    vm = pl.BlockSpec(memory_space=pltpu.VMEM)
    return pl.pallas_call(
        finish_kernel,
        out_shape=[
            jax.ShapeDtypeStruct((3, 3, NX, NY), F32),
            jax.ShapeDtypeStruct((3, NX, NY), F32),
            jax.ShapeDtypeStruct((1, 1), F32),
        ],
        in_specs=[vm] * 4,
        out_specs=[vm] * 3,
        compiler_params=pltpu.CompilerParams(vmem_limit_bytes=12 << 20),
        name="finish",
    )(rows, u, advected, m)


def after(value, *others):
    return lax.optimization_barrier((value, *others))[0]


def round_one(blocks):
    return [permute(blocks[k], first_round(k)) for k in (1, 2, 3)]


def round_two(total):
    parts = [total[2 * k : 2 * k + 2] for k in range(4)]
    got = [permute(parts[k], second_round(k)) for k in (1, 2, 3)]
    return parts[0] + got[0] + got[1] + got[2]


def step(template, subjects):
    grp = lax.axis_index("grp")
    sub = lax.axis_index("sub")
    core = grp % 2
    xl, y, z = sub // 16, (sub // 4) % 4, sub % 4
    first = jnp.where(core == 0, z, y)
    second = jnp.where(core == 0, y, z)
    idx = jnp.stack([core, first, second, xl, sub, grp // 2]).astype(jnp.int32)

    mine = lax.dynamic_slice_in_dim(template, 40 * core, WIN, axis=1)
    copies = jnp.broadcast_to(mine[None], (32, 3, WIN, NY))
    copies, moving = lax.optimization_barrier((copies, subjects))
    image = lax.all_to_all(copies, "sub", 0, 0, tiled=True).reshape(NZ, WIN, NY)

    moving = moving[0]
    give = lax.dynamic_slice_in_dim(moving, 40 * (1 - core), WIN, axis=1)
    take = permute(give, CORE_PAIRS)
    keep = lax.dynamic_slice_in_dim(moving, 40 * core, WIN, axis=1)

    j_blocks = pair_sum(idx, keep, take)
    jplane = moving_planes(after(idx, *j_blocks), keep, take)
    j_got = round_one(j_blocks)
    *f_blocks, cc, i_half = factors(idx, image, keep, take, jplane)
    f_got = round_one(f_blocks)
    j_own = after(j_blocks[0], cc)
    j_total = j_own + j_got[0] + j_got[1] + j_got[2]
    j_part = round_two(j_total)
    i_other = permute(i_half.astype(BF16), CORE_PAIRS)
    f_total = f_blocks[0] + f_got[0] + f_got[1] + f_got[2]
    f_part = round_two(f_total)

    both = jnp.concatenate(
        [
            f_part.reshape(2, 3 * OWN, NY),
            j_part.reshape(2, 3 * OWN, NY),
            jnp.broadcast_to(cc[None], (2, CC_ROWS, NY)),
        ],
        axis=1,
    )
    half = both[0] + permute(both[0], third_round(2))
    half = half + permute(both[1], third_round(1)) + permute(both[1], third_round(3))

    f_half = half[: 3 * OWN]
    m_half = half[3 * OWN : 6 * OWN]
    low = grp < 2
    near = jnp.concatenate(
        [f_half, jnp.where(low, m_half[2 * OWN :], m_half[:OWN])], axis=0
    )
    far = jnp.where(low, f_half[OWN:], f_half[: 2 * OWN])
    near = permute(near, slab_shift(1))
    far = permute(far, slab_shift(2))
    near_f, near_m = near[: 3 * OWN], near[3 * OWN :]
    f_side = jnp.where(
        low, jnp.concatenate([far, near_f], axis=0), jnp.concatenate([near_f, far], axis=0)
    )
    side = jnp.concatenate([f_side, near_m], axis=0)
    twin = permute(side, TWIN_PAIRS)
    own = jnp.concatenate([half, side], axis=0)
    other = permute(jnp.concatenate([own, twin], axis=0), CORE_PAIRS)
    u, advected, m, stats = smooth_slab(idx, own, twin, other, i_half, i_other)
    rows = lax.all_to_all(jnp.broadcast_to(stats[None], (32, 1, NY)), "sub", 0, 0, tiled=True)
    velocity, new_template, similarity = finish(rows.reshape(32, NY), u, advected, m)
    return velocity, new_template, similarity.reshape(())


def solution(mesh):
    return jax.shard_map(
        step,
        mesh=mesh,
        in_specs=(P("sub", None, None), P(("grp", "sub"), None, None, None)),
        out_specs=(P("sub", None, None, None), P("sub", None, None), P()),
        check_vma=False,
    )
```

```python
import math

import jax
import jax.numpy as jnp
from jax import lax
from jax.experimental import pallas as pl
from jax.experimental.pallas import tpu as pltpu
from jax.sharding import PartitionSpec as P


RADIUS = 4
REACH = 5
EPSILON = 1e-05
STEP_LENGTH = 0.5
VARIANCE = 3.0
F32 = jnp.float32
BF16 = jnp.bfloat16

NZ, NX, NY = 96, 96, 128
WIN = 56
OWN = 48
COUNT = 729.0
BOTH = ("grp", "sub")
DEVICES = 128


def place(xh, co, xl, y, z):
    return (xh * 2 + co) * 32 + xl * 16 + y * 4 + z


def pairs(move):
    out = []
    for xh in range(2):
        for co in range(2):
            for xl in range(2):
                for y in range(4):
                    for z in range(4):
                        target = move(xh, co, xl, y, z)
                        if target is not None:
                            out.append((place(xh, co, xl, y, z), place(*target)))
    return out


def first_round(k):
    return pairs(
        lambda xh, co, xl, y, z: (xh, co, xl, y, (z + k) % 4) if co == 0 else (xh, co, xl, (y + k) % 4, z)
    )


def second_round(k):
    return pairs(
        lambda xh, co, xl, y, z: (xh, co, xl, (y + k) % 4, z) if co == 0 else (xh, co, xl, y, (z + k) % 4)
    )


def third_round(k):
    def move(xh, co, xl, y, z):
        x = (xh * 2 + xl + k) % 4
        return (x // 2, co, x % 2, y, z)

    return pairs(move)


TWIN_PAIRS = pairs(lambda xh, co, xl, y, z: (1 - xh, co, xl, y, z))
CORE_PAIRS = pairs(lambda xh, co, xl, y, z: (xh, 1 - co, xl, y, z))


def slab_shift(k):
    return [
        (g * 32 + s, g * 32 + (s + (k if g < 2 else -k)) % 32) for g in range(4) for s in range(32)
    ]


def permute(x, table):
    return lax.ppermute(x, BOTH, table)


def slab_of(idx, kb, ka, kl):
    b = (idx[1] + kb) & 3
    a = (idx[2] + ka) & 3
    xl = (idx[3] + kl) & 1
    core = idx[0]
    y = jnp.where(core == 0, a, b)
    z = jnp.where(core == 0, b, a)
    return xl * 16 + y * 4 + z


def pair_sum_kernel(idx, ja_ref, jb_ref, o0, o1, o2, o3, page):
    shift = pl.multiple_of(idx[0] * 8, 8)
    for kb, out in enumerate((o0, o1, o2, o3)):

        def step(t, carry):
            slab = slab_of(idx, kb, t // 2, t % 2)
            for j in range(3):
                page[...] = ja_ref[slab * 3 + j].astype(F32) + jb_ref[slab * 3 + j].astype(F32)
                out[t, j] = page[pl.ds(shift, OWN), :]
            return carry

        lax.fori_loop(0, 8, step, 0)


def pair_sum(idx, ja, jb):
    vm = pl.BlockSpec(memory_space=pltpu.VMEM)
    return pl.pallas_call(
        pair_sum_kernel,
        out_shape=[jax.ShapeDtypeStruct((8, 3, OWN, NY), F32)] * 4,
        in_specs=[pl.BlockSpec(memory_space=pltpu.SMEM), vm, vm],
        out_specs=[vm] * 4,
        scratch_shapes=[pltpu.VMEM((WIN, NY), F32)],
        compiler_params=pltpu.CompilerParams(vmem_limit_bytes=24 << 20),
        cost_estimate=pl.CostEstimate(flops=10**6, bytes_accessed=6 * 10**6, transcendentals=0),
        name="pair_sum",
    )(idx, ja, jb)


TOP = 16
MOVING_CHUNK = 4
FACTOR_CHUNK = 2
MOVING_PAGES = NZ + 2 * MOVING_CHUNK
FACTOR_PAGES = NZ + 6
FIRST_ORDER = 1.0 / 27.0


def split(product):
    high = product.astype(BF16)
    low = (product - high.astype(F32)).astype(BF16)
    return jnp.concatenate([high, low], axis=1)


def bands():
    rows = lax.broadcasted_iota(jnp.int32, (2 * NY, NY), 0)
    cols = lax.broadcasted_iota(jnp.int32, (2 * NY, NY), 1)
    away = jnp.abs((rows & (NY - 1)) - cols)
    band2 = jnp.where(away <= RADIUS, 1.0, 0.0).astype(BF16)
    return band2[:NY], band2


def dot(lhs, rhs):
    return jnp.dot(lhs, rhs, preferred_element_type=F32)


def load(ref, base, chunk):
    return ref[pl.ds(base, chunk)].reshape(chunk * WIN, NY)


def triple_sums(makers, scales, shift, even, odd, three, ring, begin, emit, end):
    band1, band2 = bands()
    volumes, chunk = three.shape[:2]
    slots = ring.shape[1]
    even[...] = jnp.zeros(even.shape, F32)
    odd[...] = jnp.zeros(odd.shape, F32)
    ring[...] = jnp.zeros(ring.shape, F32)

    def along_y(thunk, v, line):
        sums = thunk(band1, band2)
        for j in range(chunk):
            line[v, j, pl.ds(TOP, WIN), :] = sums[j * WIN : (j + 1) * WIN]

    def along_x(v, line, base):
        for j in range(chunk):
            three[v, j] = (
                line[v, j, pl.ds(TOP - 9 + shift, 64), :]
                + line[v, j, pl.ds(TOP - 8 + shift, 64), :]
                + line[v, j, pl.ds(TOP - 7 + shift, 64), :]
            )
        for j in range(chunk):
            ring[v, (base + j) & (slots - 1)] = (
                three[v, j, pl.ds(5, OWN), :]
                + three[v, j, pl.ds(8, OWN), :]
                + three[v, j, pl.ds(11, OWN), :]
            )

    def both(i, line, other):
        thunks = makers(i * chunk)
        for v in range(volumes):
            along_y(thunks[v], v, line)
            along_x(v, other, (i - 1) * chunk)

    def along_z(n):
        begin(n)
        for v in range(volumes):
            for q in range(2 * chunk):
                z = 2 * chunk * n - chunk - 1 + q
                page = (
                    ring[v, (z - 1) & (slots - 1)]
                    + ring[v, z & (slots - 1)]
                    + ring[v, (z + 1) & (slots - 1)]
                )
                emit(v, n, q, page * scales[v] if scales[v] is not None else page)
        end(n)

    def step(n, carry):
        both(2 * n, even, odd)
        both(2 * n + 1, odd, even)
        along_z(n)
        return carry

    steps = NZ // (2 * chunk)
    lax.fori_loop(0, steps, step, 0)
    for v in range(volumes):
        along_x(v, odd, NZ - chunk)
        for j in range(chunk):
            ring[v, (NZ + j) & (slots - 1)] = jnp.zeros((OWN, NY), F32)
    along_z(jnp.int32(steps))


def moving_kernel(idx, ja_ref, jb_ref, out_ref, even, odd, three, ring, ready, sem):
    shift = pl.multiple_of(idx[0] * 8, 8)
    length = 2 * MOVING_CHUNK

    def makers(base):
        out = []
        for ref in (ja_ref, jb_ref):

            def square(b1, b2, ref=ref):
                f = load(ref, base, MOVING_CHUNK).astype(F32)
                return dot(split(f * f), b2)

            out.append(lambda b1, b2, ref=ref: dot(load(ref, base, MOVING_CHUNK), b1))
            out.append(square)
        return out

    def copy(n):
        slot = n & 1
        return pltpu.make_async_copy(
            ready.at[slot], out_ref.at[:, pl.ds(n * length, length)], sem.at[slot]
        )

    def begin(n):
        @pl.when(n >= 2)
        def _():
            copy(n - 2).wait()

    def emit(v, n, q, page):
        ready[n & 1, v, q] = page

    triple_sums(
        makers, (FIRST_ORDER, None) * 2, shift, even, odd, three, ring,
        begin, emit, lambda n: copy(n).start(),
    )
    last = jnp.int32(NZ // length)
    copy(last - 1).wait()
    copy(last).wait()


def moving_planes(idx, ja, jb):
    vm = pl.BlockSpec(memory_space=pltpu.VMEM)
    return pl.pallas_call(
        moving_kernel,
        out_shape=jax.ShapeDtypeStruct((4, MOVING_PAGES, OWN, NY), F32),
        in_specs=[pl.BlockSpec(memory_space=pltpu.SMEM), vm, vm],
        out_specs=pl.BlockSpec(memory_space=pltpu.HBM),
        scratch_shapes=[
            pltpu.VMEM((4, MOVING_CHUNK, 88, NY), F32),
            pltpu.VMEM((4, MOVING_CHUNK, 88, NY), F32),
            pltpu.VMEM((4, MOVING_CHUNK, 64, NY), F32),
            pltpu.VMEM((4, 4 * MOVING_CHUNK, OWN, NY), F32),
            pltpu.VMEM((2, 4, 2 * MOVING_CHUNK, OWN, NY), F32),
            pltpu.SemaphoreType.DMA((2,)),
        ],
        compiler_params=pltpu.CompilerParams(vmem_limit_bytes=24 << 20),
        cost_estimate=pl.CostEstimate(flops=4 * 10**9, bytes_accessed=13 * 10**6, transcendentals=0),
        name="moving_planes",
    )(idx, ja, jb)


def factor_kernel(
    idx, i_ref, ja_ref, jb_ref, jplane_ref, o0, o1, o2, o3, cc_ref, iext_ref,
    raw, even, odd, three, ring, iplane, jplane, sem,
):
    shift = pl.multiple_of(idx[0] * 8, 8)
    fetch = pltpu.make_async_copy(jplane_ref, jplane, sem)
    fetch.start()
    for v in range(4):
        for z in (NZ + 1, NZ + 2):
            iplane[v, z + 3] = jnp.zeros((OWN, NY), F32)

    def makers(base):
        def wide(n, keep):
            f = load((i_ref, ja_ref, jb_ref)[n], base, FACTOR_CHUNK).astype(F32)
            if keep:
                raw[n, pl.ds(base, FACTOR_CHUNK)] = f.reshape(FACTOR_CHUNK, WIN, NY)
            return f

        def square(b1, b2):
            f = wide(0, True)
            return dot(split(f * f), b2)

        return [
            lambda b1, b2: dot(load(i_ref, base, FACTOR_CHUNK), b1),
            square,
            lambda b1, b2: dot(split(wide(0, False) * wide(1, True)), b2),
            lambda b1, b2: dot(split(wide(0, False) * wide(2, True)), b2),
        ]

    def emit(v, n, q, page):
        iplane[v, 2 * FACTOR_CHUNK * n + q] = page

    nothing = lambda n: None
    triple_sums(
        makers, (FIRST_ORDER, None, None, None), shift, even, odd, three, ring,
        nothing, emit, nothing,
    )
    fetch.wait()

    eps_b = EPSILON * COUNT
    eps_bc = EPSILON * COUNT**2

    def block(out, kb, t, cc):
        slab = slab_of(idx, kb, t // 2, t % 2)
        first = slab * 3
        for r in range(OWN // 8):
            part = pl.ds(r * 8, 8)

            def boxes(ref, v, at):
                pages = [ref[v, first + at + p, part, :] for p in range(9)]
                return [pages[j] + pages[j + 3] + pages[j + 6] for j in range(3)]

            own = pl.ds(shift + r * 8, 8)
            si, sii = boxes(iplane, 0, 0), boxes(iplane, 1, 0)
            var_i = [sii[j] - si[j] * si[j] for j in range(3)]
            slope = [
                (raw[0, first + j, own, :] - si[j] * FIRST_ORDER) / (var_i[j] + eps_b)
                for j in range(3)
            ]
            total = [None] * 3
            for n in range(2):
                sj, sjj = boxes(jplane, 2 * n, 2), boxes(jplane, 2 * n + 1, 2)
                sij = boxes(iplane, 2 + n, 0)
                for j in range(3):
                    var_j = sjj[j] - sj[j] * sj[j]
                    cross = sij[j] - si[j] * sj[j]
                    gain = cross / (var_i[j] * var_j + eps_bc)
                    cc = cc + cross * gain
                    moved = raw[1 + n, first + j, own, :] - sj[j] * FIRST_ORDER - cross * slope[j]
                    term = gain * moved
                    total[j] = term if n == 0 else total[j] + term
            for j in range(3):
                out[t, j, part, :] = total[j]
        return cc

    cc = jnp.zeros((8, NY), F32)
    for kb, out in enumerate((o0, o1, o2, o3)):
        cc = lax.fori_loop(0, 8, lambda t, cc, out=out, kb=kb: block(out, kb, t, cc), cc)
    cc_ref[...] = cc

    start = idx[4] * 3 - 6
    for j in range(15):
        z = start + j
        inside = jnp.logical_and(z >= 0, z < NZ)
        page = raw[0, jnp.clip(z, 0, NZ - 1), pl.ds(shift, OWN), :]
        iext_ref[j] = jnp.where(inside, page, 0.0)


def factors(idx, image, ja, jb, jplane):
    vm = pl.BlockSpec(memory_space=pltpu.VMEM)
    block = jax.ShapeDtypeStruct((8, 3, OWN, NY), F32)
    return pl.pallas_call(
        factor_kernel,
        out_shape=[block] * 4
        + [jax.ShapeDtypeStruct((8, NY), F32), jax.ShapeDtypeStruct((15, OWN, NY), F32)],
        in_specs=[pl.BlockSpec(memory_space=pltpu.SMEM), vm, vm, vm]
        + [pl.BlockSpec(memory_space=pltpu.HBM)],
        out_specs=[vm] * 6,
        scratch_shapes=[
            pltpu.VMEM((3, NZ, WIN, NY), F32),
            pltpu.VMEM((4, FACTOR_CHUNK, 88, NY), F32),
            pltpu.VMEM((4, FACTOR_CHUNK, 88, NY), F32),
            pltpu.VMEM((4, FACTOR_CHUNK, 64, NY), F32),
            pltpu.VMEM((4, 4 * FACTOR_CHUNK, OWN, NY), F32),
            pltpu.VMEM((4, FACTOR_PAGES, OWN, NY), F32),
            pltpu.VMEM((4, MOVING_PAGES, OWN, NY), F32),
            pltpu.SemaphoreType.DMA,
        ],
        compiler_params=pltpu.CompilerParams(vmem_limit_bytes=44 << 20),
        cost_estimate=pl.CostEstimate(flops=4 * 10**9, bytes_accessed=18 * 10**6, transcendentals=0),
        name="factors",
    )(idx, image, ja, jb, jplane)


CC_ROWS = 8
SIDE = 6 * OWN
CENTRE = 6 * OWN + CC_ROWS


def smooth_kernel(
    idx, own_ref, twin_ref, other_ref, iown_ref, iother_ref, u_ref, adv_ref, m_ref, st_ref,
    ext, mext, image, prod,
):
    core, sub, xh = idx[0], idx[4], idx[5]
    mine = pl.multiple_of(core * OWN, 8)
    others = pl.multiple_of((1 - core) * OWN, 8)

    def centre(rows, ref):
        for j in range(3):
            ext[5 + j, rows, :] = ref[pl.ds(j * OWN, OWN), :]
            mext[1 + j, rows, :] = ref[pl.ds((3 + j) * OWN, OWN), :]

    def sides(rows, low, high):
        for d, (ref, at) in enumerate((low, high)):
            for j in range(5):
                z = sub * 3 + (j - 5 if d == 0 else j + 3)
                inside = jnp.logical_and(z >= 0, z < NZ)
                page = ref[pl.ds(at + j * OWN, OWN), :]
                ext[j if d == 0 else 8 + j, rows, :] = jnp.where(inside, page, 0.0)
            z = sub * 3 + (-1 if d == 0 else 3)
            inside = jnp.logical_and(z >= 0, z < NZ)
            page = ref[pl.ds(at + 5 * OWN, OWN), :]
            mext[0 if d == 0 else 4, rows, :] = jnp.where(inside, page, 0.0)

    my_rows, other_rows = pl.ds(mine, OWN), pl.ds(others, OWN)
    centre(my_rows, own_ref)
    centre(other_rows, other_ref)

    @pl.when(xh == 0)
    def _():
        sides(my_rows, (own_ref, CENTRE), (twin_ref, 0))
        sides(other_rows, (other_ref, CENTRE), (other_ref, CENTRE + SIDE))

    @pl.when(xh == 1)
    def _():
        sides(my_rows, (twin_ref, 0), (own_ref, CENTRE))
        sides(other_rows, (other_ref, CENTRE + SIDE), (other_ref, CENTRE))

    for p in range(15):
        image[p, my_rows, :] = iown_ref[p]
        image[p, other_rows, :] = iother_ref[p].astype(F32)

    weights = [math.exp(-o * o / (2.0 * VARIANCE)) for o in range(-REACH, REACH + 1)]
    norm = sum(weights)
    weights = [w / norm for w in weights]

    def matrix(n):
        r = lax.broadcasted_iota(jnp.int32, (n, n), 0)
        c = lax.broadcasted_iota(jnp.int32, (n, n), 1)
        d = (r - c).astype(F32)
        return jnp.where(jnp.abs(r - c) <= REACH, jnp.exp(-d * d / (2.0 * VARIANCE)) / norm, 0.0)

    def halves(x):
        high = x.astype(BF16)
        return high, (x - high.astype(F32)).astype(BF16)

    high, low = halves(matrix(NX))
    gx3 = jnp.concatenate([high, high, low], axis=1)
    high, low = halves(matrix(NY))
    gy3 = jnp.concatenate([high, high, low], axis=0)
    row = lax.broadcasted_iota(jnp.int32, (NX, NY), 0)
    lane = lax.broadcasted_iota(jnp.int32, (NX, NY), 1)

    def twice_slopes(here):
        below = jnp.where(row == NX - 1, 0.0, pltpu.roll(here, NX - 1, 0))
        above = jnp.where(row == 0, 0.0, pltpu.roll(here, 1, 0))
        right = jnp.where(lane == NY - 1, 0.0, pltpu.roll(here, NY - 1, 1))
        left = jnp.where(lane == 0, 0.0, pltpu.roll(here, 1, 1))
        return below - above, right - left

    for p in range(13):
        f = ext[p] * COUNT
        sx, sy = twice_slopes(image[p + 1])
        prod[0, p] = f * (image[p + 2] - image[p])
        prod[1, p] = f * sx
        prod[2, p] = f * sy
    square = jnp.zeros((NX, NY), F32)
    image_square = jnp.zeros((NX, NY), F32)
    mean = 1.0 / DEVICES
    for j in range(3):
        m = mext[1 + j] * mean
        sx, sy = twice_slopes(m)
        slopes = ((mext[2 + j] - mext[j]) * mean, sx, sy)
        image_square = image_square + m * m
        moved = None
        for d in range(3):
            acc = prod[d, j] * weights[0]
            for o in range(1, 11):
                acc = acc + prod[d, j + o] * weights[o]
            acc = dot(jnp.concatenate([*halves(acc), halves(acc)[0]], axis=1), gy3)
            high, low = halves(acc)
            acc = dot(gx3, jnp.concatenate([high, low, high], axis=0))
            u = acc * mean
            u_ref[j, d] = u
            square = square + u * u
            term = u * slopes[d]
            moved = term if d == 0 else moved + term
        adv_ref[j] = moved * 0.5
        m_ref[j] = m
    tail = pl.ds(6 * OWN, CC_ROWS)
    cc = jnp.sum(own_ref[tail, :] + other_ref[tail, :])
    one = lax.broadcasted_iota(jnp.int32, (1, NY), 1)
    st_ref[...] = jnp.where(
        one == 0, jnp.sum(square), jnp.where(one == 1, jnp.sum(image_square), cc)
    )


def smooth_slab(idx, own, twin, other, iown, iother):
    vm = pl.BlockSpec(memory_space=pltpu.VMEM)
    return pl.pallas_call(
        smooth_kernel,
        out_shape=[
            jax.ShapeDtypeStruct((3, 3, NX, NY), F32),
            jax.ShapeDtypeStruct((3, NX, NY), F32),
            jax.ShapeDtypeStruct((3, NX, NY), F32),
            jax.ShapeDtypeStruct((1, NY), F32),
        ],
        in_specs=[pl.BlockSpec(memory_space=pltpu.SMEM), vm, vm, vm, vm, vm],
        out_specs=[vm] * 4,
        scratch_shapes=[
            pltpu.VMEM((13, NX, NY), F32),
            pltpu.VMEM((5, NX, NY), F32),
            pltpu.VMEM((15, NX, NY), F32),
            pltpu.VMEM((3, 13, NX, NY), F32),
        ],
        compiler_params=pltpu.CompilerParams(vmem_limit_bytes=24 << 20),
        cost_estimate=pl.CostEstimate(flops=10**8, bytes_accessed=3 * 10**6, transcendentals=0),
        name="smooth_slab",
    )(idx, own, twin, other, iown, iother)


def finish_kernel(rows_ref, u_ref, adv_ref, m_ref, v_ref, t_ref, sim_ref):
    totals = jnp.sum(rows_ref[...], axis=0, keepdims=True)
    cells = NZ * NX * NY
    velocity_scale = STEP_LENGTH / jnp.sqrt(totals[:, 0:1] / cells + EPSILON)
    image_scale = 1.0 / jnp.sqrt(totals[:, 1:2] / cells + EPSILON)
    sim_ref[...] = totals[:, 2:3] * (0.5 / (DEVICES * cells))
    for j in range(3):
        for d in range(3):
            v_ref[j, d] = u_ref[j, d] * velocity_scale
        t_ref[j] = (m_ref[j] - adv_ref[j] * velocity_scale) * image_scale


def finish(rows, u, advected, m):
    vm = pl.BlockSpec(memory_space=pltpu.VMEM)
    return pl.pallas_call(
        finish_kernel,
        out_shape=[
            jax.ShapeDtypeStruct((3, 3, NX, NY), F32),
            jax.ShapeDtypeStruct((3, NX, NY), F32),
            jax.ShapeDtypeStruct((1, 1), F32),
        ],
        in_specs=[vm] * 4,
        out_specs=[vm] * 3,
        compiler_params=pltpu.CompilerParams(vmem_limit_bytes=12 << 20),
        name="finish",
    )(rows, u, advected, m)


def after(value, *others):
    return lax.optimization_barrier((value, *others))[0]


def round_one(blocks):
    return [permute(blocks[k], first_round(k)) for k in (1, 2, 3)]


def round_two(total):
    parts = [total[2 * k : 2 * k + 2] for k in range(4)]
    got = [permute(parts[k], second_round(k)) for k in (1, 2, 3)]
    return parts[0] + got[0] + got[1] + got[2]


def step(template, subjects):
    grp = lax.axis_index("grp")
    sub = lax.axis_index("sub")
    core = grp % 2
    xl, y, z = sub // 16, (sub // 4) % 4, sub % 4
    first = jnp.where(core == 0, z, y)
    second = jnp.where(core == 0, y, z)
    idx = jnp.stack([core, first, second, xl, sub, grp // 2]).astype(jnp.int32)

    mine = lax.dynamic_slice_in_dim(template, 40 * core, WIN, axis=1)
    copies = jnp.broadcast_to(mine[None], (32, 3, WIN, NY))
    copies, moving = lax.optimization_barrier((copies, subjects))
    image = lax.all_to_all(copies, "sub", 0, 0, tiled=True).reshape(NZ, WIN, NY)

    moving = moving[0]
    give = lax.dynamic_slice_in_dim(moving, 40 * (1 - core), WIN, axis=1)
    keep = lax.dynamic_slice_in_dim(moving, 40 * core, WIN, axis=1)
    take = permute(give, CORE_PAIRS)

    j_blocks = pair_sum(idx, keep, take)
    jplane = moving_planes(after(idx, *j_blocks), keep, take)
    j_got = round_one(j_blocks)
    *f_blocks, cc, i_half = factors(idx, image, keep, take, jplane)
    f_got = round_one(f_blocks)
    j_own = after(j_blocks[0], cc)
    j_total = j_own + j_got[0] + j_got[1] + j_got[2]
    i_other = permute(i_half.astype(BF16), CORE_PAIRS)
    f_total = f_blocks[0] + f_got[0] + f_got[1] + f_got[2]
    part = round_two(jnp.concatenate([f_total, j_total], axis=1))
    both = jnp.concatenate(
        [part.reshape(2, 6 * OWN, NY), jnp.broadcast_to(cc[None], (2, CC_ROWS, NY))], axis=1
    )
    half = both[0] + permute(both[0], third_round(2))
    half = half + permute(both[1], third_round(1)) + permute(both[1], third_round(3))

    f_half = half[: 3 * OWN]
    m_half = half[3 * OWN : 6 * OWN]
    low = grp < 2
    near = jnp.concatenate(
        [f_half, jnp.where(low, m_half[2 * OWN :], m_half[:OWN])], axis=0
    )
    far = jnp.where(low, f_half[OWN:], f_half[: 2 * OWN])
    near = permute(near, slab_shift(1))
    far = permute(far, slab_shift(2))
    near_f, near_m = near[: 3 * OWN], near[3 * OWN :]
    f_side = jnp.where(
        low, jnp.concatenate([far, near_f], axis=0), jnp.concatenate([near_f, far], axis=0)
    )
    side = jnp.concatenate([f_side, near_m], axis=0)
    twin = permute(side, TWIN_PAIRS)
    own = jnp.concatenate([half, side], axis=0)
    other = permute(jnp.concatenate([own, twin], axis=0), CORE_PAIRS)
    u, advected, m, stats = smooth_slab(idx, own, twin, other, i_half, i_other)
    rows = lax.all_to_all(jnp.broadcast_to(stats[None], (32, 1, NY)), "sub", 0, 0, tiled=True)
    velocity, new_template, similarity = finish(rows.reshape(32, NY), u, advected, m)
    return velocity, new_template, similarity.reshape(())


def solution(mesh):
    return jax.shard_map(
        step,
        mesh=mesh,
        in_specs=(P("sub", None, None), P(("grp", "sub"), None, None, None)),
        out_specs=(P("sub", None, None, None), P("sub", None, None), P()),
        check_vma=False,
    )
```

```python
import math

import jax
import jax.numpy as jnp
from jax import lax
from jax.experimental import pallas as pl
from jax.experimental.pallas import tpu as pltpu
from jax.sharding import PartitionSpec as P


RADIUS = 4
REACH = 5
EPSILON = 1e-05
STEP_LENGTH = 0.5
VARIANCE = 3.0
F32 = jnp.float32
BF16 = jnp.bfloat16

NZ, NX, NY = 96, 96, 128
WIN = 56
OWN = 48
COUNT = 729.0
BOTH = ("grp", "sub")
DEVICES = 128


def place(xh, co, xl, y, z):
    return (xh * 2 + co) * 32 + xl * 16 + y * 4 + z


def pairs(move):
    out = []
    for xh in range(2):
        for co in range(2):
            for xl in range(2):
                for y in range(4):
                    for z in range(4):
                        target = move(xh, co, xl, y, z)
                        if target is not None:
                            out.append((place(xh, co, xl, y, z), place(*target)))
    return out


def first_round(k):
    return pairs(
        lambda xh, co, xl, y, z: (xh, co, xl, y, (z + k) % 4) if co == 0 else (xh, co, xl, (y + k) % 4, z)
    )


def second_round(k):
    return pairs(
        lambda xh, co, xl, y, z: (xh, co, xl, (y + k) % 4, z) if co == 0 else (xh, co, xl, y, (z + k) % 4)
    )


def third_round(k):
    def move(xh, co, xl, y, z):
        x = (xh * 2 + xl + k) % 4
        return (x // 2, co, x % 2, y, z)

    return pairs(move)


TWIN_PAIRS = pairs(lambda xh, co, xl, y, z: (1 - xh, co, xl, y, z))
CORE_PAIRS = pairs(lambda xh, co, xl, y, z: (xh, 1 - co, xl, y, z))


def slab_shift(k):
    return [
        (g * 32 + s, g * 32 + (s + (k if g < 2 else -k)) % 32) for g in range(4) for s in range(32)
    ]


def permute(x, table):
    return lax.ppermute(x, BOTH, table)


def slab_of(idx, kb, ka, kl):
    b = (idx[1] + kb) & 3
    a = (idx[2] + ka) & 3
    xl = (idx[3] + kl) & 1
    core = idx[0]
    y = jnp.where(core == 0, a, b)
    z = jnp.where(core == 0, b, a)
    return xl * 16 + y * 4 + z


TOP = 16
MOVING_CHUNK = 4
FACTOR_CHUNK = 2
MOVING_PAGES = NZ + 2 * MOVING_CHUNK
FACTOR_PAGES = NZ + 6
FIRST_ORDER = 1.0 / 27.0


def split(product):
    high = product.astype(BF16)
    low = (product - high.astype(F32)).astype(BF16)
    return jnp.concatenate([high, low], axis=1)


def bands():
    rows = lax.broadcasted_iota(jnp.int32, (2 * NY, NY), 0)
    cols = lax.broadcasted_iota(jnp.int32, (2 * NY, NY), 1)
    away = jnp.abs((rows & (NY - 1)) - cols)
    band2 = jnp.where(away <= RADIUS, 1.0, 0.0).astype(BF16)
    return band2[:NY], band2


def dot(lhs, rhs):
    return jnp.dot(lhs, rhs, preferred_element_type=F32)


def load(ref, base, chunk):
    return ref[pl.ds(base, chunk)].reshape(chunk * WIN, NY)


def triple_sums(makers, scales, shift, even, odd, three, ring, enter, begin, emit, end):
    band1, band2 = bands()
    volumes, chunk = three.shape[:2]
    slots = ring.shape[1]
    even[...] = jnp.zeros(even.shape, F32)
    odd[...] = jnp.zeros(odd.shape, F32)
    ring[...] = jnp.zeros(ring.shape, F32)

    def along_y(thunk, v, line):
        sums = thunk(band1, band2)
        for j in range(chunk):
            line[v, j, pl.ds(TOP, WIN), :] = sums[j * WIN : (j + 1) * WIN]

    def along_x(v, line, base):
        for j in range(chunk):
            three[v, j] = (
                line[v, j, pl.ds(TOP - 9 + shift, 64), :]
                + line[v, j, pl.ds(TOP - 8 + shift, 64), :]
                + line[v, j, pl.ds(TOP - 7 + shift, 64), :]
            )
        for j in range(chunk):
            ring[v, (base + j) & (slots - 1)] = (
                three[v, j, pl.ds(5, OWN), :]
                + three[v, j, pl.ds(8, OWN), :]
                + three[v, j, pl.ds(11, OWN), :]
            )

    def both(i, line, other):
        thunks = makers(i * chunk)
        for v in range(volumes):
            along_y(thunks[v], v, line)
            along_x(v, other, (i - 1) * chunk)

    def along_z(n):
        begin(n)
        for v in range(volumes):
            for q in range(2 * chunk):
                z = 2 * chunk * n - chunk - 1 + q
                page = (
                    ring[v, (z - 1) & (slots - 1)]
                    + ring[v, z & (slots - 1)]
                    + ring[v, (z + 1) & (slots - 1)]
                )
                emit(v, n, q, page * scales[v] if scales[v] is not None else page)
        end(n)

    def step(n, carry):
        enter(n)
        both(2 * n, even, odd)
        both(2 * n + 1, odd, even)
        along_z(n)
        return carry

    steps = NZ // (2 * chunk)
    lax.fori_loop(0, steps, step, 0)
    for v in range(volumes):
        along_x(v, odd, NZ - chunk)
        for j in range(chunk):
            ring[v, (NZ + j) & (slots - 1)] = jnp.zeros((OWN, NY), F32)
    along_z(jnp.int32(steps))


PARTS = 4
PART = NZ // PARTS


def window_fetches(core, pairs_of_refs, sems):
    rows = pl.ds(pl.multiple_of(core * (NX - WIN), 8), WIN)
    return [
        [
            pltpu.make_async_copy(
                ref.at[pl.ds(p * PART, PART), rows], held.at[pl.ds(p * PART, PART)], sems.at[i, p]
            )
            for i, (ref, held) in enumerate(pairs_of_refs)
        ]
        for p in range(PARTS)
    ]


def wait_part(fetches, n, steps):
    for p in range(PARTS):

        @pl.when(n == p * (steps // PARTS))
        def _():
            for fetch in fetches[p]:
                fetch.wait()


def in_hbm(x):
    return pltpu.with_memory_space_constraint(x, pltpu.HBM)


def moving_kernel(
    idx, ja_hbm, jb_hbm, out_ref, o0, o1, o2, o3,
    ja_ref, jb_ref, pair, even, odd, three, ring, ready, sem, in_sem, pair_sem,
):
    shift = pl.multiple_of(idx[0] * 8, 8)
    length = 2 * MOVING_CHUNK
    steps = NZ // length
    fetches = window_fetches(idx[0], ((ja_hbm, ja_ref), (jb_hbm, jb_ref)), in_sem)
    for part in fetches:
        for fetch in part:
            fetch.start()

    def makers(base):
        def square(ref, b2):
            f = load(ref, base, MOVING_CHUNK).astype(F32)
            return dot(split(f * f), b2)

        def first(b1, b2):
            fa = load(ja_ref, base, MOVING_CHUNK).astype(F32)
            fb = load(jb_ref, base, MOVING_CHUNK).astype(F32)
            pair[pl.ds(base, MOVING_CHUNK)] = (fa + fb).reshape(MOVING_CHUNK, WIN, NY)
            return dot(load(ja_ref, base, MOVING_CHUNK), b1)

        return [
            first,
            lambda b1, b2: square(ja_ref, b2),
            lambda b1, b2: dot(load(jb_ref, base, MOVING_CHUNK), b1),
            lambda b1, b2: square(jb_ref, b2),
        ]

    def copy(n):
        slot = n & 1
        return pltpu.make_async_copy(
            ready.at[slot], out_ref.at[:, pl.ds(n * length, length)], sem.at[slot]
        )

    def begin(n):
        @pl.when(n >= 2)
        def _():
            copy(n - 2).wait()

    def emit(v, n, q, page):
        ready[n & 1, v, q] = page

    triple_sums(
        makers, (FIRST_ORDER, None) * 2, shift, even, odd, three, ring,
        lambda n: wait_part(fetches, n, steps), begin, emit, lambda n: copy(n).start(),
    )
    outs = []
    for kb, out in enumerate((o0, o1, o2, o3)):
        for t in range(8):
            slab = slab_of(idx, kb, t // 2, t % 2)
            outs.append(
                pltpu.make_async_copy(
                    pair.at[pl.ds(slab * 3, 3), pl.ds(shift, OWN)], out.at[t], pair_sem.at[kb * 8 + t]
                )
            )
    for out in outs:
        out.start()
    last = jnp.int32(steps)
    copy(last - 1).wait()
    copy(last).wait()
    for out in outs:
        out.wait()


def moving_planes(idx, ja, jb):
    hbm = pl.BlockSpec(memory_space=pltpu.HBM)
    return pl.pallas_call(
        moving_kernel,
        out_shape=[pltpu.HBM((4, MOVING_PAGES, OWN, NY), F32)]
        + [pltpu.HBM((8, 3, OWN, NY), F32)] * 4,
        in_specs=[pl.BlockSpec(memory_space=pltpu.SMEM), hbm, hbm],
        out_specs=[hbm] * 5,
        scratch_shapes=[
            pltpu.VMEM((NZ, WIN, NY), BF16),
            pltpu.VMEM((NZ, WIN, NY), BF16),
            pltpu.VMEM((NZ, WIN, NY), F32),
            pltpu.VMEM((4, MOVING_CHUNK, 88, NY), F32),
            pltpu.VMEM((4, MOVING_CHUNK, 88, NY), F32),
            pltpu.VMEM((4, MOVING_CHUNK, 64, NY), F32),
            pltpu.VMEM((4, 4 * MOVING_CHUNK, OWN, NY), F32),
            pltpu.VMEM((2, 4, 2 * MOVING_CHUNK, OWN, NY), F32),
            pltpu.SemaphoreType.DMA((2,)),
            pltpu.SemaphoreType.DMA((2, PARTS)),
            pltpu.SemaphoreType.DMA((32,)),
        ],
        compiler_params=pltpu.CompilerParams(vmem_limit_bytes=28 << 20),
        cost_estimate=pl.CostEstimate(flops=4 * 10**9, bytes_accessed=17 * 10**6, transcendentals=0),
        name="moving_planes",
    )(idx, in_hbm(ja), in_hbm(jb))


def factor_kernel(
    idx, i_hbm, ja_hbm, jb_hbm, jplane_ref, o0, o1, o2, o3, cc_ref, iext_ref,
    i_ref, ja_ref, jb_ref, raw, even, odd, three, ring, iplane, jplane, sem, in_sem, i_sem,
):
    shift = pl.multiple_of(idx[0] * 8, 8)
    fetches = window_fetches(idx[0], ((ja_hbm, ja_ref), (jb_hbm, jb_ref)), in_sem)
    for p in range(PARTS):
        part = pl.ds(p * PART, PART)
        fetches[p].append(pltpu.make_async_copy(i_hbm.at[part], i_ref.at[part], i_sem.at[p]))
        for fetch in fetches[p]:
            fetch.start()
    fetch = pltpu.make_async_copy(jplane_ref, jplane, sem)
    fetch.start()
    for v in range(4):
        for z in (NZ + 1, NZ + 2):
            iplane[v, z + 3] = jnp.zeros((OWN, NY), F32)

    def makers(base):
        def wide(n, keep):
            f = load((i_ref, ja_ref, jb_ref)[n], base, FACTOR_CHUNK).astype(F32)
            if keep:
                raw[n, pl.ds(base, FACTOR_CHUNK)] = f.reshape(FACTOR_CHUNK, WIN, NY)
            return f

        def square(b1, b2):
            f = wide(0, True)
            return dot(split(f * f), b2)

        return [
            lambda b1, b2: dot(load(i_ref, base, FACTOR_CHUNK), b1),
            square,
            lambda b1, b2: dot(split(wide(0, False) * wide(1, True)), b2),
            lambda b1, b2: dot(split(wide(0, False) * wide(2, True)), b2),
        ]

    def emit(v, n, q, page):
        iplane[v, 2 * FACTOR_CHUNK * n + q] = page

    nothing = lambda n: None
    steps = NZ // (2 * FACTOR_CHUNK)
    triple_sums(
        makers, (FIRST_ORDER, None, None, None), shift, even, odd, three, ring,
        lambda n: wait_part(fetches, n, steps), nothing, emit, nothing,
    )
    fetch.wait()

    eps_b = EPSILON * COUNT
    eps_bc = EPSILON * COUNT**2

    def block(out, kb, t, cc):
        slab = slab_of(idx, kb, t // 2, t % 2)
        first = slab * 3
        for r in range(OWN // 8):
            part = pl.ds(r * 8, 8)

            def boxes(ref, v, at):
                pages = [ref[v, first + at + p, part, :] for p in range(9)]
                return [pages[j] + pages[j + 3] + pages[j + 6] for j in range(3)]

            own = pl.ds(shift + r * 8, 8)
            si, sii = boxes(iplane, 0, 0), boxes(iplane, 1, 0)
            var_i = [sii[j] - si[j] * si[j] for j in range(3)]
            slope = [
                (raw[0, first + j, own, :] - si[j] * FIRST_ORDER) / (var_i[j] + eps_b)
                for j in range(3)
            ]
            total = [None] * 3
            for n in range(2):
                sj, sjj = boxes(jplane, 2 * n, 2), boxes(jplane, 2 * n + 1, 2)
                sij = boxes(iplane, 2 + n, 0)
                for j in range(3):
                    var_j = sjj[j] - sj[j] * sj[j]
                    cross = sij[j] - si[j] * sj[j]
                    gain = cross / (var_i[j] * var_j + eps_bc)
                    cc = cc + cross * gain
                    moved = raw[1 + n, first + j, own, :] - sj[j] * FIRST_ORDER - cross * slope[j]
                    term = gain * moved
                    total[j] = term if n == 0 else total[j] + term
            for j in range(3):
                out[t, j, part, :] = total[j]
        return cc

    cc = jnp.zeros((8, NY), F32)
    for kb, out in enumerate((o0, o1, o2, o3)):
        cc = lax.fori_loop(0, 8, lambda t, cc, out=out, kb=kb: block(out, kb, t, cc), cc)
    cc_ref[...] = cc

    start = idx[4] * 3 - 6
    for j in range(15):
        z = start + j
        inside = jnp.logical_and(z >= 0, z < NZ)
        page = raw[0, jnp.clip(z, 0, NZ - 1), pl.ds(shift, OWN), :]
        iext_ref[j] = jnp.where(inside, page, 0.0)


def factors(idx, image, ja, jb, jplane):
    vm = pl.BlockSpec(memory_space=pltpu.VMEM)
    block = jax.ShapeDtypeStruct((8, 3, OWN, NY), F32)
    return pl.pallas_call(
        factor_kernel,
        out_shape=[block] * 4
        + [jax.ShapeDtypeStruct((8, NY), F32), jax.ShapeDtypeStruct((15, OWN, NY), F32)],
        in_specs=[pl.BlockSpec(memory_space=pltpu.SMEM)] + [pl.BlockSpec(memory_space=pltpu.HBM)] * 4,
        out_specs=[vm] * 6,
        scratch_shapes=[
            pltpu.VMEM((NZ, WIN, NY), BF16),
            pltpu.VMEM((NZ, WIN, NY), BF16),
            pltpu.VMEM((NZ, WIN, NY), BF16),
            pltpu.VMEM((3, NZ, WIN, NY), F32),
            pltpu.VMEM((4, FACTOR_CHUNK, 88, NY), F32),
            pltpu.VMEM((4, FACTOR_CHUNK, 88, NY), F32),
            pltpu.VMEM((4, FACTOR_CHUNK, 64, NY), F32),
            pltpu.VMEM((4, 4 * FACTOR_CHUNK, OWN, NY), F32),
            pltpu.VMEM((4, FACTOR_PAGES, OWN, NY), F32),
            pltpu.VMEM((4, MOVING_PAGES, OWN, NY), F32),
            pltpu.SemaphoreType.DMA,
            pltpu.SemaphoreType.DMA((2, PARTS)),
            pltpu.SemaphoreType.DMA((PARTS,)),
        ],
        compiler_params=pltpu.CompilerParams(vmem_limit_bytes=44 << 20),
        cost_estimate=pl.CostEstimate(flops=4 * 10**9, bytes_accessed=18 * 10**6, transcendentals=0),
        name="factors",
    )(idx, image, in_hbm(ja), in_hbm(jb), in_hbm(jplane))


CC_ROWS = 8
SIDE = 6 * OWN
CENTRE = 6 * OWN + CC_ROWS


def smooth_kernel(
    idx, own_ref, twin_ref, other_ref, iown_ref, iother_ref, u_ref, adv_ref, m_ref, st_ref,
    ext, mext, image, prod,
):
    core, sub, xh = idx[0], idx[4], idx[5]
    mine = pl.multiple_of(core * OWN, 8)
    others = pl.multiple_of((1 - core) * OWN, 8)

    def centre(rows, ref):
        for j in range(3):
            ext[5 + j, rows, :] = ref[pl.ds(j * OWN, OWN), :]
            mext[1 + j, rows, :] = ref[pl.ds((3 + j) * OWN, OWN), :]

    def sides(rows, low, high):
        for d, (ref, at) in enumerate((low, high)):
            for j in range(5):
                z = sub * 3 + (j - 5 if d == 0 else j + 3)
                inside = jnp.logical_and(z >= 0, z < NZ)
                page = ref[pl.ds(at + j * OWN, OWN), :]
                ext[j if d == 0 else 8 + j, rows, :] = jnp.where(inside, page, 0.0)
            z = sub * 3 + (-1 if d == 0 else 3)
            inside = jnp.logical_and(z >= 0, z < NZ)
            page = ref[pl.ds(at + 5 * OWN, OWN), :]
            mext[0 if d == 0 else 4, rows, :] = jnp.where(inside, page, 0.0)

    my_rows, other_rows = pl.ds(mine, OWN), pl.ds(others, OWN)
    centre(my_rows, own_ref)
    centre(other_rows, other_ref)

    @pl.when(xh == 0)
    def _():
        sides(my_rows, (own_ref, CENTRE), (twin_ref, 0))
        sides(other_rows, (other_ref, CENTRE), (other_ref, CENTRE + SIDE))

    @pl.when(xh == 1)
    def _():
        sides(my_rows, (twin_ref, 0), (own_ref, CENTRE))
        sides(other_rows, (other_ref, CENTRE + SIDE), (other_ref, CENTRE))

    for p in range(15):
        image[p, my_rows, :] = iown_ref[p]
        image[p, other_rows, :] = iother_ref[p].astype(F32)

    weights = [math.exp(-o * o / (2.0 * VARIANCE)) for o in range(-REACH, REACH + 1)]
    norm = sum(weights)
    weights = [w / norm for w in weights]

    def matrix(n):
        r = lax.broadcasted_iota(jnp.int32, (n, n), 0)
        c = lax.broadcasted_iota(jnp.int32, (n, n), 1)
        d = (r - c).astype(F32)
        return jnp.where(jnp.abs(r - c) <= REACH, jnp.exp(-d * d / (2.0 * VARIANCE)) / norm, 0.0)

    def halves(x):
        high = x.astype(BF16)
        return high, (x - high.astype(F32)).astype(BF16)

    high, low = halves(matrix(NX))
    gx3 = jnp.concatenate([high, high, low], axis=1)
    high, low = halves(matrix(NY))
    gy3 = jnp.concatenate([high, high, low], axis=0)
    row = lax.broadcasted_iota(jnp.int32, (NX, NY), 0)
    lane = lax.broadcasted_iota(jnp.int32, (NX, NY), 1)

    def twice_slopes(here):
        below = jnp.where(row == NX - 1, 0.0, pltpu.roll(here, NX - 1, 0))
        above = jnp.where(row == 0, 0.0, pltpu.roll(here, 1, 0))
        right = jnp.where(lane == NY - 1, 0.0, pltpu.roll(here, NY - 1, 1))
        left = jnp.where(lane == 0, 0.0, pltpu.roll(here, 1, 1))
        return below - above, right - left

    for p in range(13):
        f = ext[p] * COUNT
        sx, sy = twice_slopes(image[p + 1])
        prod[0, p] = f * (image[p + 2] - image[p])
        prod[1, p] = f * sx
        prod[2, p] = f * sy
    square = jnp.zeros((NX, NY), F32)
    image_square = jnp.zeros((NX, NY), F32)
    mean = 1.0 / DEVICES
    for j in range(3):
        m = mext[1 + j] * mean
        sx, sy = twice_slopes(m)
        slopes = ((mext[2 + j] - mext[j]) * mean, sx, sy)
        image_square = image_square + m * m
        moved = None
        for d in range(3):
            acc = prod[d, j] * weights[0]
            for o in range(1, 11):
                acc = acc + prod[d, j + o] * weights[o]
            acc = dot(jnp.concatenate([*halves(acc), halves(acc)[0]], axis=1), gy3)
            high, low = halves(acc)
            acc = dot(gx3, jnp.concatenate([high, low, high], axis=0))
            u = acc * mean
            u_ref[j, d] = u
            square = square + u * u
            term = u * slopes[d]
            moved = term if d == 0 else moved + term
        adv_ref[j] = moved * 0.5
        m_ref[j] = m
    tail = pl.ds(6 * OWN, CC_ROWS)
    cc = jnp.sum(own_ref[tail, :] + other_ref[tail, :])
    one = lax.broadcasted_iota(jnp.int32, (1, NY), 1)
    st_ref[...] = jnp.where(
        one == 0, jnp.sum(square), jnp.where(one == 1, jnp.sum(image_square), cc)
    )


def smooth_slab(idx, own, twin, other, iown, iother):
    vm = pl.BlockSpec(memory_space=pltpu.VMEM)
    return pl.pallas_call(
        smooth_kernel,
        out_shape=[
            jax.ShapeDtypeStruct((3, 3, NX, NY), F32),
            jax.ShapeDtypeStruct((3, NX, NY), F32),
            jax.ShapeDtypeStruct((3, NX, NY), F32),
            jax.ShapeDtypeStruct((1, NY), F32),
        ],
        in_specs=[pl.BlockSpec(memory_space=pltpu.SMEM), vm, vm, vm, vm, vm],
        out_specs=[vm] * 4,
        scratch_shapes=[
            pltpu.VMEM((13, NX, NY), F32),
            pltpu.VMEM((5, NX, NY), F32),
            pltpu.VMEM((15, NX, NY), F32),
            pltpu.VMEM((3, 13, NX, NY), F32),
        ],
        compiler_params=pltpu.CompilerParams(vmem_limit_bytes=24 << 20),
        cost_estimate=pl.CostEstimate(flops=10**8, bytes_accessed=3 * 10**6, transcendentals=0),
        name="smooth_slab",
    )(idx, own, twin, other, iown, iother)


def finish_kernel(rows_ref, u_ref, adv_ref, m_ref, v_ref, t_ref, sim_ref):
    totals = jnp.sum(rows_ref[...], axis=0, keepdims=True)
    cells = NZ * NX * NY
    velocity_scale = STEP_LENGTH / jnp.sqrt(totals[:, 0:1] / cells + EPSILON)
    image_scale = 1.0 / jnp.sqrt(totals[:, 1:2] / cells + EPSILON)
    sim_ref[...] = totals[:, 2:3] * (0.5 / (DEVICES * cells))
    for j in range(3):
        for d in range(3):
            v_ref[j, d] = u_ref[j, d] * velocity_scale
        t_ref[j] = (m_ref[j] - adv_ref[j] * velocity_scale) * image_scale


def finish(rows, u, advected, m):
    vm = pl.BlockSpec(memory_space=pltpu.VMEM)
    return pl.pallas_call(
        finish_kernel,
        out_shape=[
            jax.ShapeDtypeStruct((3, 3, NX, NY), F32),
            jax.ShapeDtypeStruct((3, NX, NY), F32),
            jax.ShapeDtypeStruct((1, 1), F32),
        ],
        in_specs=[vm] * 4,
        out_specs=[vm] * 3,
        compiler_params=pltpu.CompilerParams(vmem_limit_bytes=12 << 20),
        name="finish",
    )(rows, u, advected, m)


def after(value, *others):
    return lax.optimization_barrier((value, *others))[0]


def round_one(blocks):
    return [permute(blocks[k], first_round(k)) for k in (1, 2, 3)]


def round_two(total):
    parts = [total[2 * k : 2 * k + 2] for k in range(4)]
    got = [permute(parts[k], second_round(k)) for k in (1, 2, 3)]
    return parts[0] + got[0] + got[1] + got[2]


def step(template, subjects):
    grp = lax.axis_index("grp")
    sub = lax.axis_index("sub")
    core = grp % 2
    xl, y, z = sub // 16, (sub // 4) % 4, sub % 4
    first = jnp.where(core == 0, z, y)
    second = jnp.where(core == 0, y, z)
    idx = jnp.stack([core, first, second, xl, sub, grp // 2]).astype(jnp.int32)

    keep = subjects[0]
    take = permute(keep, CORE_PAIRS)
    mine = lax.dynamic_slice_in_dim(template, 40 * core, WIN, axis=1)
    copies = jnp.broadcast_to(mine[None], (32, 3, WIN, NY))
    image = lax.all_to_all(copies, "sub", 0, 0, tiled=True).reshape(NZ, WIN, NY)

    jplane, *j_blocks = moving_planes(idx, keep, take)
    j_got = round_one(j_blocks)
    *f_blocks, cc, i_half = factors(idx, image, keep, take, jplane)
    f_got = round_one(f_blocks)
    j_own = after(j_blocks[0], cc)
    j_total = j_own + j_got[0] + j_got[1] + j_got[2]
    i_other = permute(i_half.astype(BF16), CORE_PAIRS)
    f_total = f_blocks[0] + f_got[0] + f_got[1] + f_got[2]
    part = round_two(jnp.concatenate([f_total, j_total], axis=1))
    both = jnp.concatenate(
        [part.reshape(2, 6 * OWN, NY), jnp.broadcast_to(cc[None], (2, CC_ROWS, NY))], axis=1
    )
    half = both[0] + permute(both[0], third_round(2))
    half = half + permute(both[1], third_round(1)) + permute(both[1], third_round(3))

    f_half = half[: 3 * OWN]
    m_half = half[3 * OWN : 6 * OWN]
    low = grp < 2
    near = jnp.concatenate(
        [f_half, jnp.where(low, m_half[2 * OWN :], m_half[:OWN])], axis=0
    )
    far = jnp.where(low, f_half[OWN:], f_half[: 2 * OWN])
    near = permute(near, slab_shift(1))
    far = permute(far, slab_shift(2))
    near_f, near_m = near[: 3 * OWN], near[3 * OWN :]
    f_side = jnp.where(
        low, jnp.concatenate([far, near_f], axis=0), jnp.concatenate([near_f, far], axis=0)
    )
    side = jnp.concatenate([f_side, near_m], axis=0)
    twin = permute(side, TWIN_PAIRS)
    own = jnp.concatenate([half, side], axis=0)
    other = permute(jnp.concatenate([own, twin], axis=0), CORE_PAIRS)
    u, advected, m, stats = smooth_slab(idx, own, twin, other, i_half, i_other)
    rows = lax.all_to_all(jnp.broadcast_to(stats[None], (32, 1, NY)), "sub", 0, 0, tiled=True)
    velocity, new_template, similarity = finish(rows.reshape(32, NY), u, advected, m)
    return velocity, new_template, similarity.reshape(())


def solution(mesh):
    return jax.shard_map(
        step,
        mesh=mesh,
        in_specs=(P("sub", None, None), P(("grp", "sub"), None, None, None)),
        out_specs=(P("sub", None, None, None), P("sub", None, None), P()),
        check_vma=False,
    )
```

```python
import math

import jax
import jax.numpy as jnp
from jax import lax
from jax.experimental import pallas as pl
from jax.experimental.pallas import tpu as pltpu
from jax.sharding import PartitionSpec as P


RADIUS = 4
REACH = 5
EPSILON = 1e-05
STEP_LENGTH = 0.5
VARIANCE = 3.0
F32 = jnp.float32
BF16 = jnp.bfloat16

NZ, NX, NY = 96, 96, 128
WIN = 56
OWN = 48
COUNT = 729.0
BOTH = ("grp", "sub")
DEVICES = 128


def place(xh, co, xl, y, z):
    return (xh * 2 + co) * 32 + xl * 16 + y * 4 + z


def pairs(move):
    out = []
    for xh in range(2):
        for co in range(2):
            for xl in range(2):
                for y in range(4):
                    for z in range(4):
                        target = move(xh, co, xl, y, z)
                        if target is not None:
                            out.append((place(xh, co, xl, y, z), place(*target)))
    return out


def first_round(k):
    return pairs(
        lambda xh, co, xl, y, z: (xh, co, xl, y, (z + k) % 4) if co == 0 else (xh, co, xl, (y + k) % 4, z)
    )


def second_round(k):
    return pairs(
        lambda xh, co, xl, y, z: (xh, co, xl, (y + k) % 4, z) if co == 0 else (xh, co, xl, y, (z + k) % 4)
    )


def third_round(k):
    def move(xh, co, xl, y, z):
        x = (xh * 2 + xl + k) % 4
        return (x // 2, co, x % 2, y, z)

    return pairs(move)


TWIN_PAIRS = pairs(lambda xh, co, xl, y, z: (1 - xh, co, xl, y, z))
CORE_PAIRS = pairs(lambda xh, co, xl, y, z: (xh, 1 - co, xl, y, z))


def slab_shift(k):
    return [
        (g * 32 + s, g * 32 + (s + (k if g < 2 else -k)) % 32) for g in range(4) for s in range(32)
    ]


def permute(x, table):
    return lax.ppermute(x, BOTH, table)


def slab_of(idx, kb, ka, kl):
    b = (idx[1] + kb) & 3
    a = (idx[2] + ka) & 3
    xl = (idx[3] + kl) & 1
    core = idx[0]
    y = jnp.where(core == 0, a, b)
    z = jnp.where(core == 0, b, a)
    return xl * 16 + y * 4 + z


TOP = 16
CHUNK = 4
STEPS = NZ // (2 * CHUNK)
PAGES = NZ + 2 * CHUNK
FIRST_ORDER = 1.0 / 27.0


def split(product):
    high = product.astype(BF16)
    low = (product - high.astype(F32)).astype(BF16)
    return jnp.concatenate([high, low], axis=1)


def bands():
    rows = lax.broadcasted_iota(jnp.int32, (2 * NY, NY), 0)
    cols = lax.broadcasted_iota(jnp.int32, (2 * NY, NY), 1)
    away = jnp.abs((rows & (NY - 1)) - cols)
    band2 = jnp.where(away <= RADIUS, 1.0, 0.0).astype(BF16)
    return band2[:NY], band2


def dot(lhs, rhs):
    return jnp.dot(lhs, rhs, preferred_element_type=F32)


def load(ref, base, chunk):
    return ref[pl.ds(base, chunk)].reshape(chunk * WIN, NY)


def triple_sums(makers, scales, shift, even, odd, three, last, enter, emit, leave):
    band1, band2 = bands()
    volumes = len(three)
    first = [v for v in range(volumes) if scales[v] is not None]
    second = [v for v in range(volumes) if scales[v] is None]
    for v in range(volumes):
        for ref in (even[v], odd[v], last[v]):
            ref[...] = jnp.zeros(ref.shape, F32)

    def along_y(lhs, line):
        size = CHUNK * WIN
        for members, band in ((first, band1), (second, band2)):
            sums = dot(jnp.concatenate([lhs[v]() for v in members], axis=0), band)
            for m, v in enumerate(members):
                for j in range(CHUNK):
                    at = m * size + j * WIN
                    line[v][j, pl.ds(TOP, WIN), :] = sums[at : at + WIN]

    def triples(v, n, q, rows, pages):
        before, here = last[v][0, rows, :], last[v][1, rows, :]
        left, right = here + pages[0], pages[1] + pages[2]
        sums = (before + left, left + pages[1], pages[0] + right, right + pages[3])
        for j in range(CHUNK):
            emit(v, n, q + j, rows, sums[j] * scales[v] if scales[v] is not None else sums[j])
        last[v][0, rows, :] = pages[2]
        last[v][1, rows, :] = pages[3]

    def along_x(v, line, n, q):
        for j in range(CHUNK):
            three[v][j] = (
                line[v][j, pl.ds(TOP - 9 + shift, 64), :]
                + line[v][j, pl.ds(TOP - 8 + shift, 64), :]
                + line[v][j, pl.ds(TOP - 7 + shift, 64), :]
            )
        for r in range(OWN // 8):
            pages = [
                three[v][j, pl.ds(5 + 8 * r, 8), :]
                + three[v][j, pl.ds(8 + 8 * r, 8), :]
                + three[v][j, pl.ds(11 + 8 * r, 8), :]
                for j in range(CHUNK)
            ]
            triples(v, n, q, pl.ds(8 * r, 8), pages)

    def step(n, carry):
        enter(n)
        along_y(makers(2 * n * CHUNK), even)
        for v in range(volumes):
            along_x(v, odd, n, 0)
        along_y(makers((2 * n + 1) * CHUNK), odd)
        for v in range(volumes):
            along_x(v, even, n, CHUNK)
        leave(n)
        return carry

    lax.fori_loop(0, STEPS, step, 0)
    n = jnp.int32(STEPS)
    enter(n)
    zeros = jnp.zeros((8, NY), F32)
    for v in range(volumes):
        along_x(v, odd, n, 0)
        for r in range(OWN // 8):
            triples(v, n, CHUNK, pl.ds(8 * r, 8), [zeros] * CHUNK)
    leave(n)


PARTS = 4
PART = NZ // PARTS


def window_fetches(core, pairs_of_refs, sems):
    rows = pl.ds(pl.multiple_of(core * (NX - WIN), 8), WIN)
    return [
        [
            pltpu.make_async_copy(
                ref.at[pl.ds(p * PART, PART), rows], held.at[pl.ds(p * PART, PART)], sems.at[i, p]
            )
            for i, (ref, held) in enumerate(pairs_of_refs)
        ]
        for p in range(PARTS)
    ]


def wait_part(fetches, n):
    for p in range(PARTS):

        @pl.when(n == p * (STEPS // PARTS))
        def _():
            for fetch in fetches[p]:
                fetch.wait()


def in_hbm(x):
    return pltpu.with_memory_space_constraint(x, pltpu.HBM)


def moving_kernel(
    idx, ja_hbm, jb_hbm, out_ref, o0, o1, o2, o3,
    ja_ref, jb_ref, pair, even, odd, three, last, ready, sem, in_sem, pair_sem,
):
    shift = pl.multiple_of(idx[0] * 8, 8)
    length = 2 * CHUNK
    fetches = window_fetches(idx[0], ((ja_hbm, ja_ref), (jb_hbm, jb_ref)), in_sem)
    for part in fetches:
        for fetch in part:
            fetch.start()

    def makers(base):
        def square(ref):
            f = load(ref, base, CHUNK).astype(F32)
            return split(f * f)

        def add():
            fa = load(ja_ref, base, CHUNK).astype(F32)
            fb = load(jb_ref, base, CHUNK).astype(F32)
            pair[pl.ds(base, CHUNK)] = (fa + fb).reshape(CHUNK, WIN, NY)
            return load(ja_ref, base, CHUNK)

        return [
            add,
            lambda: square(ja_ref),
            lambda: load(jb_ref, base, CHUNK),
            lambda: square(jb_ref),
        ]

    def copy(n):
        slot = n & 1
        return pltpu.make_async_copy(
            ready.at[slot], out_ref.at[:, pl.ds(n * length, length)], sem.at[slot]
        )

    def enter(n):
        wait_part(fetches, n)

        @pl.when(n >= 2)
        def _():
            copy(n - 2).wait()

    def emit(v, n, q, rows, x):
        ready[n & 1, v, q, rows, :] = x

    triple_sums(
        makers, (FIRST_ORDER, None) * 2, shift, even, odd, three, last,
        enter, emit, lambda n: copy(n).start(),
    )
    outs = []
    for kb, out in enumerate((o0, o1, o2, o3)):
        for t in range(8):
            slab = slab_of(idx, kb, t // 2, t % 2)
            outs.append(
                pltpu.make_async_copy(
                    pair.at[pl.ds(slab * 3, 3), pl.ds(shift, OWN)], out.at[t], pair_sem.at[kb * 8 + t]
                )
            )
    for out in outs:
        out.start()
    copy(jnp.int32(STEPS - 1)).wait()
    copy(jnp.int32(STEPS)).wait()
    for out in outs:
        out.wait()


def moving_planes(idx, ja, jb):
    hbm = pl.BlockSpec(memory_space=pltpu.HBM)
    return pl.pallas_call(
        moving_kernel,
        out_shape=[pltpu.HBM((4, PAGES, OWN, NY), F32)]
        + [pltpu.HBM((8, 3, OWN, NY), F32)] * 4,
        in_specs=[pl.BlockSpec(memory_space=pltpu.SMEM), hbm, hbm],
        out_specs=[hbm] * 5,
        scratch_shapes=[
            pltpu.VMEM((NZ, WIN, NY), BF16),
            pltpu.VMEM((NZ, WIN, NY), BF16),
            pltpu.VMEM((NZ, WIN, NY), F32),
            [pltpu.VMEM((CHUNK, 88, NY), F32)] * 4,
            [pltpu.VMEM((CHUNK, 88, NY), F32)] * 4,
            [pltpu.VMEM((CHUNK, 64, NY), F32)] * 4,
            [pltpu.VMEM((2, OWN, NY), F32)] * 4,
            pltpu.VMEM((2, 4, 2 * CHUNK, OWN, NY), F32),
            pltpu.SemaphoreType.DMA((2,)),
            pltpu.SemaphoreType.DMA((2, PARTS)),
            pltpu.SemaphoreType.DMA((32,)),
        ],
        compiler_params=pltpu.CompilerParams(vmem_limit_bytes=28 << 20),
        cost_estimate=pl.CostEstimate(flops=4 * 10**9, bytes_accessed=17 * 10**6, transcendentals=0),
        name="moving_planes",
    )(idx, in_hbm(ja), in_hbm(jb))


def factor_kernel(
    idx, i_hbm, ja_hbm, jb_hbm, jplane_ref, o0, o1, o2, o3, cc_ref, iext_ref,
    i_ref, ja_ref, jb_ref, raw, even, odd, three, last, iplane, jplane, sem, in_sem, i_sem,
):
    shift = pl.multiple_of(idx[0] * 8, 8)
    fetches = window_fetches(idx[0], ((ja_hbm, ja_ref), (jb_hbm, jb_ref)), in_sem)
    for p in range(PARTS):
        part = pl.ds(p * PART, PART)
        fetches[p].append(pltpu.make_async_copy(i_hbm.at[part], i_ref.at[part], i_sem.at[p]))
        for fetch in fetches[p]:
            fetch.start()
    fetch = pltpu.make_async_copy(jplane_ref, jplane, sem)
    fetch.start()

    def makers(base):
        def wide(n, keep):
            f = load((i_ref, ja_ref, jb_ref)[n], base, CHUNK).astype(F32)
            if keep:
                raw[n, pl.ds(base, CHUNK)] = f.reshape(CHUNK, WIN, NY)
            return f

        def square():
            f = wide(0, True)
            return split(f * f)

        return [
            lambda: load(i_ref, base, CHUNK),
            square,
            lambda: split(wide(0, False) * wide(1, True)),
            lambda: split(wide(0, False) * wide(2, True)),
        ]

    def emit(v, n, q, rows, x):
        iplane[v, 2 * CHUNK * n + q, rows, :] = x

    triple_sums(
        makers, (FIRST_ORDER, None, None, None), shift, even, odd, three, last,
        lambda n: wait_part(fetches, n), emit, lambda n: None,
    )
    fetch.wait()

    eps_b = EPSILON * COUNT
    eps_bc = EPSILON * COUNT**2

    def block(out, kb, t, cc):
        slab = slab_of(idx, kb, t // 2, t % 2)
        first = slab * 3
        for r in range(OWN // 8):
            part = pl.ds(r * 8, 8)

            def boxes(ref, v):
                pages = [ref[v, first + 2 + p, part, :] for p in range(9)]
                return [pages[j] + pages[j + 3] + pages[j + 6] for j in range(3)]

            own = pl.ds(shift + r * 8, 8)
            si, sii = boxes(iplane, 0), boxes(iplane, 1)
            var_i = [sii[j] - si[j] * si[j] for j in range(3)]
            slope = [
                (raw[0, first + j, own, :] - si[j] * FIRST_ORDER) / (var_i[j] + eps_b)
                for j in range(3)
            ]
            total = [None] * 3
            for n in range(2):
                sj, sjj = boxes(jplane, 2 * n), boxes(jplane, 2 * n + 1)
                sij = boxes(iplane, 2 + n)
                for j in range(3):
                    var_j = sjj[j] - sj[j] * sj[j]
                    cross = sij[j] - si[j] * sj[j]
                    gain = cross / (var_i[j] * var_j + eps_bc)
                    cc = cc + cross * gain
                    moved = raw[1 + n, first + j, own, :] - sj[j] * FIRST_ORDER - cross * slope[j]
                    term = gain * moved
                    total[j] = term if n == 0 else total[j] + term
            for j in range(3):
                out[t, j, part, :] = total[j]
        return cc

    cc = jnp.zeros((8, NY), F32)
    for kb, out in enumerate((o0, o1, o2, o3)):
        cc = lax.fori_loop(0, 8, lambda t, cc, out=out, kb=kb: block(out, kb, t, cc), cc)
    cc_ref[...] = cc

    start = idx[4] * 3 - 6
    for j in range(15):
        z = start + j
        inside = jnp.logical_and(z >= 0, z < NZ)
        page = raw[0, jnp.clip(z, 0, NZ - 1), pl.ds(shift, OWN), :]
        iext_ref[j] = jnp.where(inside, page, 0.0)


def factors(idx, image, ja, jb, jplane):
    vm = pl.BlockSpec(memory_space=pltpu.VMEM)
    block = jax.ShapeDtypeStruct((8, 3, OWN, NY), F32)
    return pl.pallas_call(
        factor_kernel,
        out_shape=[block] * 4
        + [jax.ShapeDtypeStruct((8, NY), F32), jax.ShapeDtypeStruct((15, OWN, NY), F32)],
        in_specs=[pl.BlockSpec(memory_space=pltpu.SMEM)] + [pl.BlockSpec(memory_space=pltpu.HBM)] * 4,
        out_specs=[vm] * 6,
        scratch_shapes=[
            pltpu.VMEM((NZ, WIN, NY), BF16),
            pltpu.VMEM((NZ, WIN, NY), BF16),
            pltpu.VMEM((NZ, WIN, NY), BF16),
            pltpu.VMEM((3, NZ, WIN, NY), F32),
            [pltpu.VMEM((CHUNK, 88, NY), F32)] * 4,
            [pltpu.VMEM((CHUNK, 88, NY), F32)] * 4,
            [pltpu.VMEM((CHUNK, 64, NY), F32)] * 4,
            [pltpu.VMEM((2, OWN, NY), F32)] * 4,
            pltpu.VMEM((4, PAGES, OWN, NY), F32),
            pltpu.VMEM((4, PAGES, OWN, NY), F32),
            pltpu.SemaphoreType.DMA,
            pltpu.SemaphoreType.DMA((2, PARTS)),
            pltpu.SemaphoreType.DMA((PARTS,)),
        ],
        compiler_params=pltpu.CompilerParams(vmem_limit_bytes=44 << 20),
        cost_estimate=pl.CostEstimate(flops=4 * 10**9, bytes_accessed=18 * 10**6, transcendentals=0),
        name="factors",
    )(idx, image, in_hbm(ja), in_hbm(jb), in_hbm(jplane))


CC_ROWS = 8
SIDE = 6 * OWN
CENTRE = 6 * OWN + CC_ROWS


def smooth_kernel(
    idx, own_ref, twin_ref, other_ref, iown_ref, iother_ref, u_ref, adv_ref, m_ref, st_ref,
    ext, mext, image, prod,
):
    core, sub, xh = idx[0], idx[4], idx[5]
    mine = pl.multiple_of(core * OWN, 8)
    others = pl.multiple_of((1 - core) * OWN, 8)

    def centre(rows, ref):
        for j in range(3):
            ext[5 + j, rows, :] = ref[pl.ds(j * OWN, OWN), :]
            mext[1 + j, rows, :] = ref[pl.ds((3 + j) * OWN, OWN), :]

    def sides(rows, low, high):
        for d, (ref, at) in enumerate((low, high)):
            for j in range(5):
                z = sub * 3 + (j - 5 if d == 0 else j + 3)
                inside = jnp.logical_and(z >= 0, z < NZ)
                page = ref[pl.ds(at + j * OWN, OWN), :]
                ext[j if d == 0 else 8 + j, rows, :] = jnp.where(inside, page, 0.0)
            z = sub * 3 + (-1 if d == 0 else 3)
            inside = jnp.logical_and(z >= 0, z < NZ)
            page = ref[pl.ds(at + 5 * OWN, OWN), :]
            mext[0 if d == 0 else 4, rows, :] = jnp.where(inside, page, 0.0)

    my_rows, other_rows = pl.ds(mine, OWN), pl.ds(others, OWN)
    centre(my_rows, own_ref)
    centre(other_rows, other_ref)

    @pl.when(xh == 0)
    def _():
        sides(my_rows, (own_ref, CENTRE), (twin_ref, 0))
        sides(other_rows, (other_ref, CENTRE), (other_ref, CENTRE + SIDE))

    @pl.when(xh == 1)
    def _():
        sides(my_rows, (twin_ref, 0), (own_ref, CENTRE))
        sides(other_rows, (other_ref, CENTRE + SIDE), (other_ref, CENTRE))

    for p in range(15):
        image[p, my_rows, :] = iown_ref[p]
        image[p, other_rows, :] = iother_ref[p].astype(F32)

    weights = [math.exp(-o * o / (2.0 * VARIANCE)) for o in range(-REACH, REACH + 1)]
    norm = sum(weights)
    weights = [w / norm for w in weights]

    def matrix(n):
        r = lax.broadcasted_iota(jnp.int32, (n, n), 0)
        c = lax.broadcasted_iota(jnp.int32, (n, n), 1)
        d = (r - c).astype(F32)
        return jnp.where(jnp.abs(r - c) <= REACH, jnp.exp(-d * d / (2.0 * VARIANCE)) / norm, 0.0)

    def halves(x):
        high = x.astype(BF16)
        return high, (x - high.astype(F32)).astype(BF16)

    high, low = halves(matrix(NX))
    gx3 = jnp.concatenate([high, high, low], axis=1)
    high, low = halves(matrix(NY))
    gy3 = jnp.concatenate([high, high, low], axis=0)
    row = lax.broadcasted_iota(jnp.int32, (NX, NY), 0)
    lane = lax.broadcasted_iota(jnp.int32, (NX, NY), 1)

    def twice_slopes(here):
        below = jnp.where(row == NX - 1, 0.0, pltpu.roll(here, NX - 1, 0))
        above = jnp.where(row == 0, 0.0, pltpu.roll(here, 1, 0))
        right = jnp.where(lane == NY - 1, 0.0, pltpu.roll(here, NY - 1, 1))
        left = jnp.where(lane == 0, 0.0, pltpu.roll(here, 1, 1))
        return below - above, right - left

    for p in range(13):
        f = ext[p] * COUNT
        sx, sy = twice_slopes(image[p + 1])
        prod[0, p] = f * (image[p + 2] - image[p])
        prod[1, p] = f * sx
        prod[2, p] = f * sy
    square = jnp.zeros((NX, NY), F32)
    image_square = jnp.zeros((NX, NY), F32)
    mean = 1.0 / DEVICES
    for j in range(3):
        m = mext[1 + j] * mean
        sx, sy = twice_slopes(m)
        slopes = ((mext[2 + j] - mext[j]) * mean, sx, sy)
        image_square = image_square + m * m
        moved = None
        for d in range(3):
            acc = prod[d, j] * weights[0]
            for o in range(1, 11):
                acc = acc + prod[d, j + o] * weights[o]
            acc = dot(jnp.concatenate([*halves(acc), halves(acc)[0]], axis=1), gy3)
            high, low = halves(acc)
            acc = dot(gx3, jnp.concatenate([high, low, high], axis=0))
            u = acc * mean
            u_ref[j, d] = u
            square = square + u * u
            term = u * slopes[d]
            moved = term if d == 0 else moved + term
        adv_ref[j] = moved * 0.5
        m_ref[j] = m
    tail = pl.ds(6 * OWN, CC_ROWS)
    cc = jnp.sum(own_ref[tail, :] + other_ref[tail, :])
    one = lax.broadcasted_iota(jnp.int32, (1, NY), 1)
    st_ref[...] = jnp.where(
        one == 0, jnp.sum(square), jnp.where(one == 1, jnp.sum(image_square), cc)
    )


def smooth_slab(idx, own, twin, other, iown, iother):
    vm = pl.BlockSpec(memory_space=pltpu.VMEM)
    return pl.pallas_call(
        smooth_kernel,
        out_shape=[
            jax.ShapeDtypeStruct((3, 3, NX, NY), F32),
            jax.ShapeDtypeStruct((3, NX, NY), F32),
            jax.ShapeDtypeStruct((3, NX, NY), F32),
            jax.ShapeDtypeStruct((1, NY), F32),
        ],
        in_specs=[pl.BlockSpec(memory_space=pltpu.SMEM), vm, vm, vm, vm, vm],
        out_specs=[vm] * 4,
        scratch_shapes=[
            pltpu.VMEM((13, NX, NY), F32),
            pltpu.VMEM((5, NX, NY), F32),
            pltpu.VMEM((15, NX, NY), F32),
            pltpu.VMEM((3, 13, NX, NY), F32),
        ],
        compiler_params=pltpu.CompilerParams(vmem_limit_bytes=24 << 20),
        cost_estimate=pl.CostEstimate(flops=10**8, bytes_accessed=3 * 10**6, transcendentals=0),
        name="smooth_slab",
    )(idx, own, twin, other, iown, iother)


def finish_kernel(rows_ref, u_ref, adv_ref, m_ref, v_ref, t_ref, sim_ref):
    totals = jnp.sum(rows_ref[...], axis=0, keepdims=True)
    cells = NZ * NX * NY
    velocity_scale = STEP_LENGTH / jnp.sqrt(totals[:, 0:1] / cells + EPSILON)
    image_scale = 1.0 / jnp.sqrt(totals[:, 1:2] / cells + EPSILON)
    sim_ref[...] = totals[:, 2:3] * (0.5 / (DEVICES * cells))
    for j in range(3):
        for d in range(3):
            v_ref[j, d] = u_ref[j, d] * velocity_scale
        t_ref[j] = (m_ref[j] - adv_ref[j] * velocity_scale) * image_scale


def finish(rows, u, advected, m):
    vm = pl.BlockSpec(memory_space=pltpu.VMEM)
    return pl.pallas_call(
        finish_kernel,
        out_shape=[
            jax.ShapeDtypeStruct((3, 3, NX, NY), F32),
            jax.ShapeDtypeStruct((3, NX, NY), F32),
            jax.ShapeDtypeStruct((1, 1), F32),
        ],
        in_specs=[vm] * 4,
        out_specs=[vm] * 3,
        compiler_params=pltpu.CompilerParams(vmem_limit_bytes=12 << 20),
        name="finish",
    )(rows, u, advected, m)


def after(value, *others):
    return lax.optimization_barrier((value, *others))[0]


def round_one(blocks):
    return [permute(blocks[k], first_round(k)) for k in (1, 2, 3)]


def round_two(total):
    parts = [total[2 * k : 2 * k + 2] for k in range(4)]
    got = [permute(parts[k], second_round(k)) for k in (1, 2, 3)]
    return parts[0] + got[0] + got[1] + got[2]


def step(template, subjects):
    grp = lax.axis_index("grp")
    sub = lax.axis_index("sub")
    core = grp % 2
    xl, y, z = sub // 16, (sub // 4) % 4, sub % 4
    first = jnp.where(core == 0, z, y)
    second = jnp.where(core == 0, y, z)
    idx = jnp.stack([core, first, second, xl, sub, grp // 2]).astype(jnp.int32)

    keep = subjects[0]
    take = permute(keep, CORE_PAIRS)
    mine = lax.dynamic_slice_in_dim(template, 40 * core, WIN, axis=1)
    copies = jnp.broadcast_to(mine[None], (32, 3, WIN, NY))
    image = lax.all_to_all(copies, "sub", 0, 0, tiled=True).reshape(NZ, WIN, NY)

    jplane, *j_blocks = moving_planes(idx, keep, take)
    j_got = round_one(j_blocks)
    *f_blocks, cc, i_half = factors(idx, image, keep, take, jplane)
    f_got = round_one(f_blocks)
    j_own = after(j_blocks[0], cc)
    j_total = j_own + j_got[0] + j_got[1] + j_got[2]
    i_other = permute(i_half.astype(BF16), CORE_PAIRS)
    f_total = f_blocks[0] + f_got[0] + f_got[1] + f_got[2]
    part = round_two(jnp.concatenate([f_total, j_total], axis=1))
    both = jnp.concatenate(
        [part.reshape(2, 6 * OWN, NY), jnp.broadcast_to(cc[None], (2, CC_ROWS, NY))], axis=1
    )
    half = both[0] + permute(both[0], third_round(2))
    half = half + permute(both[1], third_round(1)) + permute(both[1], third_round(3))

    f_half = half[: 3 * OWN]
    m_half = half[3 * OWN : 6 * OWN]
    low = grp < 2
    near = jnp.concatenate(
        [f_half, jnp.where(low, m_half[2 * OWN :], m_half[:OWN])], axis=0
    )
    far = jnp.where(low, f_half[OWN:], f_half[: 2 * OWN])
    near = permute(near, slab_shift(1))
    far = permute(far, slab_shift(2))
    near_f, near_m = near[: 3 * OWN], near[3 * OWN :]
    f_side = jnp.where(
        low, jnp.concatenate([far, near_f], axis=0), jnp.concatenate([near_f, far], axis=0)
    )
    side = jnp.concatenate([f_side, near_m], axis=0)
    twin = permute(side, TWIN_PAIRS)
    own = jnp.concatenate([half, side], axis=0)
    other = permute(jnp.concatenate([own, twin], axis=0), CORE_PAIRS)
    u, advected, m, stats = smooth_slab(idx, own, twin, other, i_half, i_other)
    rows = lax.all_to_all(jnp.broadcast_to(stats[None], (32, 1, NY)), "sub", 0, 0, tiled=True)
    velocity, new_template, similarity = finish(rows.reshape(32, NY), u, advected, m)
    return velocity, new_template, similarity.reshape(())


def solution(mesh):
    return jax.shard_map(
        step,
        mesh=mesh,
        in_specs=(P("sub", None, None), P(("grp", "sub"), None, None, None)),
        out_specs=(P("sub", None, None, None), P("sub", None, None), P()),
        check_vma=False,
    )
```

```python
import functools
import math

import jax
import jax.numpy as jnp
from jax import lax
from jax.experimental import pallas as pl
from jax.experimental.pallas import tpu as pltpu
from jax.sharding import PartitionSpec as P


RADIUS = 4
REACH = 5
EPSILON = 1e-05
STEP_LENGTH = 0.5
VARIANCE = 3.0
F32 = jnp.float32
BF16 = jnp.bfloat16

NZ, NX, NY = 96, 96, 128
WIN = 56
OWN = 48
COUNT = 729.0
BOTH = ("grp", "sub")
DEVICES = 128


def place(xh, co, xl, y, z):
    return (xh * 2 + co) * 32 + xl * 16 + y * 4 + z


def pairs(move):
    out = []
    for xh in range(2):
        for co in range(2):
            for xl in range(2):
                for y in range(4):
                    for z in range(4):
                        target = move(xh, co, xl, y, z)
                        if target is not None:
                            out.append((place(xh, co, xl, y, z), place(*target)))
    return out


def first_round(k):
    return pairs(
        lambda xh, co, xl, y, z: (xh, co, xl, y, (z + k) % 4) if co == 0 else (xh, co, xl, (y + k) % 4, z)
    )


def second_round(k):
    return pairs(
        lambda xh, co, xl, y, z: (xh, co, xl, (y + k) % 4, z) if co == 0 else (xh, co, xl, y, (z + k) % 4)
    )


def third_round(k):
    def move(xh, co, xl, y, z):
        x = (xh * 2 + xl + k) % 4
        return (x // 2, co, x % 2, y, z)

    return pairs(move)


TWIN_PAIRS = pairs(lambda xh, co, xl, y, z: (1 - xh, co, xl, y, z))
CORE_PAIRS = pairs(lambda xh, co, xl, y, z: (xh, 1 - co, xl, y, z))


def slab_shift(k):
    return [
        (g * 32 + s, g * 32 + (s + (k if g < 2 else -k)) % 32) for g in range(4) for s in range(32)
    ]


def permute(x, table):
    return lax.ppermute(x, BOTH, table)


def slab_of(idx, kb, ka, kl):
    b = (idx[1] + kb) & 3
    a = (idx[2] + ka) & 3
    xl = (idx[3] + kl) & 1
    core = idx[0]
    y = jnp.where(core == 0, a, b)
    z = jnp.where(core == 0, b, a)
    return xl * 16 + y * 4 + z


TOP = 16
CHUNK = 4
STEPS = NZ // (2 * CHUNK)
PAGES = NZ + 2 * CHUNK
FIRST_ORDER = 1.0 / 27.0


def split(product):
    high = product.astype(BF16)
    low = (product - high.astype(F32)).astype(BF16)
    return jnp.concatenate([high, low], axis=1)


def bands():
    rows = lax.broadcasted_iota(jnp.int32, (2 * NY, NY), 0)
    cols = lax.broadcasted_iota(jnp.int32, (2 * NY, NY), 1)
    away = jnp.abs((rows & (NY - 1)) - cols)
    band2 = jnp.where(away <= RADIUS, 1.0, 0.0).astype(BF16)
    return band2[:NY], band2


def dot(lhs, rhs):
    return jnp.dot(lhs, rhs, preferred_element_type=F32)


def load(ref, base, chunk):
    return ref[pl.ds(base, chunk)].reshape(chunk * WIN, NY)


def triple_sums(makers, scales, shift, even, odd, three, last, enter, emit, leave):
    band1, band2 = bands()
    volumes = len(three)
    first = [v for v in range(volumes) if scales[v] is not None]
    second = [v for v in range(volumes) if scales[v] is None]
    for v in range(volumes):
        for ref in (even[v], odd[v], last[v]):
            ref[...] = jnp.zeros(ref.shape, F32)

    def along_y(lhs, line):
        size = CHUNK * WIN
        for members, band in ((first, band1), (second, band2)):
            sums = dot(jnp.concatenate([lhs[v]() for v in members], axis=0), band)
            for m, v in enumerate(members):
                for j in range(CHUNK):
                    at = m * size + j * WIN
                    line[v][j, pl.ds(TOP, WIN), :] = sums[at : at + WIN]

    def triples(v, n, q, rows, pages):
        before, here = last[v][0, rows, :], last[v][1, rows, :]
        left, right = here + pages[0], pages[1] + pages[2]
        sums = (before + left, left + pages[1], pages[0] + right, right + pages[3])
        for j in range(CHUNK):
            emit(v, n, q + j, rows, sums[j] * scales[v] if scales[v] is not None else sums[j])
        last[v][0, rows, :] = pages[2]
        last[v][1, rows, :] = pages[3]

    def along_x(v, line, n, q):
        for j in range(CHUNK):
            three[v][j] = (
                line[v][j, pl.ds(TOP - 9 + shift, 64), :]
                + line[v][j, pl.ds(TOP - 8 + shift, 64), :]
                + line[v][j, pl.ds(TOP - 7 + shift, 64), :]
            )
        for r in range(OWN // 8):
            pages = [
                three[v][j, pl.ds(5 + 8 * r, 8), :]
                + three[v][j, pl.ds(8 + 8 * r, 8), :]
                + three[v][j, pl.ds(11 + 8 * r, 8), :]
                for j in range(CHUNK)
            ]
            triples(v, n, q, pl.ds(8 * r, 8), pages)

    def step(n, carry):
        enter(n)
        along_y(makers(2 * n * CHUNK), even)
        for v in range(volumes):
            along_x(v, odd, n, 0)
        along_y(makers((2 * n + 1) * CHUNK), odd)
        for v in range(volumes):
            along_x(v, even, n, CHUNK)
        leave(n)
        return carry

    lax.fori_loop(0, STEPS, step, 0)
    n = jnp.int32(STEPS)
    enter(n)
    zeros = jnp.zeros((8, NY), F32)
    for v in range(volumes):
        along_x(v, odd, n, 0)
        for r in range(OWN // 8):
            triples(v, n, CHUNK, pl.ds(8 * r, 8), [zeros] * CHUNK)
    leave(n)


PARTS = 4
PART = NZ // PARTS


def window_fetches(core, pairs_of_refs, sems):
    rows = pl.ds(pl.multiple_of(core * (NX - WIN), 8), WIN)
    return [
        [
            pltpu.make_async_copy(
                ref.at[pl.ds(p * PART, PART), rows], held.at[pl.ds(p * PART, PART)], sems.at[i, p]
            )
            for i, (ref, held) in enumerate(pairs_of_refs)
        ]
        for p in range(PARTS)
    ]


def wait_part(fetches, n):
    for p in range(PARTS):

        @pl.when(n == p * (STEPS // PARTS))
        def _():
            for fetch in fetches[p]:
                fetch.wait()


def in_hbm(x):
    return pltpu.with_memory_space_constraint(x, pltpu.HBM)


def moving_kernel(
    idx, ja_hbm, jb_hbm, plane_hbm, o0, o1, o2, o3,
    ja_ref, jb_ref, pair, even, odd, three, last, ready, in_sem, pair_sem, sem,
):
    shift = pl.multiple_of(idx[0] * 8, 8)
    length = 2 * CHUNK
    fetches = window_fetches(idx[0], ((ja_hbm, ja_ref), (jb_hbm, jb_ref)), in_sem)
    for part in fetches:
        for fetch in part:
            fetch.start()

    def makers(base):
        def square(ref):
            f = load(ref, base, CHUNK).astype(F32)
            return split(f * f)

        def add():
            fa = load(ja_ref, base, CHUNK).astype(F32)
            fb = load(jb_ref, base, CHUNK).astype(F32)
            pair[pl.ds(base, CHUNK)] = (fa + fb).reshape(CHUNK, WIN, NY)
            return load(ja_ref, base, CHUNK)

        return [
            add,
            lambda: square(ja_ref),
            lambda: load(jb_ref, base, CHUNK),
            lambda: square(jb_ref),
        ]

    def copy(n):
        slot = n & (SLOTS - 1)
        return pltpu.make_async_copy(
            ready.at[slot], plane_hbm.at[:, pl.ds(n * length, length)], sem.at[slot]
        )

    outs = []
    for kb, out in enumerate((o0, o1, o2, o3)):
        for t in range(8):
            slab = slab_of(idx, kb, t // 2, t % 2)
            outs.append(
                pltpu.make_async_copy(
                    pair.at[pl.ds(slab * 3, 3), pl.ds(shift, OWN)], out.at[t], pair_sem.at[kb * 8 + t]
                )
            )

    def enter(n):
        wait_part(fetches, n)

        @pl.when(n >= SLOTS)
        def _():
            copy(n - SLOTS).wait()

        @pl.when(n == STEPS)
        def _():
            for out in outs:
                out.start()

    def emit(v, n, q, rows, x):
        ready[n & (SLOTS - 1), v, q, rows, :] = x

    triple_sums(
        makers, (FIRST_ORDER, None) * 2, shift, even, odd, three, last,
        enter, emit, lambda n: copy(n).start(),
    )
    for n in range(STEPS + 1 - SLOTS, STEPS + 1):
        copy(jnp.int32(n)).wait()
    for out in outs:
        out.wait()


SLOTS = 4
LINES = [
    [pltpu.VMEM((CHUNK, 88, NY), F32)] * 4,
    [pltpu.VMEM((CHUNK, 88, NY), F32)] * 4,
    [pltpu.VMEM((CHUNK, 64, NY), F32)] * 4,
    [pltpu.VMEM((2, OWN, NY), F32)] * 4,
]
SMALL = pl.BlockSpec(memory_space=pltpu.SMEM)
FAR = pl.BlockSpec(memory_space=pltpu.HBM)
NEAR = pl.BlockSpec(memory_space=pltpu.VMEM)
WINDOW = pltpu.VMEM((NZ, WIN, NY), BF16)
PLANES = pltpu.VMEM((4, PAGES, OWN, NY), F32)
RAW = pltpu.VMEM((3, NZ, WIN, NY), F32)


def in_vmem(x):
    return pltpu.with_memory_space_constraint(x, pltpu.VMEM)


def moving_planes(idx, ja, jb):
    return pl.pallas_call(
        moving_kernel,
        out_shape=[pltpu.HBM((4, PAGES, OWN, NY), F32)] + [pltpu.HBM((8, 3, OWN, NY), F32)] * 4,
        in_specs=[SMALL, FAR, FAR],
        out_specs=[FAR] * 5,
        scratch_shapes=[
            WINDOW,
            WINDOW,
            pltpu.VMEM((NZ, WIN, NY), F32),
            *LINES,
            pltpu.VMEM((SLOTS, 4, 2 * CHUNK, OWN, NY), F32),
            pltpu.SemaphoreType.DMA((2, PARTS)),
            pltpu.SemaphoreType.DMA((32,)),
            pltpu.SemaphoreType.DMA((SLOTS,)),
        ],
        compiler_params=pltpu.CompilerParams(vmem_limit_bytes=24 << 20),
        cost_estimate=pl.CostEstimate(flops=4 * 10**9, bytes_accessed=6 * 10**6, transcendentals=0),
        name="moving_planes",
    )(idx, in_hbm(ja), in_hbm(jb))


def template_kernel(
    idx, i_hbm, ja_hbm, jb_hbm, plane, raw, iext_ref,
    i_ref, ja_ref, jb_ref, even, odd, three, last, in_sem, i_sem,
):
    shift = pl.multiple_of(idx[0] * 8, 8)
    fetches = window_fetches(idx[0], ((ja_hbm, ja_ref), (jb_hbm, jb_ref)), in_sem)
    for p in range(PARTS):
        part = pl.ds(p * PART, PART)
        fetches[p].append(pltpu.make_async_copy(i_hbm.at[part], i_ref.at[part], i_sem.at[p]))
        for fetch in fetches[p]:
            fetch.start()

    def makers(base):
        def wide(n, keep):
            f = load((i_ref, ja_ref, jb_ref)[n], base, CHUNK).astype(F32)
            if keep:
                raw[n, pl.ds(base, CHUNK)] = f.reshape(CHUNK, WIN, NY)
            return f

        def square():
            f = wide(0, True)
            return split(f * f)

        return [
            lambda: load(i_ref, base, CHUNK),
            square,
            lambda: split(wide(0, False) * wide(1, True)),
            lambda: split(wide(0, False) * wide(2, True)),
        ]

    def emit(v, n, q, rows, x):
        plane[v, 2 * CHUNK * n + q, rows, :] = x

    triple_sums(
        makers, (FIRST_ORDER, None, None, None), shift, even, odd, three, last,
        lambda n: wait_part(fetches, n), emit, lambda n: None,
    )
    start = idx[4] * 3 - 6
    for j in range(15):
        z = start + j
        inside = jnp.logical_and(z >= 0, z < NZ)
        page = raw[0, jnp.clip(z, 0, NZ - 1), pl.ds(shift, OWN), :]
        iext_ref[j] = jnp.where(inside, page, 0.0).astype(BF16)


def template_planes(idx, image, ja, jb):
    return pl.pallas_call(
        template_kernel,
        out_shape=[PLANES, RAW, jax.ShapeDtypeStruct((15, OWN, NY), BF16)],
        in_specs=[SMALL, FAR, FAR, FAR],
        out_specs=[NEAR] * 3,
        scratch_shapes=[
            WINDOW,
            WINDOW,
            WINDOW,
            *LINES,
            pltpu.SemaphoreType.DMA((2, PARTS)),
            pltpu.SemaphoreType.DMA((PARTS,)),
        ],
        compiler_params=pltpu.CompilerParams(vmem_limit_bytes=16 << 20),
        cost_estimate=pl.CostEstimate(flops=4 * 10**9, bytes_accessed=5 * 10**6, transcendentals=0),
        name="template_planes",
    )(idx, image, in_hbm(ja), in_hbm(jb))


def factor_kernel(kb, idx, iplane, jplane, raw, out, cc_ref):
    shift = pl.multiple_of(idx[0] * 8, 8)
    eps_b = EPSILON * COUNT
    eps_bc = EPSILON * COUNT**2

    def block(t, cc):
        slab = slab_of(idx, kb, t // 2, t % 2)
        first = slab * 3
        for r in range(OWN // 8):
            part = pl.ds(r * 8, 8)

            def boxes(ref, v):
                pages = [ref[v, first + 2 + p, part, :] for p in range(9)]
                return [pages[j] + pages[j + 3] + pages[j + 6] for j in range(3)]

            own = pl.ds(shift + r * 8, 8)
            si, sii = boxes(iplane, 0), boxes(iplane, 1)
            var_i = [sii[j] - si[j] * si[j] for j in range(3)]
            slope = [
                (raw[0, first + j, own, :] - si[j] * FIRST_ORDER) / (var_i[j] + eps_b)
                for j in range(3)
            ]
            total = [None] * 3
            for n in range(2):
                sj, sjj = boxes(jplane, 2 * n), boxes(jplane, 2 * n + 1)
                sij = boxes(iplane, 2 + n)
                for j in range(3):
                    var_j = sjj[j] - sj[j] * sj[j]
                    cross = sij[j] - si[j] * sj[j]
                    gain = cross / (var_i[j] * var_j + eps_bc)
                    cc = cc + cross * gain
                    moved = raw[1 + n, first + j, own, :] - sj[j] * FIRST_ORDER - cross * slope[j]
                    term = gain * moved
                    total[j] = term if n == 0 else total[j] + term
            for j in range(3):
                out[t, j, part, :] = total[j]
        return cc

    cc_ref[...] = lax.fori_loop(0, 8, block, jnp.zeros((8, NY), F32))


def factors(kb, idx, iplane, jplane, raw):
    return pl.pallas_call(
        functools.partial(factor_kernel, kb),
        out_shape=[
            jax.ShapeDtypeStruct((8, 3, OWN, NY), F32),
            jax.ShapeDtypeStruct((8, NY), F32),
        ],
        in_specs=[SMALL, NEAR, NEAR, NEAR],
        out_specs=[NEAR] * 2,
        compiler_params=pltpu.CompilerParams(vmem_limit_bytes=4 << 20),
        cost_estimate=pl.CostEstimate(flops=4 * 10**8, bytes_accessed=10**6, transcendentals=0),
        name="factors",
    )(idx, in_vmem(iplane), in_vmem(jplane), in_vmem(raw))


CC_ROWS = 8
SIDE = 6 * OWN
CENTRE = 6 * OWN + CC_ROWS


def smooth_kernel(
    idx, own_ref, twin_ref, other_ref, iown_ref, iother_ref, u_ref, adv_ref, m_ref, st_ref,
    ext, mext, image, prod,
):
    core, sub, xh = idx[0], idx[4], idx[5]
    mine = pl.multiple_of(core * OWN, 8)
    others = pl.multiple_of((1 - core) * OWN, 8)

    def centre(rows, ref):
        for j in range(3):
            ext[5 + j, rows, :] = ref[pl.ds(j * OWN, OWN), :]
            mext[1 + j, rows, :] = ref[pl.ds((3 + j) * OWN, OWN), :]

    def sides(rows, low, high):
        for d, (ref, at) in enumerate((low, high)):
            for j in range(5):
                z = sub * 3 + (j - 5 if d == 0 else j + 3)
                inside = jnp.logical_and(z >= 0, z < NZ)
                page = ref[pl.ds(at + j * OWN, OWN), :]
                ext[j if d == 0 else 8 + j, rows, :] = jnp.where(inside, page, 0.0)
            z = sub * 3 + (-1 if d == 0 else 3)
            inside = jnp.logical_and(z >= 0, z < NZ)
            page = ref[pl.ds(at + 5 * OWN, OWN), :]
            mext[0 if d == 0 else 4, rows, :] = jnp.where(inside, page, 0.0)

    my_rows, other_rows = pl.ds(mine, OWN), pl.ds(others, OWN)
    centre(my_rows, own_ref)
    centre(other_rows, other_ref)

    @pl.when(xh == 0)
    def _():
        sides(my_rows, (own_ref, CENTRE), (twin_ref, 0))
        sides(other_rows, (other_ref, CENTRE), (other_ref, CENTRE + SIDE))

    @pl.when(xh == 1)
    def _():
        sides(my_rows, (twin_ref, 0), (own_ref, CENTRE))
        sides(other_rows, (other_ref, CENTRE + SIDE), (other_ref, CENTRE))

    for p in range(15):
        image[p, my_rows, :] = iown_ref[p].astype(F32)
        image[p, other_rows, :] = iother_ref[p].astype(F32)

    weights = [math.exp(-o * o / (2.0 * VARIANCE)) for o in range(-REACH, REACH + 1)]
    norm = sum(weights)
    weights = [w / norm for w in weights]

    def matrix(n):
        r = lax.broadcasted_iota(jnp.int32, (n, n), 0)
        c = lax.broadcasted_iota(jnp.int32, (n, n), 1)
        d = (r - c).astype(F32)
        return jnp.where(jnp.abs(r - c) <= REACH, jnp.exp(-d * d / (2.0 * VARIANCE)) / norm, 0.0)

    def halves(x):
        high = x.astype(BF16)
        return high, (x - high.astype(F32)).astype(BF16)

    high, low = halves(matrix(NX))
    gx3 = jnp.concatenate([high, high, low], axis=1)
    high, low = halves(matrix(NY))
    gy3 = jnp.concatenate([high, high, low], axis=0)
    row = lax.broadcasted_iota(jnp.int32, (NX, NY), 0)
    lane = lax.broadcasted_iota(jnp.int32, (NX, NY), 1)

    def twice_slopes(here):
        below = jnp.where(row == NX - 1, 0.0, pltpu.roll(here, NX - 1, 0))
        above = jnp.where(row == 0, 0.0, pltpu.roll(here, 1, 0))
        right = jnp.where(lane == NY - 1, 0.0, pltpu.roll(here, NY - 1, 1))
        left = jnp.where(lane == 0, 0.0, pltpu.roll(here, 1, 1))
        return below - above, right - left

    for p in range(13):
        f = ext[p] * COUNT
        sx, sy = twice_slopes(image[p + 1])
        prod[0, p] = f * (image[p + 2] - image[p])
        prod[1, p] = f * sx
        prod[2, p] = f * sy
    square = jnp.zeros((NX, NY), F32)
    image_square = jnp.zeros((NX, NY), F32)
    mean = 1.0 / DEVICES
    for j in range(3):
        m = mext[1 + j] * mean
        sx, sy = twice_slopes(m)
        slopes = ((mext[2 + j] - mext[j]) * mean, sx, sy)
        image_square = image_square + m * m
        moved = None
        for d in range(3):
            acc = prod[d, j] * weights[0]
            for o in range(1, 11):
                acc = acc + prod[d, j + o] * weights[o]
            acc = dot(jnp.concatenate([*halves(acc), halves(acc)[0]], axis=1), gy3)
            high, low = halves(acc)
            acc = dot(gx3, jnp.concatenate([high, low, high], axis=0))
            u = acc * mean
            u_ref[j, d] = u
            square = square + u * u
            term = u * slopes[d]
            moved = term if d == 0 else moved + term
        adv_ref[j] = moved * 0.5
        m_ref[j] = m
    tail = pl.ds(6 * OWN, CC_ROWS)
    cc = jnp.sum(own_ref[tail, :] + other_ref[tail, :])
    one = lax.broadcasted_iota(jnp.int32, (1, NY), 1)
    st_ref[...] = jnp.where(
        one == 0, jnp.sum(square), jnp.where(one == 1, jnp.sum(image_square), cc)
    )


def smooth_slab(idx, own, twin, other, iown, iother):
    vm = pl.BlockSpec(memory_space=pltpu.VMEM)
    return pl.pallas_call(
        smooth_kernel,
        out_shape=[
            jax.ShapeDtypeStruct((3, 3, NX, NY), F32),
            jax.ShapeDtypeStruct((3, NX, NY), F32),
            jax.ShapeDtypeStruct((3, NX, NY), F32),
            jax.ShapeDtypeStruct((1, NY), F32),
        ],
        in_specs=[pl.BlockSpec(memory_space=pltpu.SMEM), vm, vm, vm, vm, vm],
        out_specs=[vm] * 4,
        scratch_shapes=[
            pltpu.VMEM((13, NX, NY), F32),
            pltpu.VMEM((5, NX, NY), F32),
            pltpu.VMEM((15, NX, NY), F32),
            pltpu.VMEM((3, 13, NX, NY), F32),
        ],
        compiler_params=pltpu.CompilerParams(vmem_limit_bytes=24 << 20),
        cost_estimate=pl.CostEstimate(flops=10**8, bytes_accessed=3 * 10**6, transcendentals=0),
        name="smooth_slab",
    )(idx, own, twin, other, iown, iother)


def finish_kernel(rows_ref, u_ref, adv_ref, m_ref, v_ref, t_ref, sim_ref):
    totals = jnp.sum(rows_ref[...], axis=0, keepdims=True)
    cells = NZ * NX * NY
    velocity_scale = STEP_LENGTH / jnp.sqrt(totals[:, 0:1] / cells + EPSILON)
    image_scale = 1.0 / jnp.sqrt(totals[:, 1:2] / cells + EPSILON)
    sim_ref[...] = totals[:, 2:3] * (0.5 / (DEVICES * cells))
    for j in range(3):
        for d in range(3):
            v_ref[j, d] = u_ref[j, d] * velocity_scale
        t_ref[j] = (m_ref[j] - adv_ref[j] * velocity_scale) * image_scale


def finish(rows, u, advected, m):
    vm = pl.BlockSpec(memory_space=pltpu.VMEM)
    return pl.pallas_call(
        finish_kernel,
        out_shape=[
            jax.ShapeDtypeStruct((3, 3, NX, NY), F32),
            jax.ShapeDtypeStruct((3, NX, NY), F32),
            jax.ShapeDtypeStruct((1, 1), F32),
        ],
        in_specs=[vm] * 4,
        out_specs=[vm] * 3,
        compiler_params=pltpu.CompilerParams(vmem_limit_bytes=12 << 20),
        name="finish",
    )(rows, u, advected, m)


def after(value, *others):
    return lax.optimization_barrier((value, *others))[0]


def round_one(blocks):
    return [permute(blocks[k], first_round(k)) for k in (1, 2, 3)]


def round_two(total):
    parts = [total[2 * k : 2 * k + 2] for k in range(4)]
    got = [permute(parts[k], second_round(k)) for k in (1, 2, 3)]
    return parts[0] + got[0] + got[1] + got[2]


def step(template, subjects):
    grp = lax.axis_index("grp")
    sub = lax.axis_index("sub")
    core = grp % 2
    xl, y, z = sub // 16, (sub // 4) % 4, sub % 4
    first = jnp.where(core == 0, z, y)
    second = jnp.where(core == 0, y, z)
    idx = jnp.stack([core, first, second, xl, sub, grp // 2]).astype(jnp.int32)

    keep = subjects[0]
    take = permute(keep, CORE_PAIRS)
    mine = lax.dynamic_slice_in_dim(template, 40 * core, WIN, axis=1)
    copies = jnp.broadcast_to(mine[None], (32, 3, WIN, NY))
    image = lax.all_to_all(copies, "sub", 0, 0, tiled=True).reshape(NZ, WIN, NY)

    jplane, *j_blocks = moving_planes(idx, keep, take)
    j_got = round_one(j_blocks)
    iplane, raw, i_half = template_planes(idx, image, keep, take)
    f_blocks, f_got, cc = [None] * 4, [None] * 4, None
    for k in (2, 1, 3, 0):
        f_blocks[k], part = factors(k, idx, iplane, jplane, raw)
        cc = part if cc is None else cc + part
        if k:
            f_got[k] = permute(f_blocks[k], first_round(k))
    j_own = after(j_blocks[0], cc)
    j_total = j_own + j_got[0] + j_got[1] + j_got[2]
    i_other = permute(i_half, CORE_PAIRS)
    f_total = f_blocks[0] + f_got[1] + f_got[2] + f_got[3]
    part = round_two(jnp.concatenate([f_total, j_total], axis=1))
    both = jnp.concatenate(
        [part.reshape(2, 6 * OWN, NY), jnp.broadcast_to(cc[None], (2, CC_ROWS, NY))], axis=1
    )
    half = both[0] + permute(both[0], third_round(2))
    half = half + permute(both[1], third_round(1)) + permute(both[1], third_round(3))

    f_half = half[: 3 * OWN]
    m_half = half[3 * OWN : 6 * OWN]
    low = grp < 2
    near = jnp.concatenate(
        [f_half, jnp.where(low, m_half[2 * OWN :], m_half[:OWN])], axis=0
    )
    far = jnp.where(low, f_half[OWN:], f_half[: 2 * OWN])
    near = permute(near, slab_shift(1))
    far = permute(far, slab_shift(2))
    near_f, near_m = near[: 3 * OWN], near[3 * OWN :]
    f_side = jnp.where(
        low, jnp.concatenate([far, near_f], axis=0), jnp.concatenate([near_f, far], axis=0)
    )
    side = jnp.concatenate([f_side, near_m], axis=0)
    twin = permute(side, TWIN_PAIRS)
    own = jnp.concatenate([half, side], axis=0)
    other = permute(jnp.concatenate([own, twin], axis=0), CORE_PAIRS)
    u, advected, m, stats = smooth_slab(idx, own, twin, other, i_half, i_other)
    rows = lax.all_to_all(jnp.broadcast_to(stats[None], (32, 1, NY)), "sub", 0, 0, tiled=True)
    velocity, new_template, similarity = finish(rows.reshape(32, NY), u, advected, m)
    return velocity, new_template, similarity.reshape(())


def solution(mesh):
    return jax.shard_map(
        step,
        mesh=mesh,
        in_specs=(P("sub", None, None), P(("grp", "sub"), None, None, None)),
        out_specs=(P("sub", None, None, None), P("sub", None, None), P()),
        check_vma=False,
    )
```

```python
import functools
import math

import jax
import jax.numpy as jnp
from jax import lax
from jax.experimental import pallas as pl
from jax.experimental.pallas import tpu as pltpu
from jax.sharding import PartitionSpec as P


RADIUS = 4
REACH = 5
EPSILON = 1e-05
STEP_LENGTH = 0.5
VARIANCE = 3.0
F32 = jnp.float32
BF16 = jnp.bfloat16

NZ, NX, NY = 96, 96, 128
WIN = 56
OWN = 48
COUNT = 729.0
BOTH = ("grp", "sub")
DEVICES = 128


def place(xh, co, xl, y, z):
    return (xh * 2 + co) * 32 + xl * 16 + y * 4 + z


def pairs(move):
    out = []
    for xh in range(2):
        for co in range(2):
            for xl in range(2):
                for y in range(4):
                    for z in range(4):
                        target = move(xh, co, xl, y, z)
                        if target is not None:
                            out.append((place(xh, co, xl, y, z), place(*target)))
    return out


def first_round(k):
    return pairs(
        lambda xh, co, xl, y, z: (xh, co, xl, y, (z + k) % 4) if co == 0 else (xh, co, xl, (y + k) % 4, z)
    )


def second_round(k):
    return pairs(
        lambda xh, co, xl, y, z: (xh, co, xl, (y + k) % 4, z) if co == 0 else (xh, co, xl, y, (z + k) % 4)
    )


def third_round(k):
    def move(xh, co, xl, y, z):
        x = (xh * 2 + xl + k) % 4
        return (x // 2, co, x % 2, y, z)

    return pairs(move)


TWIN_PAIRS = pairs(lambda xh, co, xl, y, z: (1 - xh, co, xl, y, z))
CORE_PAIRS = pairs(lambda xh, co, xl, y, z: (xh, 1 - co, xl, y, z))


def slab_shift(k):
    return [
        (g * 32 + s, g * 32 + (s + (k if g < 2 else -k)) % 32) for g in range(4) for s in range(32)
    ]


def permute(x, table):
    return lax.ppermute(x, BOTH, table)


def slab_of(idx, kb, ka, kl):
    b = (idx[1] + kb) & 3
    a = (idx[2] + ka) & 3
    xl = (idx[3] + kl) & 1
    core = idx[0]
    y = jnp.where(core == 0, a, b)
    z = jnp.where(core == 0, b, a)
    return xl * 16 + y * 4 + z


TOP = 16
CHUNK = 4
STEPS = NZ // (2 * CHUNK)
PAGES = NZ + 2 * CHUNK
FIRST_ORDER = 1.0 / 27.0


def split(product):
    high = product.astype(BF16)
    low = (product - high.astype(F32)).astype(BF16)
    return jnp.concatenate([high, low], axis=1)


def bands():
    rows = lax.broadcasted_iota(jnp.int32, (2 * NY, NY), 0)
    cols = lax.broadcasted_iota(jnp.int32, (2 * NY, NY), 1)
    away = jnp.abs((rows & (NY - 1)) - cols)
    band2 = jnp.where(away <= RADIUS, 1.0, 0.0).astype(BF16)
    return band2[:NY], band2


def dot(lhs, rhs):
    return jnp.dot(lhs, rhs, preferred_element_type=F32)


def load(ref, base, chunk):
    return ref[pl.ds(base, chunk)].reshape(chunk * WIN, NY)


def triple_sums(makers, scales, shift, even, odd, three, last, enter, emit, leave):
    band1, band2 = bands()
    volumes = len(three)
    first = [v for v in range(volumes) if scales[v] is not None]
    second = [v for v in range(volumes) if scales[v] is None]
    for v in range(volumes):
        for ref in (even[v], odd[v], last[v]):
            ref[...] = jnp.zeros(ref.shape, F32)

    def along_y(lhs, line):
        size = CHUNK * WIN
        for members, band in ((first, band1), (second, band2)):
            sums = dot(jnp.concatenate([lhs[v]() for v in members], axis=0), band)
            for m, v in enumerate(members):
                for j in range(CHUNK):
                    at = m * size + j * WIN
                    line[v][j, pl.ds(TOP, WIN), :] = sums[at : at + WIN]

    def triples(v, n, q, rows, pages):
        before, here = last[v][0, rows, :], last[v][1, rows, :]
        left, right = here + pages[0], pages[1] + pages[2]
        sums = (before + left, left + pages[1], pages[0] + right, right + pages[3])
        for j in range(CHUNK):
            emit(v, n, q + j, rows, sums[j] * scales[v] if scales[v] is not None else sums[j])
        last[v][0, rows, :] = pages[2]
        last[v][1, rows, :] = pages[3]

    def along_x(v, line, n, q):
        for j in range(CHUNK):
            three[v][j] = (
                line[v][j, pl.ds(TOP - 9 + shift, 64), :]
                + line[v][j, pl.ds(TOP - 8 + shift, 64), :]
                + line[v][j, pl.ds(TOP - 7 + shift, 64), :]
            )
        for r in range(OWN // 8):
            pages = [
                three[v][j, pl.ds(5 + 8 * r, 8), :]
                + three[v][j, pl.ds(8 + 8 * r, 8), :]
                + three[v][j, pl.ds(11 + 8 * r, 8), :]
                for j in range(CHUNK)
            ]
            triples(v, n, q, pl.ds(8 * r, 8), pages)

    def step(n, carry):
        enter(n)
        along_y(makers(2 * n * CHUNK), even)
        for v in range(volumes):
            along_x(v, odd, n, 0)
        along_y(makers((2 * n + 1) * CHUNK), odd)
        for v in range(volumes):
            along_x(v, even, n, CHUNK)
        leave(n)
        return carry

    lax.fori_loop(0, STEPS, step, 0)
    n = jnp.int32(STEPS)
    enter(n)
    zeros = jnp.zeros((8, NY), F32)
    for v in range(volumes):
        along_x(v, odd, n, 0)
        for r in range(OWN // 8):
            triples(v, n, CHUNK, pl.ds(8 * r, 8), [zeros] * CHUNK)
    leave(n)


PARTS = 4
PART = NZ // PARTS


def window_fetches(core, pairs_of_refs, sems):
    rows = pl.ds(pl.multiple_of(core * (NX - WIN), 8), WIN)
    return [
        [
            pltpu.make_async_copy(
                ref.at[pl.ds(p * PART, PART), rows], held.at[pl.ds(p * PART, PART)], sems.at[i, p]
            )
            for i, (ref, held) in enumerate(pairs_of_refs)
        ]
        for p in range(PARTS)
    ]


def wait_part(fetches, n):
    for p in range(PARTS):

        @pl.when(n == p * (STEPS // PARTS))
        def _():
            for fetch in fetches[p]:
                fetch.wait()


def in_hbm(x):
    return pltpu.with_memory_space_constraint(x, pltpu.HBM)


def moving_kernel(
    idx, ja_hbm, jb_hbm, plane_hbm, o0, o1, o2, o3,
    ja_ref, jb_ref, pair, even, odd, three, last, ready, in_sem, pair_sem, sem,
):
    shift = pl.multiple_of(idx[0] * 8, 8)
    length = 2 * CHUNK
    fetches = window_fetches(idx[0], ((ja_hbm, ja_ref), (jb_hbm, jb_ref)), in_sem)
    for part in fetches:
        for fetch in part:
            fetch.start()

    def makers(base):
        def square(ref):
            f = load(ref, base, CHUNK).astype(F32)
            return split(f * f)

        def add():
            fa = load(ja_ref, base, CHUNK).astype(F32)
            fb = load(jb_ref, base, CHUNK).astype(F32)
            pair[pl.ds(base, CHUNK)] = (fa + fb).reshape(CHUNK, WIN, NY)
            return load(ja_ref, base, CHUNK)

        return [
            add,
            lambda: square(ja_ref),
            lambda: load(jb_ref, base, CHUNK),
            lambda: square(jb_ref),
        ]

    def copy(n):
        slot = n & (SLOTS - 1)
        return pltpu.make_async_copy(
            ready.at[slot], plane_hbm.at[:, pl.ds(n * length, length)], sem.at[slot]
        )

    outs = []
    for kb, out in enumerate((o0, o1, o2, o3)):
        for t in range(8):
            slab = slab_of(idx, kb, t // 2, t % 2)
            outs.append(
                pltpu.make_async_copy(
                    pair.at[pl.ds(slab * 3, 3), pl.ds(shift, OWN)], out.at[t], pair_sem.at[kb * 8 + t]
                )
            )

    def enter(n):
        wait_part(fetches, n)

        @pl.when(n >= SLOTS)
        def _():
            copy(n - SLOTS).wait()

        @pl.when(n == STEPS)
        def _():
            for out in outs:
                out.start()

    def emit(v, n, q, rows, x):
        ready[n & (SLOTS - 1), v, q, rows, :] = x

    triple_sums(
        makers, (FIRST_ORDER, None) * 2, shift, even, odd, three, last,
        enter, emit, lambda n: copy(n).start(),
    )
    for n in range(STEPS + 1 - SLOTS, STEPS + 1):
        copy(jnp.int32(n)).wait()
    for out in outs:
        out.wait()


SLOTS = 4
LINES = [
    [pltpu.VMEM((CHUNK, 88, NY), F32)] * 4,
    [pltpu.VMEM((CHUNK, 88, NY), F32)] * 4,
    [pltpu.VMEM((CHUNK, 64, NY), F32)] * 4,
    [pltpu.VMEM((2, OWN, NY), F32)] * 4,
]
SMALL = pl.BlockSpec(memory_space=pltpu.SMEM)
FAR = pl.BlockSpec(memory_space=pltpu.HBM)
NEAR = pl.BlockSpec(memory_space=pltpu.VMEM)
WINDOW = pltpu.VMEM((NZ, WIN, NY), BF16)
PLANES = pltpu.VMEM((4, PAGES, OWN, NY), F32)
RAW = pltpu.VMEM((3, NZ, WIN, NY), F32)


def in_vmem(x):
    return pltpu.with_memory_space_constraint(x, pltpu.VMEM)


def window_kernel(core, template, out, held, sem):
    rows = pl.ds(pl.multiple_of(core[0] * (NX - WIN), 8), WIN)
    fetch = pltpu.make_async_copy(template.at[:, rows], held, sem)
    fetch.start()
    fetch.wait()
    window = held[...]
    for d in range(32):
        out[d] = window


def window_copies(core, template):
    return pl.pallas_call(
        window_kernel,
        out_shape=pltpu.VMEM((32, 3, WIN, NY), BF16),
        in_specs=[SMALL, FAR],
        out_specs=NEAR,
        scratch_shapes=[pltpu.VMEM((3, WIN, NY), BF16), pltpu.SemaphoreType.DMA],
        compiler_params=pltpu.CompilerParams(vmem_limit_bytes=2 << 20),
        cost_estimate=pl.CostEstimate(flops=1, bytes_accessed=10**6, transcendentals=0),
        name="window_copies",
    )(core, in_hbm(template))


def moving_planes(idx, ja, jb):
    return pl.pallas_call(
        moving_kernel,
        out_shape=[pltpu.HBM((4, PAGES, OWN, NY), F32)] + [pltpu.HBM((8, 3, OWN, NY), F32)] * 4,
        in_specs=[SMALL, FAR, FAR],
        out_specs=[FAR] * 5,
        scratch_shapes=[
            WINDOW,
            WINDOW,
            pltpu.VMEM((NZ, WIN, NY), F32),
            *LINES,
            pltpu.VMEM((SLOTS, 4, 2 * CHUNK, OWN, NY), F32),
            pltpu.SemaphoreType.DMA((2, PARTS)),
            pltpu.SemaphoreType.DMA((32,)),
            pltpu.SemaphoreType.DMA((SLOTS,)),
        ],
        compiler_params=pltpu.CompilerParams(vmem_limit_bytes=24 << 20),
        cost_estimate=pl.CostEstimate(flops=4 * 10**9, bytes_accessed=6 * 10**6, transcendentals=0),
        name="moving_planes",
    )(idx, in_hbm(ja), in_hbm(jb))


def template_kernel(
    idx, i_hbm, ja_hbm, jb_hbm, plane, raw, iext_ref,
    i_ref, ja_ref, jb_ref, even, odd, three, last, in_sem, i_sem,
):
    shift = pl.multiple_of(idx[0] * 8, 8)
    fetches = window_fetches(idx[0], ((ja_hbm, ja_ref), (jb_hbm, jb_ref)), in_sem)
    for p in range(PARTS):
        part = pl.ds(p * PART, PART)
        fetches[p].append(pltpu.make_async_copy(i_hbm.at[part], i_ref.at[part], i_sem.at[p]))
        for fetch in fetches[p]:
            fetch.start()

    def makers(base):
        def wide(n, keep):
            f = load((i_ref, ja_ref, jb_ref)[n], base, CHUNK).astype(F32)
            if keep:
                raw[n, pl.ds(base, CHUNK)] = f.reshape(CHUNK, WIN, NY)
            return f

        def square():
            f = wide(0, True)
            return split(f * f)

        return [
            lambda: load(i_ref, base, CHUNK),
            square,
            lambda: split(wide(0, False) * wide(1, True)),
            lambda: split(wide(0, False) * wide(2, True)),
        ]

    def emit(v, n, q, rows, x):
        plane[v, 2 * CHUNK * n + q, rows, :] = x

    triple_sums(
        makers, (FIRST_ORDER, None, None, None), shift, even, odd, three, last,
        lambda n: wait_part(fetches, n), emit, lambda n: None,
    )
    start = idx[4] * 3 - 6
    for j in range(15):
        z = start + j
        inside = jnp.logical_and(z >= 0, z < NZ)
        page = raw[0, jnp.clip(z, 0, NZ - 1), pl.ds(shift, OWN), :]
        iext_ref[j] = jnp.where(inside, page, 0.0).astype(BF16)


def template_planes(idx, image, ja, jb):
    return pl.pallas_call(
        template_kernel,
        out_shape=[PLANES, RAW, jax.ShapeDtypeStruct((15, OWN, NY), BF16)],
        in_specs=[SMALL, FAR, FAR, FAR],
        out_specs=[NEAR] * 3,
        scratch_shapes=[
            WINDOW,
            WINDOW,
            WINDOW,
            *LINES,
            pltpu.SemaphoreType.DMA((2, PARTS)),
            pltpu.SemaphoreType.DMA((PARTS,)),
        ],
        compiler_params=pltpu.CompilerParams(vmem_limit_bytes=16 << 20),
        cost_estimate=pl.CostEstimate(flops=4 * 10**9, bytes_accessed=5 * 10**6, transcendentals=0),
        name="template_planes",
    )(idx, image, in_hbm(ja), in_hbm(jb))


def factor_kernel(kb, idx, iplane, jplane, raw, out, cc_ref):
    shift = pl.multiple_of(idx[0] * 8, 8)
    eps_b = EPSILON * COUNT
    eps_bc = EPSILON * COUNT**2

    def block(t, cc):
        slab = slab_of(idx, kb, t // 2, t % 2)
        first = slab * 3
        for r in range(OWN // 8):
            part = pl.ds(r * 8, 8)

            def boxes(ref, v):
                pages = [ref[v, first + 2 + p, part, :] for p in range(9)]
                return [pages[j] + pages[j + 3] + pages[j + 6] for j in range(3)]

            own = pl.ds(shift + r * 8, 8)
            si, sii = boxes(iplane, 0), boxes(iplane, 1)
            var_i = [sii[j] - si[j] * si[j] for j in range(3)]
            slope = [
                (raw[0, first + j, own, :] - si[j] * FIRST_ORDER) / (var_i[j] + eps_b)
                for j in range(3)
            ]
            total = [None] * 3
            for n in range(2):
                sj, sjj = boxes(jplane, 2 * n), boxes(jplane, 2 * n + 1)
                sij = boxes(iplane, 2 + n)
                for j in range(3):
                    var_j = sjj[j] - sj[j] * sj[j]
                    cross = sij[j] - si[j] * sj[j]
                    gain = cross / (var_i[j] * var_j + eps_bc)
                    cc = cc + cross * gain
                    moved = raw[1 + n, first + j, own, :] - sj[j] * FIRST_ORDER - cross * slope[j]
                    term = gain * moved
                    total[j] = term if n == 0 else total[j] + term
            for j in range(3):
                out[t, j, part, :] = total[j]
        return cc

    cc_ref[...] = lax.fori_loop(0, 8, block, jnp.zeros((8, NY), F32))


def factors(kb, idx, iplane, jplane, raw):
    return pl.pallas_call(
        functools.partial(factor_kernel, kb),
        out_shape=[
            jax.ShapeDtypeStruct((8, 3, OWN, NY), F32),
            jax.ShapeDtypeStruct((8, NY), F32),
        ],
        in_specs=[SMALL, NEAR, NEAR, NEAR],
        out_specs=[NEAR] * 2,
        compiler_params=pltpu.CompilerParams(vmem_limit_bytes=4 << 20),
        cost_estimate=pl.CostEstimate(flops=4 * 10**8, bytes_accessed=10**6, transcendentals=0),
        name="factors",
    )(idx, in_vmem(iplane), in_vmem(jplane), in_vmem(raw))


CC_ROWS = 8
SIDE = 6 * OWN
CENTRE = 6 * OWN + CC_ROWS


def twice_slopes(here):
    row = lax.broadcasted_iota(jnp.int32, (NX, NY), 0)
    lane = lax.broadcasted_iota(jnp.int32, (NX, NY), 1)
    below = jnp.where(row == NX - 1, 0.0, pltpu.roll(here, NX - 1, 0))
    above = jnp.where(row == 0, 0.0, pltpu.roll(here, 1, 0))
    right = jnp.where(lane == NY - 1, 0.0, pltpu.roll(here, NY - 1, 1))
    left = jnp.where(lane == 0, 0.0, pltpu.roll(here, 1, 1))
    return below - above, right - left


def slope_kernel(idx, iown_ref, iother_ref, slope_ref, image):
    mine = pl.multiple_of(idx[0] * OWN, 8)
    others = pl.multiple_of((1 - idx[0]) * OWN, 8)
    for p in range(15):
        image[p, pl.ds(mine, OWN), :] = iown_ref[p].astype(F32)
        image[p, pl.ds(others, OWN), :] = iother_ref[p].astype(F32)
    scale = COUNT
    for p in range(13):
        sx, sy = twice_slopes(image[p + 1])
        slope_ref[0, p] = (image[p + 2] - image[p]) * scale
        slope_ref[1, p] = sx * scale
        slope_ref[2, p] = sy * scale


def slopes(idx, iown, iother):
    return pl.pallas_call(
        slope_kernel,
        out_shape=pltpu.VMEM((3, 13, NX, NY), F32),
        in_specs=[SMALL, NEAR, NEAR],
        out_specs=NEAR,
        scratch_shapes=[pltpu.VMEM((15, NX, NY), F32)],
        compiler_params=pltpu.CompilerParams(vmem_limit_bytes=6 << 20),
        cost_estimate=pl.CostEstimate(flops=10**6, bytes_accessed=10**6, transcendentals=0),
        name="slopes",
    )(idx, iown, iother)


def smooth_kernel(
    idx, own_ref, twin_ref, other_ref, slope_ref, u_ref, adv_ref, m_ref, st_ref, ext, mext, prod,
):
    core, sub, xh = idx[0], idx[4], idx[5]
    mine = pl.multiple_of(core * OWN, 8)
    others = pl.multiple_of((1 - core) * OWN, 8)

    def centre(rows, ref):
        for j in range(3):
            ext[5 + j, rows, :] = ref[pl.ds(j * OWN, OWN), :]
            mext[1 + j, rows, :] = ref[pl.ds((3 + j) * OWN, OWN), :]

    def sides(rows, low, high):
        for d, (ref, at) in enumerate((low, high)):
            for j in range(5):
                z = sub * 3 + (j - 5 if d == 0 else j + 3)
                inside = jnp.logical_and(z >= 0, z < NZ)
                page = ref[pl.ds(at + j * OWN, OWN), :]
                ext[j if d == 0 else 8 + j, rows, :] = jnp.where(inside, page, 0.0)
            z = sub * 3 + (-1 if d == 0 else 3)
            inside = jnp.logical_and(z >= 0, z < NZ)
            page = ref[pl.ds(at + 5 * OWN, OWN), :]
            mext[0 if d == 0 else 4, rows, :] = jnp.where(inside, page, 0.0)

    my_rows, other_rows = pl.ds(mine, OWN), pl.ds(others, OWN)
    centre(my_rows, own_ref)
    centre(other_rows, other_ref)

    @pl.when(xh == 0)
    def _():
        sides(my_rows, (own_ref, CENTRE), (twin_ref, 0))
        sides(other_rows, (other_ref, CENTRE), (other_ref, CENTRE + SIDE))

    @pl.when(xh == 1)
    def _():
        sides(my_rows, (twin_ref, 0), (own_ref, CENTRE))
        sides(other_rows, (other_ref, CENTRE + SIDE), (other_ref, CENTRE))

    weights = [math.exp(-o * o / (2.0 * VARIANCE)) for o in range(-REACH, REACH + 1)]
    norm = sum(weights)
    weights = [w / norm for w in weights]

    def matrix(n):
        r = lax.broadcasted_iota(jnp.int32, (n, n), 0)
        c = lax.broadcasted_iota(jnp.int32, (n, n), 1)
        d = (r - c).astype(F32)
        return jnp.where(jnp.abs(r - c) <= REACH, jnp.exp(-d * d / (2.0 * VARIANCE)) / norm, 0.0)

    def halves(x):
        high = x.astype(BF16)
        return high, (x - high.astype(F32)).astype(BF16)

    high, low = halves(matrix(NX))
    gx3 = jnp.concatenate([high, high, low], axis=1)
    high, low = halves(matrix(NY))
    gy3 = jnp.concatenate([high, high, low], axis=0)
    for p in range(13):
        for d in range(3):
            prod[d, p] = ext[p] * slope_ref[d, p]
    square = jnp.zeros((NX, NY), F32)
    image_square = jnp.zeros((NX, NY), F32)
    mean = 1.0 / DEVICES
    for j in range(3):
        m = mext[1 + j] * mean
        sx, sy = twice_slopes(m)
        slopes = ((mext[2 + j] - mext[j]) * mean, sx, sy)
        image_square = image_square + m * m
        moved = None
        for d in range(3):
            acc = prod[d, j] * weights[0]
            for o in range(1, 11):
                acc = acc + prod[d, j + o] * weights[o]
            acc = dot(jnp.concatenate([*halves(acc), halves(acc)[0]], axis=1), gy3)
            high, low = halves(acc)
            acc = dot(gx3, jnp.concatenate([high, low, high], axis=0))
            u = acc * mean
            u_ref[j, d] = u
            square = square + u * u
            term = u * slopes[d]
            moved = term if d == 0 else moved + term
        adv_ref[j] = moved * 0.5
        m_ref[j] = m
    tail = pl.ds(6 * OWN, CC_ROWS)
    cc = jnp.sum(own_ref[tail, :] + other_ref[tail, :])
    one = lax.broadcasted_iota(jnp.int32, (1, NY), 1)
    st_ref[...] = jnp.where(
        one == 0, jnp.sum(square), jnp.where(one == 1, jnp.sum(image_square), cc)
    )


def smooth_slab(idx, own, twin, other, slope):
    vm = pl.BlockSpec(memory_space=pltpu.VMEM)
    return pl.pallas_call(
        smooth_kernel,
        out_shape=[
            jax.ShapeDtypeStruct((3, 3, NX, NY), F32),
            jax.ShapeDtypeStruct((3, NX, NY), F32),
            jax.ShapeDtypeStruct((3, NX, NY), F32),
            jax.ShapeDtypeStruct((1, NY), F32),
        ],
        in_specs=[pl.BlockSpec(memory_space=pltpu.SMEM), vm, vm, vm, vm],
        out_specs=[vm] * 4,
        scratch_shapes=[
            pltpu.VMEM((13, NX, NY), F32),
            pltpu.VMEM((5, NX, NY), F32),
            pltpu.VMEM((3, 13, NX, NY), F32),
        ],
        compiler_params=pltpu.CompilerParams(vmem_limit_bytes=24 << 20),
        cost_estimate=pl.CostEstimate(flops=10**8, bytes_accessed=3 * 10**6, transcendentals=0),
        name="smooth_slab",
    )(idx, own, twin, other, slope)


def finish_kernel(rows_ref, u_ref, adv_ref, m_ref, v_ref, t_ref, sim_ref):
    totals = jnp.sum(rows_ref[...], axis=0, keepdims=True)
    cells = NZ * NX * NY
    velocity_scale = STEP_LENGTH / jnp.sqrt(totals[:, 0:1] / cells + EPSILON)
    image_scale = 1.0 / jnp.sqrt(totals[:, 1:2] / cells + EPSILON)
    sim_ref[...] = totals[:, 2:3] * (0.5 / (DEVICES * cells))
    for j in range(3):
        for d in range(3):
            v_ref[j, d] = u_ref[j, d] * velocity_scale
        t_ref[j] = (m_ref[j] - adv_ref[j] * velocity_scale) * image_scale


def finish(rows, u, advected, m):
    vm = pl.BlockSpec(memory_space=pltpu.VMEM)
    return pl.pallas_call(
        finish_kernel,
        out_shape=[
            jax.ShapeDtypeStruct((3, 3, NX, NY), F32),
            jax.ShapeDtypeStruct((3, NX, NY), F32),
            jax.ShapeDtypeStruct((1, 1), F32),
        ],
        in_specs=[vm] * 4,
        out_specs=[vm] * 3,
        compiler_params=pltpu.CompilerParams(vmem_limit_bytes=12 << 20),
        name="finish",
    )(rows, u, advected, m)


def after(value, *others):
    return lax.optimization_barrier((value, *others))[0]


def round_one(blocks):
    return [permute(blocks[k], first_round(k)) for k in (1, 2, 3)]


def round_two(total):
    parts = [total[2 * k : 2 * k + 2] for k in range(4)]
    got = []
    for k in (2, 1, 3):
        got.append(permute(parts[k], second_round(k)))
    return parts[0] + got[0] + got[1] + got[2]


def step(template, subjects):
    grp = lax.axis_index("grp")
    sub = lax.axis_index("sub")
    core = grp % 2
    xl, y, z = sub // 16, (sub // 4) % 4, sub % 4
    first = jnp.where(core == 0, z, y)
    second = jnp.where(core == 0, y, z)
    idx = jnp.stack([core, first, second, xl, sub, grp // 2]).astype(jnp.int32)

    keep = subjects[0]
    take = permute(keep, CORE_PAIRS)
    copies = window_copies(core.astype(jnp.int32).reshape(1), template)
    image = lax.all_to_all(copies, "sub", 0, 0, tiled=True).reshape(NZ, WIN, NY)

    jplane, *j_blocks = moving_planes(idx, keep, take)
    j_got = round_one(j_blocks)
    iplane, raw, i_half = template_planes(idx, image, keep, take)
    f_blocks, f_got, cc = [None] * 4, [None] * 4, None
    for k in (2, 1, 3, 0):
        f_blocks[k], part = factors(k, idx, iplane, jplane, raw)
        cc = part if cc is None else cc + part
        if k:
            f_got[k] = permute(f_blocks[k], first_round(k))
    j_own = after(j_blocks[0], cc)
    j_total = j_own + j_got[0] + j_got[1] + j_got[2]
    i_other = permute(i_half, CORE_PAIRS)
    slope = slopes(idx, i_half, i_other)
    f_total = f_blocks[0] + f_got[1] + f_got[2] + f_got[3]
    part = round_two(jnp.concatenate([f_total, j_total], axis=1))
    both = jnp.concatenate(
        [part.reshape(2, 6 * OWN, NY), jnp.broadcast_to(cc[None], (2, CC_ROWS, NY))], axis=1
    )
    half = both[0]
    for k in (2, 1, 3):
        half = half + permute(both[k % 2], third_round(k))

    f_half = half[: 3 * OWN]
    m_half = half[3 * OWN : 6 * OWN]
    low = grp < 2
    near = jnp.concatenate(
        [f_half, jnp.where(low, m_half[2 * OWN :], m_half[:OWN])], axis=0
    )
    far = jnp.where(low, f_half[OWN:], f_half[: 2 * OWN])
    near = permute(near, slab_shift(1))
    far = permute(far, slab_shift(2))
    near_f, near_m = near[: 3 * OWN], near[3 * OWN :]
    f_side = jnp.where(
        low, jnp.concatenate([far, near_f], axis=0), jnp.concatenate([near_f, far], axis=0)
    )
    side = jnp.concatenate([f_side, near_m], axis=0)
    twin = permute(side, TWIN_PAIRS)
    own = jnp.concatenate([half, side], axis=0)
    other = permute(jnp.concatenate([own, twin], axis=0), CORE_PAIRS)
    u, advected, m, stats = smooth_slab(idx, own, twin, other, slope)
    rows = lax.all_to_all(jnp.broadcast_to(stats[None], (32, 1, NY)), "sub", 0, 0, tiled=True)
    velocity, new_template, similarity = finish(rows.reshape(32, NY), u, advected, m)
    return velocity, new_template, similarity.reshape(())


def solution(mesh):
    return jax.shard_map(
        step,
        mesh=mesh,
        in_specs=(P("sub", None, None), P(("grp", "sub"), None, None, None)),
        out_specs=(P("sub", None, None, None), P("sub", None, None), P()),
        check_vma=False,
    )
```

```python
import functools
import math

import jax
import jax.numpy as jnp
from jax import lax
from jax.experimental import pallas as pl
from jax.experimental.pallas import tpu as pltpu
from jax.sharding import PartitionSpec as P


RADIUS = 4
REACH = 5
EPSILON = 1e-05
STEP_LENGTH = 0.5
VARIANCE = 3.0
F32 = jnp.float32
BF16 = jnp.bfloat16

NZ, NX, NY = 96, 96, 128
WIN = 56
OWN = 48
COUNT = 729.0
BOTH = ("grp", "sub")
DEVICES = 128


def place(xh, co, xl, y, z):
    return (xh * 2 + co) * 32 + xl * 16 + y * 4 + z


def pairs(move):
    out = []
    for xh in range(2):
        for co in range(2):
            for xl in range(2):
                for y in range(4):
                    for z in range(4):
                        target = move(xh, co, xl, y, z)
                        if target is not None:
                            out.append((place(xh, co, xl, y, z), place(*target)))
    return out


def first_round(k):
    return pairs(
        lambda xh, co, xl, y, z: (xh, co, xl, y, (z + k) % 4) if co == 0 else (xh, co, xl, (y + k) % 4, z)
    )


def second_round(k):
    return pairs(
        lambda xh, co, xl, y, z: (xh, co, xl, (y + k) % 4, z) if co == 0 else (xh, co, xl, y, (z + k) % 4)
    )


def third_round(k):
    def move(xh, co, xl, y, z):
        x = (xh * 2 + xl + k) % 4
        return (x // 2, co, x % 2, y, z)

    return pairs(move)


TWIN_PAIRS = pairs(lambda xh, co, xl, y, z: (1 - xh, co, xl, y, z))
CORE_PAIRS = pairs(lambda xh, co, xl, y, z: (xh, 1 - co, xl, y, z))


def slab_shift(k):
    return [
        (g * 32 + s, g * 32 + (s + (k if g < 2 else -k)) % 32) for g in range(4) for s in range(32)
    ]


def permute(x, table):
    return lax.ppermute(x, BOTH, table)


def slab_of(idx, kb, ka, kl):
    b = (idx[1] + kb) & 3
    a = (idx[2] + ka) & 3
    xl = (idx[3] + kl) & 1
    core = idx[0]
    y = jnp.where(core == 0, a, b)
    z = jnp.where(core == 0, b, a)
    return xl * 16 + y * 4 + z


TOP = 16
CHUNK = 4
STEPS = NZ // (2 * CHUNK)
PAGES = NZ + 2 * CHUNK
FIRST_ORDER = 1.0 / 27.0


def split(product):
    high = product.astype(BF16)
    low = (product - high.astype(F32)).astype(BF16)
    return jnp.concatenate([high, low], axis=1)


def bands():
    rows = lax.broadcasted_iota(jnp.int32, (2 * NY, NY), 0)
    cols = lax.broadcasted_iota(jnp.int32, (2 * NY, NY), 1)
    away = jnp.abs((rows & (NY - 1)) - cols)
    band2 = jnp.where(away <= RADIUS, 1.0, 0.0).astype(BF16)
    return band2[:NY], band2


def dot(lhs, rhs):
    return jnp.dot(lhs, rhs, preferred_element_type=F32)


def load(ref, base, chunk):
    return ref[pl.ds(base, chunk)].reshape(chunk * WIN, NY)


def triple_sums(makers, scales, shift, even, odd, three, last, enter, emit, leave):
    band1, band2 = bands()
    volumes = len(three)
    first = [v for v in range(volumes) if scales[v] is not None]
    second = [v for v in range(volumes) if scales[v] is None]
    for v in range(volumes):
        for ref in (even[v], odd[v], last[v]):
            ref[...] = jnp.zeros(ref.shape, F32)

    def along_y(lhs, line):
        size = CHUNK * WIN
        for members, band in ((first, band1), (second, band2)):
            sums = dot(jnp.concatenate([lhs[v]() for v in members], axis=0), band)
            for m, v in enumerate(members):
                for j in range(CHUNK):
                    at = m * size + j * WIN
                    line[v][j, pl.ds(TOP, WIN), :] = sums[at : at + WIN]

    def triples(v, n, q, rows, pages):
        before, here = last[v][0, rows, :], last[v][1, rows, :]
        left, right = here + pages[0], pages[1] + pages[2]
        sums = (before + left, left + pages[1], pages[0] + right, right + pages[3])
        for j in range(CHUNK):
            emit(v, n, q + j, rows, sums[j] * scales[v] if scales[v] is not None else sums[j])
        last[v][0, rows, :] = pages[2]
        last[v][1, rows, :] = pages[3]

    def along_x(v, line, n, q):
        for j in range(CHUNK):
            three[v][j] = (
                line[v][j, pl.ds(TOP - 9 + shift, 64), :]
                + line[v][j, pl.ds(TOP - 8 + shift, 64), :]
                + line[v][j, pl.ds(TOP - 7 + shift, 64), :]
            )
        for r in range(OWN // 8):
            pages = [
                three[v][j, pl.ds(5 + 8 * r, 8), :]
                + three[v][j, pl.ds(8 + 8 * r, 8), :]
                + three[v][j, pl.ds(11 + 8 * r, 8), :]
                for j in range(CHUNK)
            ]
            triples(v, n, q, pl.ds(8 * r, 8), pages)

    def step(n, carry):
        enter(n)
        along_y(makers(2 * n * CHUNK), even)
        for v in range(volumes):
            along_x(v, odd, n, 0)
        along_y(makers((2 * n + 1) * CHUNK), odd)
        for v in range(volumes):
            along_x(v, even, n, CHUNK)
        leave(n)
        return carry

    lax.fori_loop(0, STEPS, step, 0)
    n = jnp.int32(STEPS)
    enter(n)
    zeros = jnp.zeros((8, NY), F32)
    for v in range(volumes):
        along_x(v, odd, n, 0)
        for r in range(OWN // 8):
            triples(v, n, CHUNK, pl.ds(8 * r, 8), [zeros] * CHUNK)
    leave(n)


PARTS = 4
PART = NZ // PARTS


def window_fetches(core, pairs_of_refs, sems):
    rows = pl.ds(pl.multiple_of(core * (NX - WIN), 8), WIN)
    return [
        [
            pltpu.make_async_copy(
                ref.at[pl.ds(p * PART, PART), rows], held.at[pl.ds(p * PART, PART)], sems.at[i, p]
            )
            for i, (ref, held) in enumerate(pairs_of_refs)
        ]
        for p in range(PARTS)
    ]


def wait_part(fetches, n):
    for p in range(PARTS):

        @pl.when(n == p * (STEPS // PARTS))
        def _():
            for fetch in fetches[p]:
                fetch.wait()


def in_hbm(x):
    return pltpu.with_memory_space_constraint(x, pltpu.HBM)


def moving_kernel(
    idx, ja_hbm, jb_hbm, plane_hbm, o0, o1, o2, o3,
    ja_ref, jb_ref, pair, even, odd, three, last, ready, in_sem, pair_sem, sem,
):
    shift = pl.multiple_of(idx[0] * 8, 8)
    length = 2 * CHUNK
    fetches = window_fetches(idx[0], ((ja_hbm, ja_ref), (jb_hbm, jb_ref)), in_sem)
    for part in fetches:
        for fetch in part:
            fetch.start()

    def makers(base):
        def square(ref):
            f = load(ref, base, CHUNK).astype(F32)
            return split(f * f)

        def add():
            fa = load(ja_ref, base, CHUNK).astype(F32)
            fb = load(jb_ref, base, CHUNK).astype(F32)
            pair[pl.ds(base, CHUNK)] = (fa + fb).reshape(CHUNK, WIN, NY)
            return load(ja_ref, base, CHUNK)

        return [
            add,
            lambda: square(ja_ref),
            lambda: load(jb_ref, base, CHUNK),
            lambda: square(jb_ref),
        ]

    def copy(n):
        slot = n & (SLOTS - 1)
        return pltpu.make_async_copy(
            ready.at[slot], plane_hbm.at[:, pl.ds(n * length, length)], sem.at[slot]
        )

    outs = []
    for kb, out in enumerate((o0, o1, o2, o3)):
        for t in range(8):
            slab = slab_of(idx, kb, t // 2, t % 2)
            outs.append(
                pltpu.make_async_copy(
                    pair.at[pl.ds(slab * 3, 3), pl.ds(shift, OWN)], out.at[t], pair_sem.at[kb * 8 + t]
                )
            )

    def enter(n):
        wait_part(fetches, n)

        @pl.when(n >= SLOTS)
        def _():
            copy(n - SLOTS).wait()

        @pl.when(n == STEPS)
        def _():
            for out in outs:
                out.start()

    def emit(v, n, q, rows, x):
        ready[n & (SLOTS - 1), v, q, rows, :] = x

    triple_sums(
        makers, (FIRST_ORDER, None) * 2, shift, even, odd, three, last,
        enter, emit, lambda n: copy(n).start(),
    )
    for n in range(STEPS + 1 - SLOTS, STEPS + 1):
        copy(jnp.int32(n)).wait()
    for out in outs:
        out.wait()


SLOTS = 4
LINES = [
    [pltpu.VMEM((CHUNK, 88, NY), F32)] * 4,
    [pltpu.VMEM((CHUNK, 88, NY), F32)] * 4,
    [pltpu.VMEM((CHUNK, 64, NY), F32)] * 4,
    [pltpu.VMEM((2, OWN, NY), F32)] * 4,
]
SMALL = pl.BlockSpec(memory_space=pltpu.SMEM)
FAR = pl.BlockSpec(memory_space=pltpu.HBM)
NEAR = pl.BlockSpec(memory_space=pltpu.VMEM)
WINDOW = pltpu.VMEM((NZ, WIN, NY), BF16)
PLANES = pltpu.VMEM((4, PAGES, OWN, NY), F32)
RAW = pltpu.VMEM((3, NZ, WIN, NY), F32)


def in_vmem(x):
    return pltpu.with_memory_space_constraint(x, pltpu.VMEM)


def moving_planes(idx, ja, jb):
    return pl.pallas_call(
        moving_kernel,
        out_shape=[pltpu.HBM((4, PAGES, OWN, NY), F32)] + [pltpu.HBM((8, 3, OWN, NY), F32)] * 4,
        in_specs=[SMALL, FAR, FAR],
        out_specs=[FAR] * 5,
        scratch_shapes=[
            WINDOW,
            WINDOW,
            pltpu.VMEM((NZ, WIN, NY), F32),
            *LINES,
            pltpu.VMEM((SLOTS, 4, 2 * CHUNK, OWN, NY), F32),
            pltpu.SemaphoreType.DMA((2, PARTS)),
            pltpu.SemaphoreType.DMA((32,)),
            pltpu.SemaphoreType.DMA((SLOTS,)),
        ],
        compiler_params=pltpu.CompilerParams(vmem_limit_bytes=24 << 20),
        cost_estimate=pl.CostEstimate(flops=4 * 10**9, bytes_accessed=6 * 10**6, transcendentals=0),
        name="moving_planes",
    )(idx, in_hbm(ja), in_hbm(jb))


def template_kernel(
    idx, i_hbm, ja_hbm, jb_hbm, plane, raw, iext_ref,
    i_ref, ja_ref, jb_ref, even, odd, three, last, in_sem, i_sem,
):
    shift = pl.multiple_of(idx[0] * 8, 8)
    fetches = window_fetches(idx[0], ((ja_hbm, ja_ref), (jb_hbm, jb_ref)), in_sem)
    for p in range(PARTS):
        part = pl.ds(p * PART, PART)
        fetches[p].append(pltpu.make_async_copy(i_hbm.at[part], i_ref.at[part], i_sem.at[p]))
        for fetch in fetches[p]:
            fetch.start()

    def makers(base):
        def wide(n, keep):
            f = load((i_ref, ja_ref, jb_ref)[n], base, CHUNK).astype(F32)
            if keep:
                raw[n, pl.ds(base, CHUNK)] = f.reshape(CHUNK, WIN, NY)
            return f

        def square():
            f = wide(0, True)
            return split(f * f)

        return [
            lambda: load(i_ref, base, CHUNK),
            square,
            lambda: split(wide(0, False) * wide(1, True)),
            lambda: split(wide(0, False) * wide(2, True)),
        ]

    def emit(v, n, q, rows, x):
        plane[v, 2 * CHUNK * n + q, rows, :] = x

    triple_sums(
        makers, (FIRST_ORDER, None, None, None), shift, even, odd, three, last,
        lambda n: wait_part(fetches, n), emit, lambda n: None,
    )
    start = idx[4] * 3 - 6
    for j in range(15):
        z = start + j
        inside = jnp.logical_and(z >= 0, z < NZ)
        page = raw[0, jnp.clip(z, 0, NZ - 1), pl.ds(shift, OWN), :]
        iext_ref[j] = jnp.where(inside, page, 0.0).astype(BF16)


def template_planes(idx, image, ja, jb):
    return pl.pallas_call(
        template_kernel,
        out_shape=[PLANES, RAW, jax.ShapeDtypeStruct((15, OWN, NY), BF16)],
        in_specs=[SMALL, FAR, FAR, FAR],
        out_specs=[NEAR] * 3,
        scratch_shapes=[
            WINDOW,
            WINDOW,
            WINDOW,
            *LINES,
            pltpu.SemaphoreType.DMA((2, PARTS)),
            pltpu.SemaphoreType.DMA((PARTS,)),
        ],
        compiler_params=pltpu.CompilerParams(vmem_limit_bytes=16 << 20),
        cost_estimate=pl.CostEstimate(flops=4 * 10**9, bytes_accessed=5 * 10**6, transcendentals=0),
        name="template_planes",
    )(idx, image, in_hbm(ja), in_hbm(jb))


def factor_kernel(kb, idx, iplane, jplane, raw, out, cc_ref):
    shift = pl.multiple_of(idx[0] * 8, 8)
    eps_b = EPSILON * COUNT
    eps_bc = EPSILON * COUNT**2

    def block(t, cc):
        slab = slab_of(idx, kb, t // 2, t % 2)
        first = slab * 3
        for r in range(OWN // 8):
            part = pl.ds(r * 8, 8)

            def boxes(ref, v):
                pages = [ref[v, first + 2 + p, part, :] for p in range(9)]
                return [pages[j] + pages[j + 3] + pages[j + 6] for j in range(3)]

            own = pl.ds(shift + r * 8, 8)
            si, sii = boxes(iplane, 0), boxes(iplane, 1)
            var_i = [sii[j] - si[j] * si[j] for j in range(3)]
            slope = [
                (raw[0, first + j, own, :] - si[j] * FIRST_ORDER) / (var_i[j] + eps_b)
                for j in range(3)
            ]
            total = [None] * 3
            for n in range(2):
                sj, sjj = boxes(jplane, 2 * n), boxes(jplane, 2 * n + 1)
                sij = boxes(iplane, 2 + n)
                for j in range(3):
                    var_j = sjj[j] - sj[j] * sj[j]
                    cross = sij[j] - si[j] * sj[j]
                    gain = cross / (var_i[j] * var_j + eps_bc)
                    cc = cc + cross * gain
                    moved = raw[1 + n, first + j, own, :] - sj[j] * FIRST_ORDER - cross * slope[j]
                    term = gain * moved
                    total[j] = term if n == 0 else total[j] + term
            for j in range(3):
                out[t, j, part, :] = total[j]
        return cc

    cc_ref[...] = lax.fori_loop(0, 8, block, jnp.zeros((8, NY), F32))


def factors(kb, idx, iplane, jplane, raw):
    return pl.pallas_call(
        functools.partial(factor_kernel, kb),
        out_shape=[
            jax.ShapeDtypeStruct((8, 3, OWN, NY), F32),
            jax.ShapeDtypeStruct((8, NY), F32),
        ],
        in_specs=[SMALL, NEAR, NEAR, NEAR],
        out_specs=[NEAR] * 2,
        compiler_params=pltpu.CompilerParams(vmem_limit_bytes=4 << 20),
        cost_estimate=pl.CostEstimate(flops=4 * 10**8, bytes_accessed=10**6, transcendentals=0),
        name="factors",
    )(idx, in_vmem(iplane), in_vmem(jplane), in_vmem(raw))


CC_ROWS = 8
SIDE = 6 * OWN
CENTRE = 6 * OWN + CC_ROWS


def twice_slopes(here):
    row = lax.broadcasted_iota(jnp.int32, (NX, NY), 0)
    lane = lax.broadcasted_iota(jnp.int32, (NX, NY), 1)
    below = jnp.where(row == NX - 1, 0.0, pltpu.roll(here, NX - 1, 0))
    above = jnp.where(row == 0, 0.0, pltpu.roll(here, 1, 0))
    right = jnp.where(lane == NY - 1, 0.0, pltpu.roll(here, NY - 1, 1))
    left = jnp.where(lane == 0, 0.0, pltpu.roll(here, 1, 1))
    return below - above, right - left


def slope_kernel(idx, iown_ref, iother_ref, slope_ref, image):
    mine = pl.multiple_of(idx[0] * OWN, 8)
    others = pl.multiple_of((1 - idx[0]) * OWN, 8)
    for p in range(15):
        image[p, pl.ds(mine, OWN), :] = iown_ref[p].astype(F32)
        image[p, pl.ds(others, OWN), :] = iother_ref[p].astype(F32)
    scale = COUNT
    for p in range(13):
        sx, sy = twice_slopes(image[p + 1])
        slope_ref[0, p] = (image[p + 2] - image[p]) * scale
        slope_ref[1, p] = sx * scale
        slope_ref[2, p] = sy * scale


def slopes(idx, iown, iother):
    return pl.pallas_call(
        slope_kernel,
        out_shape=pltpu.VMEM((3, 13, NX, NY), F32),
        in_specs=[SMALL, NEAR, NEAR],
        out_specs=NEAR,
        scratch_shapes=[pltpu.VMEM((15, NX, NY), F32)],
        compiler_params=pltpu.CompilerParams(vmem_limit_bytes=6 << 20),
        cost_estimate=pl.CostEstimate(flops=10**6, bytes_accessed=10**6, transcendentals=0),
        name="slopes",
    )(idx, iown, iother)


def smooth_kernel(
    idx, own_ref, twin_ref, other_ref, slope_ref, u_ref, adv_ref, m_ref, st_ref, ext, mext, prod,
):
    core, sub, xh = idx[0], idx[4], idx[5]
    mine = pl.multiple_of(core * OWN, 8)
    others = pl.multiple_of((1 - core) * OWN, 8)

    def centre(rows, ref):
        for j in range(3):
            ext[5 + j, rows, :] = ref[pl.ds(j * OWN, OWN), :]
            mext[1 + j, rows, :] = ref[pl.ds((3 + j) * OWN, OWN), :]

    def sides(rows, low, high):
        for d, (ref, at) in enumerate((low, high)):
            for j in range(5):
                z = sub * 3 + (j - 5 if d == 0 else j + 3)
                inside = jnp.logical_and(z >= 0, z < NZ)
                page = ref[pl.ds(at + j * OWN, OWN), :]
                ext[j if d == 0 else 8 + j, rows, :] = jnp.where(inside, page, 0.0)
            z = sub * 3 + (-1 if d == 0 else 3)
            inside = jnp.logical_and(z >= 0, z < NZ)
            page = ref[pl.ds(at + 5 * OWN, OWN), :]
            mext[0 if d == 0 else 4, rows, :] = jnp.where(inside, page, 0.0)

    my_rows, other_rows = pl.ds(mine, OWN), pl.ds(others, OWN)
    centre(my_rows, own_ref)
    centre(other_rows, other_ref)

    @pl.when(xh == 0)
    def _():
        sides(my_rows, (own_ref, CENTRE), (twin_ref, 0))
        sides(other_rows, (other_ref, CENTRE), (other_ref, CENTRE + SIDE))

    @pl.when(xh == 1)
    def _():
        sides(my_rows, (twin_ref, 0), (own_ref, CENTRE))
        sides(other_rows, (other_ref, CENTRE + SIDE), (other_ref, CENTRE))

    weights = [math.exp(-o * o / (2.0 * VARIANCE)) for o in range(-REACH, REACH + 1)]
    norm = sum(weights)
    weights = [w / norm for w in weights]

    def matrix(n):
        r = lax.broadcasted_iota(jnp.int32, (n, n), 0)
        c = lax.broadcasted_iota(jnp.int32, (n, n), 1)
        d = (r - c).astype(F32)
        return jnp.where(jnp.abs(r - c) <= REACH, jnp.exp(-d * d / (2.0 * VARIANCE)) / norm, 0.0)

    def halves(x):
        high = x.astype(BF16)
        return high, (x - high.astype(F32)).astype(BF16)

    high, low = halves(matrix(NX))
    gx3 = jnp.concatenate([high, high, low], axis=1)
    high, low = halves(matrix(NY))
    gy3 = jnp.concatenate([high, high, low], axis=0)
    for p in range(13):
        for d in range(3):
            prod[d, p] = ext[p] * slope_ref[d, p]
    square = jnp.zeros((NX, NY), F32)
    image_square = jnp.zeros((NX, NY), F32)
    mean = 1.0 / DEVICES
    for j in range(3):
        m = mext[1 + j] * mean
        sx, sy = twice_slopes(m)
        slopes = ((mext[2 + j] - mext[j]) * mean, sx, sy)
        image_square = image_square + m * m
        moved = None
        for d in range(3):
            acc = prod[d, j] * weights[0]
            for o in range(1, 11):
                acc = acc + prod[d, j + o] * weights[o]
            acc = dot(jnp.concatenate([*halves(acc), halves(acc)[0]], axis=1), gy3)
            high, low = halves(acc)
            acc = dot(gx3, jnp.concatenate([high, low, high], axis=0))
            u = acc * mean
            u_ref[j, d] = u
            square = square + u * u
            term = u * slopes[d]
            moved = term if d == 0 else moved + term
        adv_ref[j] = moved * 0.5
        m_ref[j] = m
    tail = pl.ds(6 * OWN, CC_ROWS)
    cc = jnp.sum(own_ref[tail, :] + other_ref[tail, :])
    one = lax.broadcasted_iota(jnp.int32, (1, NY), 1)
    st_ref[...] = jnp.where(
        one == 0, jnp.sum(square), jnp.where(one == 1, jnp.sum(image_square), cc)
    )


def smooth_slab(idx, own, twin, other, slope):
    vm = pl.BlockSpec(memory_space=pltpu.VMEM)
    return pl.pallas_call(
        smooth_kernel,
        out_shape=[
            jax.ShapeDtypeStruct((3, 3, NX, NY), F32),
            jax.ShapeDtypeStruct((3, NX, NY), F32),
            jax.ShapeDtypeStruct((3, NX, NY), F32),
            jax.ShapeDtypeStruct((1, NY), F32),
        ],
        in_specs=[pl.BlockSpec(memory_space=pltpu.SMEM), vm, vm, vm, vm],
        out_specs=[vm] * 4,
        scratch_shapes=[
            pltpu.VMEM((13, NX, NY), F32),
            pltpu.VMEM((5, NX, NY), F32),
            pltpu.VMEM((3, 13, NX, NY), F32),
        ],
        compiler_params=pltpu.CompilerParams(vmem_limit_bytes=24 << 20),
        cost_estimate=pl.CostEstimate(flops=10**8, bytes_accessed=3 * 10**6, transcendentals=0),
        name="smooth_slab",
    )(idx, own, twin, other, slope)


def finish_kernel(rows_ref, u_ref, adv_ref, m_ref, v_ref, t_ref, sim_ref):
    totals = jnp.sum(rows_ref[...], axis=0, keepdims=True)
    cells = NZ * NX * NY
    velocity_scale = STEP_LENGTH / jnp.sqrt(totals[:, 0:1] / cells + EPSILON)
    image_scale = 1.0 / jnp.sqrt(totals[:, 1:2] / cells + EPSILON)
    sim_ref[...] = totals[:, 2:3] * (0.5 / (DEVICES * cells))
    for j in range(3):
        for d in range(3):
            v_ref[j, d] = u_ref[j, d] * velocity_scale
        t_ref[j] = (m_ref[j] - adv_ref[j] * velocity_scale) * image_scale


def finish(rows, u, advected, m):
    vm = pl.BlockSpec(memory_space=pltpu.VMEM)
    return pl.pallas_call(
        finish_kernel,
        out_shape=[
            jax.ShapeDtypeStruct((3, 3, NX, NY), F32),
            jax.ShapeDtypeStruct((3, NX, NY), F32),
            jax.ShapeDtypeStruct((1, 1), F32),
        ],
        in_specs=[vm] * 4,
        out_specs=[vm] * 3,
        compiler_params=pltpu.CompilerParams(vmem_limit_bytes=12 << 20),
        name="finish",
    )(rows, u, advected, m)


def after(value, *others):
    return lax.optimization_barrier((value, *others))[0]


def round_one(blocks):
    return [permute(blocks[k], first_round(k)) for k in (1, 2, 3)]


def round_two(total):
    parts = [total[2 * k : 2 * k + 2] for k in range(4)]
    got = []
    for k in (2, 1, 3):
        got.append(permute(parts[k], second_round(k)))
    return parts[0] + got[0] + got[1] + got[2]


def step(template, subjects):
    grp = lax.axis_index("grp")
    sub = lax.axis_index("sub")
    core = grp % 2
    xl, y, z = sub // 16, (sub // 4) % 4, sub % 4
    first = jnp.where(core == 0, z, y)
    second = jnp.where(core == 0, y, z)
    idx = jnp.stack([core, first, second, xl, sub, grp // 2]).astype(jnp.int32)

    keep = subjects[0]
    take = permute(keep, CORE_PAIRS)
    mine = lax.dynamic_slice_in_dim(template, 40 * core, WIN, axis=1)
    copies = jnp.broadcast_to(mine[None], (32, 3, WIN, NY))
    image = lax.all_to_all(copies, "sub", 0, 0, tiled=True).reshape(NZ, WIN, NY)

    jplane, *j_blocks = moving_planes(idx, keep, take)
    j_got = round_one(j_blocks)
    iplane, raw, i_half = template_planes(idx, image, keep, take)
    f_blocks, f_got, cc = [None] * 4, [None] * 4, None
    for k in (2, 1, 3, 0):
        f_blocks[k], part = factors(k, idx, iplane, jplane, raw)
        cc = part if cc is None else cc + part
        if k:
            f_got[k] = permute(f_blocks[k], first_round(k))
    j_own = after(j_blocks[0], cc)
    j_total = j_own + j_got[0] + j_got[1] + j_got[2]
    i_other = permute(i_half, CORE_PAIRS)
    slope = slopes(idx, i_half, i_other)
    f_total = f_blocks[0] + f_got[1] + f_got[2] + f_got[3]
    part = round_two(jnp.concatenate([f_total, j_total], axis=1))
    both = jnp.concatenate(
        [part.reshape(2, 6 * OWN, NY), jnp.broadcast_to(cc[None], (2, CC_ROWS, NY))], axis=1
    )
    half = both[0]
    for k in (2, 1, 3):
        half = half + permute(both[k % 2], third_round(k))

    f_half = half[: 3 * OWN]
    m_half = half[3 * OWN : 6 * OWN]
    low = grp < 2
    near = jnp.concatenate(
        [f_half, jnp.where(low, m_half[2 * OWN :], m_half[:OWN])], axis=0
    )
    far = jnp.where(low, f_half[OWN:], f_half[: 2 * OWN])
    far = permute(far, slab_shift(2))
    near = permute(near, slab_shift(1))
    near_f, near_m = near[: 3 * OWN], near[3 * OWN :]
    f_side = jnp.where(
        low, jnp.concatenate([far, near_f], axis=0), jnp.concatenate([near_f, far], axis=0)
    )
    side = jnp.concatenate([f_side, near_m], axis=0)
    twin = permute(side, TWIN_PAIRS)
    own = jnp.concatenate([half, side], axis=0)
    other = permute(jnp.concatenate([own, twin], axis=0), CORE_PAIRS)
    u, advected, m, stats = smooth_slab(idx, own, twin, other, slope)
    rows = lax.all_to_all(jnp.broadcast_to(stats[None], (32, 1, NY)), "sub", 0, 0, tiled=True)
    velocity, new_template, similarity = finish(rows.reshape(32, NY), u, advected, m)
    return velocity, new_template, similarity.reshape(())


def solution(mesh):
    return jax.shard_map(
        step,
        mesh=mesh,
        in_specs=(P("sub", None, None), P(("grp", "sub"), None, None, None)),
        out_specs=(P("sub", None, None, None), P("sub", None, None), P()),
        check_vma=False,
    )
```

```python
import functools
import math

import jax
import jax.numpy as jnp
from jax import lax
from jax.experimental import pallas as pl
from jax.experimental.pallas import tpu as pltpu
from jax.sharding import PartitionSpec as P


RADIUS = 4
REACH = 5
EPSILON = 1e-05
STEP_LENGTH = 0.5
VARIANCE = 3.0
F32 = jnp.float32
BF16 = jnp.bfloat16

NZ, NX, NY = 96, 96, 128
WIN = 56
OWN = 48
COUNT = 729.0
BOTH = ("grp", "sub")
DEVICES = 128


def place(xh, co, xl, y, z):
    return (xh * 2 + co) * 32 + xl * 16 + y * 4 + z


def pairs(move):
    out = []
    for xh in range(2):
        for co in range(2):
            for xl in range(2):
                for y in range(4):
                    for z in range(4):
                        target = move(xh, co, xl, y, z)
                        if target is not None:
                            out.append((place(xh, co, xl, y, z), place(*target)))
    return out


def first_round(k):
    return pairs(
        lambda xh, co, xl, y, z: (xh, co, xl, y, (z + k) % 4) if co == 0 else (xh, co, xl, (y + k) % 4, z)
    )


def second_round(k):
    return pairs(
        lambda xh, co, xl, y, z: (xh, co, xl, (y + k) % 4, z) if co == 0 else (xh, co, xl, y, (z + k) % 4)
    )


def third_round(k):
    def move(xh, co, xl, y, z):
        x = (xh * 2 + xl + k) % 4
        return (x // 2, co, x % 2, y, z)

    return pairs(move)


TWIN_PAIRS = pairs(lambda xh, co, xl, y, z: (1 - xh, co, xl, y, z))
CORE_PAIRS = pairs(lambda xh, co, xl, y, z: (xh, 1 - co, xl, y, z))


def slab_shift(k):
    return [
        (g * 32 + s, g * 32 + (s + (k if g < 2 else -k)) % 32) for g in range(4) for s in range(32)
    ]


def permute(x, table):
    return lax.ppermute(x, BOTH, table)


def slab_of(idx, kb, ka, kl):
    b = (idx[1] + kb) & 3
    a = (idx[2] + ka) & 3
    xl = (idx[3] + kl) & 1
    core = idx[0]
    y = jnp.where(core == 0, a, b)
    z = jnp.where(core == 0, b, a)
    return xl * 16 + y * 4 + z


TOP = 16
CHUNK = 4
STEPS = NZ // (2 * CHUNK)
PAGES = NZ + 2 * CHUNK
FIRST_ORDER = 1.0 / 27.0


def split(product):
    high = product.astype(BF16)
    low = (product - high.astype(F32)).astype(BF16)
    return jnp.concatenate([high, low], axis=1)


def bands():
    rows = lax.broadcasted_iota(jnp.int32, (2 * NY, NY), 0)
    cols = lax.broadcasted_iota(jnp.int32, (2 * NY, NY), 1)
    away = jnp.abs((rows & (NY - 1)) - cols)
    band2 = jnp.where(away <= RADIUS, 1.0, 0.0).astype(BF16)
    return band2[:NY], band2


def dot(lhs, rhs):
    return jnp.dot(lhs, rhs, preferred_element_type=F32)


def load(ref, base, chunk):
    return ref[pl.ds(base, chunk)].reshape(chunk * WIN, NY)


def triple_sums(makers, scales, shift, even, odd, three, last, enter, emit, leave):
    band1, band2 = bands()
    volumes = len(three)
    first = [v for v in range(volumes) if scales[v] is not None]
    second = [v for v in range(volumes) if scales[v] is None]
    for v in range(volumes):
        for ref in (even[v], odd[v], last[v]):
            ref[...] = jnp.zeros(ref.shape, F32)

    def along_y(lhs, line):
        size = CHUNK * WIN
        for members, band in ((first, band1), (second, band2)):
            sums = dot(jnp.concatenate([lhs[v]() for v in members], axis=0), band)
            for m, v in enumerate(members):
                for j in range(CHUNK):
                    at = m * size + j * WIN
                    line[v][j, pl.ds(TOP, WIN), :] = sums[at : at + WIN]

    def triples(v, n, q, rows, pages):
        before, here = last[v][0, rows, :], last[v][1, rows, :]
        left, right = here + pages[0], pages[1] + pages[2]
        sums = (before + left, left + pages[1], pages[0] + right, right + pages[3])
        for j in range(CHUNK):
            emit(v, n, q + j, rows, sums[j] * scales[v] if scales[v] is not None else sums[j])
        last[v][0, rows, :] = pages[2]
        last[v][1, rows, :] = pages[3]

    def along_x(v, line, n, q):
        for j in range(CHUNK):
            three[v][j] = (
                line[v][j, pl.ds(TOP - 9 + shift, 64), :]
                + line[v][j, pl.ds(TOP - 8 + shift, 64), :]
                + line[v][j, pl.ds(TOP - 7 + shift, 64), :]
            )
        for r in range(OWN // 8):
            pages = [
                three[v][j, pl.ds(5 + 8 * r, 8), :]
                + three[v][j, pl.ds(8 + 8 * r, 8), :]
                + three[v][j, pl.ds(11 + 8 * r, 8), :]
                for j in range(CHUNK)
            ]
            triples(v, n, q, pl.ds(8 * r, 8), pages)

    def step(n, carry):
        enter(n)
        along_y(makers(2 * n * CHUNK), even)
        for v in range(volumes):
            along_x(v, odd, n, 0)
        along_y(makers((2 * n + 1) * CHUNK), odd)
        for v in range(volumes):
            along_x(v, even, n, CHUNK)
        leave(n)
        return carry

    lax.fori_loop(0, STEPS, step, 0)
    n = jnp.int32(STEPS)
    enter(n)
    zeros = jnp.zeros((8, NY), F32)
    for v in range(volumes):
        along_x(v, odd, n, 0)
        for r in range(OWN // 8):
            triples(v, n, CHUNK, pl.ds(8 * r, 8), [zeros] * CHUNK)
    leave(n)


PARTS = 4
PART = NZ // PARTS


def window_fetches(core, pairs_of_refs, sems):
    rows = pl.ds(pl.multiple_of(core * (NX - WIN), 8), WIN)
    return [
        [
            pltpu.make_async_copy(
                ref.at[pl.ds(p * PART, PART), rows], held.at[pl.ds(p * PART, PART)], sems.at[i, p]
            )
            for i, (ref, held) in enumerate(pairs_of_refs)
        ]
        for p in range(PARTS)
    ]


def wait_part(fetches, n):
    for p in range(PARTS):

        @pl.when(n == p * (STEPS // PARTS))
        def _():
            for fetch in fetches[p]:
                fetch.wait()


def in_hbm(x):
    return pltpu.with_memory_space_constraint(x, pltpu.HBM)


def moving_kernel(
    idx, ja_hbm, jb_hbm, plane_hbm, o0, o1, o2, o3,
    ja_ref, jb_ref, pair, even, odd, three, last, ready, in_sem, pair_sem, sem,
):
    shift = pl.multiple_of(idx[0] * 8, 8)
    length = 2 * CHUNK
    fetches = window_fetches(idx[0], ((ja_hbm, ja_ref), (jb_hbm, jb_ref)), in_sem)
    for part in fetches:
        for fetch in part:
            fetch.start()

    def makers(base):
        def square(ref):
            f = load(ref, base, CHUNK).astype(F32)
            return split(f * f)

        def add():
            fa = load(ja_ref, base, CHUNK).astype(F32)
            fb = load(jb_ref, base, CHUNK).astype(F32)
            pair[pl.ds(base, CHUNK)] = (fa + fb).reshape(CHUNK, WIN, NY)
            return load(ja_ref, base, CHUNK)

        return [
            add,
            lambda: square(ja_ref),
            lambda: load(jb_ref, base, CHUNK),
            lambda: square(jb_ref),
        ]

    def copy(n):
        slot = n & (SLOTS - 1)
        return pltpu.make_async_copy(
            ready.at[slot], plane_hbm.at[:, pl.ds(n * length, length)], sem.at[slot]
        )

    outs = []
    for kb, out in enumerate((o0, o1, o2, o3)):
        for t in range(8):
            slab = slab_of(idx, kb, t // 2, t % 2)
            outs.append(
                pltpu.make_async_copy(
                    pair.at[pl.ds(slab * 3, 3), pl.ds(shift, OWN)], out.at[t], pair_sem.at[kb * 8 + t]
                )
            )

    def enter(n):
        wait_part(fetches, n)

        @pl.when(n >= SLOTS)
        def _():
            copy(n - SLOTS).wait()

        @pl.when(n == STEPS)
        def _():
            for out in outs:
                out.start()

    def emit(v, n, q, rows, x):
        ready[n & (SLOTS - 1), v, q, rows, :] = x

    triple_sums(
        makers, (FIRST_ORDER, None) * 2, shift, even, odd, three, last,
        enter, emit, lambda n: copy(n).start(),
    )
    for n in range(STEPS + 1 - SLOTS, STEPS + 1):
        copy(jnp.int32(n)).wait()
    for out in outs:
        out.wait()


SLOTS = 4
LINES = [
    [pltpu.VMEM((CHUNK, 88, NY), F32)] * 4,
    [pltpu.VMEM((CHUNK, 88, NY), F32)] * 4,
    [pltpu.VMEM((CHUNK, 64, NY), F32)] * 4,
    [pltpu.VMEM((2, OWN, NY), F32)] * 4,
]
SMALL = pl.BlockSpec(memory_space=pltpu.SMEM)
FAR = pl.BlockSpec(memory_space=pltpu.HBM)
NEAR = pl.BlockSpec(memory_space=pltpu.VMEM)
WINDOW = pltpu.VMEM((NZ, WIN, NY), BF16)
PLANES = pltpu.VMEM((4, PAGES, OWN, NY), F32)
RAW = pltpu.VMEM((3, NZ, WIN, NY), F32)


def in_vmem(x):
    return pltpu.with_memory_space_constraint(x, pltpu.VMEM)


def moving_planes(idx, ja, jb):
    return pl.pallas_call(
        moving_kernel,
        out_shape=[pltpu.HBM((4, PAGES, OWN, NY), F32)] + [pltpu.HBM((8, 3, OWN, NY), F32)] * 4,
        in_specs=[SMALL, FAR, FAR],
        out_specs=[FAR] * 5,
        scratch_shapes=[
            WINDOW,
            WINDOW,
            pltpu.VMEM((NZ, WIN, NY), F32),
            *LINES,
            pltpu.VMEM((SLOTS, 4, 2 * CHUNK, OWN, NY), F32),
            pltpu.SemaphoreType.DMA((2, PARTS)),
            pltpu.SemaphoreType.DMA((32,)),
            pltpu.SemaphoreType.DMA((SLOTS,)),
        ],
        compiler_params=pltpu.CompilerParams(vmem_limit_bytes=24 << 20),
        cost_estimate=pl.CostEstimate(flops=4 * 10**9, bytes_accessed=6 * 10**6, transcendentals=0),
        name="moving_planes",
    )(idx, in_hbm(ja), in_hbm(jb))


def template_kernel(
    idx, i_hbm, ja_hbm, jb_hbm, plane, raw, iext_ref,
    i_ref, ja_ref, jb_ref, even, odd, three, last, in_sem, i_sem,
):
    shift = pl.multiple_of(idx[0] * 8, 8)
    fetches = window_fetches(idx[0], ((ja_hbm, ja_ref), (jb_hbm, jb_ref)), in_sem)
    for p in range(PARTS):
        part = pl.ds(p * PART, PART)
        fetches[p].append(pltpu.make_async_copy(i_hbm.at[part], i_ref.at[part], i_sem.at[p]))
        for fetch in fetches[p]:
            fetch.start()

    def makers(base):
        def wide(n, keep):
            f = load((i_ref, ja_ref, jb_ref)[n], base, CHUNK).astype(F32)
            if keep:
                raw[n, pl.ds(base, CHUNK)] = f.reshape(CHUNK, WIN, NY)
            return f

        def square():
            f = wide(0, True)
            return split(f * f)

        return [
            lambda: load(i_ref, base, CHUNK),
            square,
            lambda: split(wide(0, False) * wide(1, True)),
            lambda: split(wide(0, False) * wide(2, True)),
        ]

    def emit(v, n, q, rows, x):
        plane[v, 2 * CHUNK * n + q, rows, :] = x

    triple_sums(
        makers, (FIRST_ORDER, None, None, None), shift, even, odd, three, last,
        lambda n: wait_part(fetches, n), emit, lambda n: None,
    )
    start = idx[4] * 3 - 6
    for j in range(15):
        z = start + j
        inside = jnp.logical_and(z >= 0, z < NZ)
        page = raw[0, jnp.clip(z, 0, NZ - 1), pl.ds(shift, OWN), :]
        iext_ref[j] = jnp.where(inside, page, 0.0).astype(BF16)


def template_planes(idx, image, ja, jb):
    return pl.pallas_call(
        template_kernel,
        out_shape=[PLANES, RAW, jax.ShapeDtypeStruct((15, OWN, NY), BF16)],
        in_specs=[SMALL, FAR, FAR, FAR],
        out_specs=[NEAR] * 3,
        scratch_shapes=[
            WINDOW,
            WINDOW,
            WINDOW,
            *LINES,
            pltpu.SemaphoreType.DMA((2, PARTS)),
            pltpu.SemaphoreType.DMA((PARTS,)),
        ],
        compiler_params=pltpu.CompilerParams(vmem_limit_bytes=16 << 20),
        cost_estimate=pl.CostEstimate(flops=4 * 10**9, bytes_accessed=5 * 10**6, transcendentals=0),
        name="template_planes",
    )(idx, image, in_hbm(ja), in_hbm(jb))


def factor_kernel(kb, idx, iplane, jplane, raw, out, cc_ref):
    shift = pl.multiple_of(idx[0] * 8, 8)
    eps_b = EPSILON * COUNT
    eps_bc = EPSILON * COUNT**2

    def block(t, cc):
        slab = slab_of(idx, kb, t // 2, t % 2)
        first = slab * 3
        for r in range(OWN // 8):
            part = pl.ds(r * 8, 8)

            def boxes(ref, v):
                pages = [ref[v, first + 2 + p, part, :] for p in range(9)]
                return [pages[j] + pages[j + 3] + pages[j + 6] for j in range(3)]

            own = pl.ds(shift + r * 8, 8)
            si, sii = boxes(iplane, 0), boxes(iplane, 1)
            var_i = [sii[j] - si[j] * si[j] for j in range(3)]
            slope = [
                (raw[0, first + j, own, :] - si[j] * FIRST_ORDER) / (var_i[j] + eps_b)
                for j in range(3)
            ]
            total = [None] * 3
            for n in range(2):
                sj, sjj = boxes(jplane, 2 * n), boxes(jplane, 2 * n + 1)
                sij = boxes(iplane, 2 + n)
                for j in range(3):
                    var_j = sjj[j] - sj[j] * sj[j]
                    cross = sij[j] - si[j] * sj[j]
                    gain = cross / (var_i[j] * var_j + eps_bc)
                    cc = cc + cross * gain
                    moved = raw[1 + n, first + j, own, :] - sj[j] * FIRST_ORDER - cross * slope[j]
                    term = gain * moved
                    total[j] = term if n == 0 else total[j] + term
            for j in range(3):
                out[t, j, part, :] = total[j]
        return cc

    cc_ref[...] = lax.fori_loop(0, 8, block, jnp.zeros((8, NY), F32))


def factors(kb, idx, iplane, jplane, raw):
    return pl.pallas_call(
        functools.partial(factor_kernel, kb),
        out_shape=[
            jax.ShapeDtypeStruct((8, 3, OWN, NY), F32),
            jax.ShapeDtypeStruct((8, NY), F32),
        ],
        in_specs=[SMALL, NEAR, NEAR, NEAR],
        out_specs=[NEAR] * 2,
        compiler_params=pltpu.CompilerParams(vmem_limit_bytes=4 << 20),
        cost_estimate=pl.CostEstimate(flops=4 * 10**8, bytes_accessed=10**6, transcendentals=0),
        name="factors",
    )(idx, in_vmem(iplane), in_vmem(jplane), in_vmem(raw))


CC_ROWS = 8
SIDE = 6 * OWN
CENTRE = 6 * OWN + CC_ROWS


def twice_slopes(here):
    row = lax.broadcasted_iota(jnp.int32, (NX, NY), 0)
    lane = lax.broadcasted_iota(jnp.int32, (NX, NY), 1)
    below = jnp.where(row == NX - 1, 0.0, pltpu.roll(here, NX - 1, 0))
    above = jnp.where(row == 0, 0.0, pltpu.roll(here, 1, 0))
    right = jnp.where(lane == NY - 1, 0.0, pltpu.roll(here, NY - 1, 1))
    left = jnp.where(lane == 0, 0.0, pltpu.roll(here, 1, 1))
    return below - above, right - left


def slope_kernel(idx, iown_ref, iother_ref, slope_ref, image):
    mine = pl.multiple_of(idx[0] * OWN, 8)
    others = pl.multiple_of((1 - idx[0]) * OWN, 8)
    for p in range(15):
        image[p, pl.ds(mine, OWN), :] = iown_ref[p].astype(F32)
        image[p, pl.ds(others, OWN), :] = iother_ref[p].astype(F32)
    scale = COUNT
    for p in range(13):
        sx, sy = twice_slopes(image[p + 1])
        slope_ref[0, p] = (image[p + 2] - image[p]) * scale
        slope_ref[1, p] = sx * scale
        slope_ref[2, p] = sy * scale


def slopes(idx, iown, iother):
    return pl.pallas_call(
        slope_kernel,
        out_shape=pltpu.VMEM((3, 13, NX, NY), F32),
        in_specs=[SMALL, NEAR, NEAR],
        out_specs=NEAR,
        scratch_shapes=[pltpu.VMEM((15, NX, NY), F32)],
        compiler_params=pltpu.CompilerParams(vmem_limit_bytes=6 << 20),
        cost_estimate=pl.CostEstimate(flops=10**6, bytes_accessed=10**6, transcendentals=0),
        name="slopes",
    )(idx, iown, iother)


def smooth_kernel(
    idx, own_ref, twin_ref, other_ref, slope_ref, u_ref, adv_ref, m_ref, st_ref, ext, mext, prod,
):
    core, sub, xh = idx[0], idx[4], idx[5]
    mine = pl.multiple_of(core * OWN, 8)
    others = pl.multiple_of((1 - core) * OWN, 8)

    def centre(rows, ref):
        for j in range(3):
            ext[5 + j, rows, :] = ref[pl.ds(j * OWN, OWN), :]
            mext[1 + j, rows, :] = ref[pl.ds((3 + j) * OWN, OWN), :]

    def sides(rows, low, high):
        for d, (ref, at) in enumerate((low, high)):
            for j in range(5):
                z = sub * 3 + (j - 5 if d == 0 else j + 3)
                inside = jnp.logical_and(z >= 0, z < NZ)
                page = ref[pl.ds(at + j * OWN, OWN), :]
                ext[j if d == 0 else 8 + j, rows, :] = jnp.where(inside, page, 0.0)
            z = sub * 3 + (-1 if d == 0 else 3)
            inside = jnp.logical_and(z >= 0, z < NZ)
            page = ref[pl.ds(at + 5 * OWN, OWN), :]
            mext[0 if d == 0 else 4, rows, :] = jnp.where(inside, page, 0.0)

    my_rows, other_rows = pl.ds(mine, OWN), pl.ds(others, OWN)
    centre(my_rows, own_ref)
    centre(other_rows, other_ref)

    @pl.when(xh == 0)
    def _():
        sides(my_rows, (own_ref, CENTRE), (twin_ref, 0))
        sides(other_rows, (other_ref, CENTRE), (other_ref, CENTRE + SIDE))

    @pl.when(xh == 1)
    def _():
        sides(my_rows, (twin_ref, 0), (own_ref, CENTRE))
        sides(other_rows, (other_ref, CENTRE + SIDE), (other_ref, CENTRE))

    weights = [math.exp(-o * o / (2.0 * VARIANCE)) for o in range(-REACH, REACH + 1)]
    norm = sum(weights)
    weights = [w / norm for w in weights]

    def matrix(n):
        r = lax.broadcasted_iota(jnp.int32, (n, n), 0)
        c = lax.broadcasted_iota(jnp.int32, (n, n), 1)
        d = (r - c).astype(F32)
        return jnp.where(jnp.abs(r - c) <= REACH, jnp.exp(-d * d / (2.0 * VARIANCE)) / norm, 0.0)

    def halves(x):
        high = x.astype(BF16)
        return high, (x - high.astype(F32)).astype(BF16)

    high, low = halves(matrix(NX))
    gx3 = jnp.concatenate([high, high, low], axis=1)
    high, low = halves(matrix(NY))
    gy3 = jnp.concatenate([high, high, low], axis=0)
    for p in range(13):
        for d in range(3):
            prod[d, p] = ext[p] * slope_ref[d, p]
    square = jnp.zeros((NX, NY), F32)
    image_square = jnp.zeros((NX, NY), F32)
    mean = 1.0 / DEVICES
    for j in range(3):
        m = mext[1 + j] * mean
        sx, sy = twice_slopes(m)
        slopes = ((mext[2 + j] - mext[j]) * mean, sx, sy)
        image_square = image_square + m * m
        moved = None
        for d in range(3):
            acc = prod[d, j] * weights[0]
            for o in range(1, 11):
                acc = acc + prod[d, j + o] * weights[o]
            acc = dot(jnp.concatenate([*halves(acc), halves(acc)[0]], axis=1), gy3)
            high, low = halves(acc)
            acc = dot(gx3, jnp.concatenate([high, low, high], axis=0))
            u = acc * mean
            u_ref[j, d] = u
            square = square + u * u
            term = u * slopes[d]
            moved = term if d == 0 else moved + term
        adv_ref[j] = moved * 0.5
        m_ref[j] = m
    tail = pl.ds(6 * OWN, CC_ROWS)
    cc = jnp.sum(own_ref[tail, :] + other_ref[tail, :])
    one = lax.broadcasted_iota(jnp.int32, (1, NY), 1)
    st_ref[...] = jnp.where(
        one == 0, jnp.sum(square), jnp.where(one == 1, jnp.sum(image_square), cc)
    )


def smooth_slab(idx, own, twin, other, slope):
    vm = pl.BlockSpec(memory_space=pltpu.VMEM)
    return pl.pallas_call(
        smooth_kernel,
        out_shape=[
            jax.ShapeDtypeStruct((3, 3, NX, NY), F32),
            jax.ShapeDtypeStruct((3, NX, NY), F32),
            jax.ShapeDtypeStruct((3, NX, NY), F32),
            jax.ShapeDtypeStruct((1, NY), F32),
        ],
        in_specs=[pl.BlockSpec(memory_space=pltpu.SMEM), vm, vm, vm, vm],
        out_specs=[vm] * 4,
        scratch_shapes=[
            pltpu.VMEM((13, NX, NY), F32),
            pltpu.VMEM((5, NX, NY), F32),
            pltpu.VMEM((3, 13, NX, NY), F32),
        ],
        compiler_params=pltpu.CompilerParams(vmem_limit_bytes=24 << 20),
        cost_estimate=pl.CostEstimate(flops=10**8, bytes_accessed=3 * 10**6, transcendentals=0),
        name="smooth_slab",
    )(idx, own, twin, other, slope)


def finish_kernel(rows_ref, u_ref, adv_ref, m_ref, v_ref, t_ref, sim_ref):
    totals = jnp.sum(rows_ref[...], axis=0, keepdims=True)
    cells = NZ * NX * NY
    velocity_scale = STEP_LENGTH / jnp.sqrt(totals[:, 0:1] / cells + EPSILON)
    image_scale = 1.0 / jnp.sqrt(totals[:, 1:2] / cells + EPSILON)
    sim_ref[...] = totals[:, 2:3] * (0.5 / (DEVICES * cells))
    for j in range(3):
        for d in range(3):
            v_ref[j, d] = u_ref[j, d] * velocity_scale
        t_ref[j] = (m_ref[j] - adv_ref[j] * velocity_scale) * image_scale


def finish(rows, u, advected, m):
    vm = pl.BlockSpec(memory_space=pltpu.VMEM)
    return pl.pallas_call(
        finish_kernel,
        out_shape=[
            jax.ShapeDtypeStruct((3, 3, NX, NY), F32),
            jax.ShapeDtypeStruct((3, NX, NY), F32),
            jax.ShapeDtypeStruct((1, 1), F32),
        ],
        in_specs=[vm] * 4,
        out_specs=[vm] * 3,
        compiler_params=pltpu.CompilerParams(vmem_limit_bytes=12 << 20),
        name="finish",
    )(rows, u, advected, m)


def after(value, *others):
    return lax.optimization_barrier((value, *others))[0]


def round_one(blocks):
    got = []
    for k in (1, 3, 2):
        got.append(permute(blocks[k], first_round(k)))
    return got


def round_two(total):
    parts = [total[2 * k : 2 * k + 2] for k in range(4)]
    got = []
    for k in (2, 1, 3):
        got.append(permute(parts[k], second_round(k)))
    return parts[0] + got[0] + got[1] + got[2]


def step(template, subjects):
    grp = lax.axis_index("grp")
    sub = lax.axis_index("sub")
    core = grp % 2
    xl, y, z = sub // 16, (sub // 4) % 4, sub % 4
    first = jnp.where(core == 0, z, y)
    second = jnp.where(core == 0, y, z)
    idx = jnp.stack([core, first, second, xl, sub, grp // 2]).astype(jnp.int32)

    keep = subjects[0]
    take = permute(keep, CORE_PAIRS)
    mine = lax.dynamic_slice_in_dim(template, 40 * core, WIN, axis=1)
    copies = jnp.broadcast_to(mine[None], (32, 3, WIN, NY))
    image = lax.all_to_all(copies, "sub", 0, 0, tiled=True).reshape(NZ, WIN, NY)

    jplane, *j_blocks = moving_planes(idx, keep, take)
    j_got = round_one(j_blocks)
    iplane, raw, i_half = template_planes(idx, image, keep, take)
    f_blocks, f_got, cc = [None] * 4, [None] * 4, None
    for k in (2, 1, 3, 0):
        f_blocks[k], part = factors(k, idx, iplane, jplane, raw)
        cc = part if cc is None else cc + part
        if k:
            f_got[k] = permute(f_blocks[k], first_round(k))
    j_own = after(j_blocks[0], cc)
    j_total = j_own + j_got[0] + j_got[1] + j_got[2]
    i_other = permute(i_half, CORE_PAIRS)
    slope = slopes(idx, i_half, i_other)
    f_total = f_blocks[0] + f_got[1] + f_got[2] + f_got[3]
    part = round_two(jnp.concatenate([f_total, j_total], axis=1))
    both = jnp.concatenate(
        [part.reshape(2, 6 * OWN, NY), jnp.broadcast_to(cc[None], (2, CC_ROWS, NY))], axis=1
    )
    half = both[0]
    for k in (2, 1, 3):
        half = half + permute(both[k % 2], third_round(k))

    f_half = half[: 3 * OWN]
    m_half = half[3 * OWN : 6 * OWN]
    low = grp < 2
    near = jnp.concatenate(
        [f_half, jnp.where(low, m_half[2 * OWN :], m_half[:OWN])], axis=0
    )
    far = jnp.where(low, f_half[OWN:], f_half[: 2 * OWN])
    near = permute(near, slab_shift(1))
    far = permute(far, slab_shift(2))
    near_f, near_m = near[: 3 * OWN], near[3 * OWN :]
    f_side = jnp.where(
        low, jnp.concatenate([far, near_f], axis=0), jnp.concatenate([near_f, far], axis=0)
    )
    side = jnp.concatenate([f_side, near_m], axis=0)
    twin = permute(side, TWIN_PAIRS)
    own = jnp.concatenate([half, side], axis=0)
    other = permute(jnp.concatenate([own, twin], axis=0), CORE_PAIRS)
    u, advected, m, stats = smooth_slab(idx, own, twin, other, slope)
    rows = lax.all_to_all(jnp.broadcast_to(stats[None], (32, 1, NY)), "sub", 0, 0, tiled=True)
    velocity, new_template, similarity = finish(rows.reshape(32, NY), u, advected, m)
    return velocity, new_template, similarity.reshape(())


def solution(mesh):
    return jax.shard_map(
        step,
        mesh=mesh,
        in_specs=(P("sub", None, None), P(("grp", "sub"), None, None, None)),
        out_specs=(P("sub", None, None, None), P("sub", None, None), P()),
        check_vma=False,
    )
```
